32 devices in a mesh: seq: 2 (over x), fsdp: 16 (over z, y, core).
Axes of the slice: x: 2, y: 2, z: 4, core: 2. Of those that a mesh axis runs over, the one named last changes fastest.
Arguments:
- tokens: bfloat16 [16, 2048, 768], P('fsdp', 'seq'), may hold values from -13 to 13
- lengths: int32 [16, 16], P('fsdp'), may hold values from 0 to 2048, as said below
- block_order: int32 [16, 16], P('fsdp'), may hold values from 0 to 15, each once within a row
- qkv_weight: bfloat16 [768, 2304], P(('seq', 'fsdp')), may hold values from -0.21875 to 0.21875
- query_bias: bfloat16 [768], P(('seq', 'fsdp')), may hold values from -3 to 3
- value_bias: bfloat16 [768], P(('seq', 'fsdp')), may hold values from -3 to 3
- out_weight: bfloat16 [768, 768], P(('seq', 'fsdp')), may hold values from -0.875 to 0.875
- out_bias: bfloat16 [768], P(('seq', 'fsdp')), may hold values from -3 to 3
- norm1_gain: bfloat16 [768], P(('seq', 'fsdp')), may hold values from 0.099609375 to 1.8984375
- norm1_shift: bfloat16 [768], P(('seq', 'fsdp')), may hold values from -3 to 3
- in_weight: bfloat16 [768, 3072], P(('seq', 'fsdp')), may hold values from -0.21875 to 0.21875
- in_bias: bfloat16 [3072], P(('seq', 'fsdp')), may hold values from -3 to 3
- down_weight: bfloat16 [3072, 768], P(('seq', 'fsdp')), may hold values from -0.109375 to 0.109375
- down_bias: bfloat16 [768], P(('seq', 'fsdp')), may hold values from -3 to 3
- norm2_gain: bfloat16 [768], P(('seq', 'fsdp')), may hold values from 0.099609375 to 1.8984375
- norm2_shift: bfloat16 [768], P(('seq', 'fsdp')), may hold values from -3 to 3
- cotangent: bfloat16 [16, 2048, 768], P('fsdp', 'seq'), may hold values from -6 to 6
Outputs:
- output: bfloat16 [16, 2048, 768], P('fsdp', 'seq')
- input_grad: bfloat16 [16, 2048, 768], P('fsdp', 'seq')
- qkv_weight_grad: float32 [768, 2304], P(('seq', 'fsdp'))
- query_bias_grad: float32 [768], P(('seq', 'fsdp'))
- value_bias_grad: float32 [768], P(('seq', 'fsdp'))
- out_weight_grad: float32 [768, 768], P(('seq', 'fsdp'))
- out_bias_grad: float32 [768], P(('seq', 'fsdp'))
- norm1_gain_grad: float32 [768], P(('seq', 'fsdp'))
- norm1_shift_grad: float32 [768], P(('seq', 'fsdp'))
- in_weight_grad: float32 [768, 3072], P(('seq', 'fsdp'))
- in_bias_grad: float32 [3072], P(('seq', 'fsdp'))
- down_weight_grad: float32 [3072, 768], P(('seq', 'fsdp'))
- down_bias_grad: float32 [768], P(('seq', 'fsdp'))
- norm2_gain_grad: float32 [768], P(('seq', 'fsdp'))
- norm2_shift_grad: float32 [768], P(('seq', 'fsdp'))
The draws below stay inside these ranges and needn't reach their ends.
Inputs may be any that keep to these rules, and one draw needn't show every extreme that they name: Each row holds the lengths of one group's packed sequences in order, at most 4 of them, multiples of 128, followed by zeros, and sums to 2048; in every draw some group holds one sequence of 2048 tokens. `block_order`: each row is a permutation of the numbers 0 to 15.
All inputs are finite; a program needn't handle non-finite values.
Results may differ from the reference program's by a relative error of at most 0.015.
Values may be sent and summed in bfloat16 or wider, within the bound.
No kernel may reach another device: no remote copies, remote signals or barrier semaphores. Data moves between devices by JAX's collectives and lax.ppermute only.
A program may use at most 256 MiB of HBM per device.

```python
import jax
import jax.numpy as jnp
from jax import lax

D = 768
H = 12
HD = 64
FF = 3072
UNITS = 16
GROUPS = 16
GROUP_TOK = 2048
MINLEN = 128


def draw_tokens(key, part):
    subkeys = jax.random.split(key, 3)
    full_shape = (GROUPS, GROUP_TOK, D)
    base_vals = jax.random.truncated_normal(subkeys[0], -4.0, 4.0, full_shape, jnp.float32)
    row_scale = jnp.exp(jax.random.uniform(subkeys[1], (GROUPS, GROUP_TOK, 1), jnp.float32, -0.8, 0.8))
    col_scale = jnp.exp(jax.random.uniform(subkeys[2], (1, 1, D), jnp.float32, -0.35, 0.35))
    return (base_vals * row_scale * col_scale).astype(jnp.bfloat16)


def draw_lengths(key, part):
    first_key, second_key = jax.random.split(jax.random.fold_in(key, 7))
    cut_places = jax.random.randint(first_key, (GROUPS, 3), 1, UNITS).astype(jnp.int32)
    boundary_ids = jnp.arange(1, UNITS, dtype=jnp.int32)
    unit_cuts = jnp.max((cut_places[:, :, None] == boundary_ids[None, None, :]).astype(jnp.int32), axis=1)
    whole_group = jax.random.randint(second_key, (), 0, GROUPS).astype(jnp.int32)
    group_index = jnp.arange(GROUPS, dtype=jnp.int32)
    unit_cuts = jnp.where(group_index[:, None] == whole_group, 0, unit_cuts).astype(jnp.int32)
    unit_ids = jnp.concatenate([jnp.zeros((GROUPS, 1), jnp.int32), jnp.cumsum(unit_cuts, axis=1).astype(jnp.int32)], axis=1)
    slot_ids = jnp.arange(UNITS, dtype=jnp.int32)
    counts = jnp.sum((unit_ids[:, :, None] == slot_ids[None, None, :]).astype(jnp.int32), axis=1)
    return (counts * MINLEN).astype(jnp.int32)


def levels(rng, shape, cuts, least, top_value):
    def one(axis_at, parts):
        heights = jax.random.uniform(jax.random.fold_in(jax.random.fold_in(rng, 6), axis_at), (parts,), jnp.float32, least / len(cuts), top_value / len(cuts))
        return jnp.repeat(jnp.exp(heights), shape[axis_at] // parts).reshape((-1,) + (1,) * (len(shape) - axis_at - 1))

    level = one(*cuts[0])
    for cut in cuts[1:]:
        level = level * one(*cut)
    return level


def gaussian(own_key, shape, scale, limit, cuts=(), kind=jnp.bfloat16):
    values = jax.random.normal(own_key, shape, jnp.float32) * scale
    if len(cuts) > 0:
        values = levels(own_key, shape, cuts, -0.22, 0.18) * values
    return jnp.clip(values, min=-limit, max=limit).astype(kind)


def setup_inputs(seed: int = 0) -> dict:
    streams_of = jax.random.split(jax.random.key(seed), 18)
    return {
        "tokens": draw_tokens(jax.random.fold_in(streams_of[17], 71), 0),
        "lengths": draw_lengths(jax.random.fold_in(streams_of[17], 71), 0),
        "block_order": jax.vmap(lambda own: jax.random.permutation(own, UNITS))(jax.random.split(streams_of[2], GROUPS)).reshape((GROUPS, UNITS)).astype(jnp.int32),
        "qkv_weight": gaussian(streams_of[3], (D, 3 * D), D ** -0.5, 0.21875, ((0, 32),)),
        "query_bias": gaussian(streams_of[4], (D,), 0.5, 3.0, ((0, 32),)),
        "value_bias": gaussian(streams_of[5], (D,), 0.5, 3.0, ((0, 32),)),
        "out_weight": gaussian(streams_of[6], (D, D), (D // 16) ** -0.5, 0.875, ((0, 32),)),
        "out_bias": gaussian(streams_of[7], (D,), 0.5, 3.0, ((0, 32),)),
        "norm1_gain": jnp.clip(1.0 + 0.18 * jax.random.normal(streams_of[8], (D,), jnp.float32), 0.099609375, 1.8984375).astype(jnp.bfloat16),
        "norm1_shift": gaussian(streams_of[9], (D,), 0.5, 3.0, ((0, 32),)),
        "in_weight": gaussian(streams_of[10], (D, FF), D ** -0.5, 0.21875, ((0, 32),)),
        "in_bias": gaussian(streams_of[11], (FF,), 0.5, 3.0, ((0, 32),)),
        "down_weight": gaussian(streams_of[12], (FF, D), FF ** -0.5, 0.109375, ((0, 32),)),
        "down_bias": gaussian(streams_of[13], (D,), 0.5, 3.0, ((0, 32),)),
        "norm2_gain": jnp.clip(1.0 + 0.18 * jax.random.normal(streams_of[14], (D,), jnp.float32), 0.099609375, 1.8984375).astype(jnp.bfloat16),
        "norm2_shift": gaussian(streams_of[15], (D,), 0.5, 3.0, ((0, 32),)),
        "cotangent": gaussian(streams_of[16], (GROUPS, GROUP_TOK, D), 1.0, 6.0, ((0, 16), (1, 2))),
    }


@jax.custom_vjp
def low(v):
    return lax.optimization_barrier(v.astype(jnp.bfloat16)).astype(jnp.float32)

@jax.custom_vjp
def low_back(v):
    return v

def low_keep(v):
    return (low(v), None)

def low_pass(kept, grad):
    return (grad,)

def back_keep(v):
    return (v, None)

def back_low(kept, grad):
    return (low(grad),)
low.defvjp(low_keep, low_pass)
low_back.defvjp(back_keep, back_low)
highest = lax.Precision.HIGHEST
norm_eps = 1e-12

def layer_norm(values, norm_gain, norm_shift):
    row_mean = lax.optimization_barrier(jnp.mean(values, axis=-1, keepdims=True))
    centered = values - row_mean
    row_var = lax.optimization_barrier(jnp.mean(centered * centered, axis=-1, keepdims=True))
    return centered * lax.rsqrt(row_var + norm_eps) * norm_gain + norm_shift

def segment_ids(length_row, length_all):
    seq_ends = jnp.cumsum(length_row).astype(jnp.int32)
    places = jnp.arange(length_all, dtype=jnp.int32)
    return lax.optimization_barrier(jnp.sum((places[:, None] >= seq_ends[None, :]).astype(jnp.int32), axis=1)).astype(jnp.int32)

def attend_block(key_rows, value_rows, segment_all, query_block, segment_block):
    scores = low_back(jnp.einsum('qhd,khd->hqk', query_block, key_rows, precision=highest) * HD ** (-0.5))
    same_doc = (segment_block[:, None] == segment_all[None, :])[None]
    scores = jnp.where(same_doc, scores, -1e+30)
    soft_weights = low(jax.nn.softmax(scores, axis=-1))
    return low(low_back(jnp.einsum('hqk,khd->qhd', soft_weights, value_rows, precision=highest)))

def forward(params, group_rows, segment_all):
    qkv_weight, query_bias, value_bias, out_weight, out_bias, first_gain, first_shift, in_weight, in_bias, down_weight, down_bias, second_gain, second_shift = params
    length_all = group_rows.shape[0]
    qkv_bias = jnp.concatenate([query_bias, jnp.zeros_like(query_bias), value_bias])
    qkv_rows = low(low_back(jnp.dot(group_rows, qkv_weight, precision=highest) + qkv_bias))
    qkv_rows = qkv_rows.reshape(length_all, 3, H, HD)
    query_rows = qkv_rows[:, 0]
    key_rows = qkv_rows[:, 1]
    value_rows = qkv_rows[:, 2]
    block_rows = min(512, length_all)
    block_count = length_all // block_rows
    checked = jax.checkpoint(attend_block)
    head_blocks = lax.map(lambda block_items: checked(key_rows, value_rows, segment_all, block_items[0], block_items[1]), (query_rows.reshape(block_count, block_rows, H, HD), segment_all.reshape(block_count, block_rows)))
    mixed_heads = head_blocks.reshape(length_all, D)
    attn_out = low_back(jnp.dot(mixed_heads, out_weight, precision=highest) + out_bias)
    hidden_one = layer_norm(group_rows + attn_out, first_gain, first_shift)
    ffn_inner = low_back(jnp.dot(low(hidden_one), in_weight, precision=highest) + in_bias)
    ffn_act = low(jax.nn.gelu(ffn_inner, approximate=False))
    branch = low_back(jnp.dot(ffn_act, down_weight, precision=highest) + down_bias)
    return layer_norm(hidden_one + branch, second_gain, second_shift)

def reference(tokens, lengths, block_order, qkv_weight, query_bias, value_bias, out_weight, out_bias, norm1_gain, norm1_shift, in_weight, in_bias, down_weight, down_bias, norm2_gain, norm2_shift, cotangent):
    params = tuple((param.astype(jnp.float32) for param in (qkv_weight, query_bias, value_bias, out_weight, out_bias, norm1_gain, norm1_shift, in_weight, in_bias, down_weight, down_bias, norm2_gain, norm2_shift)))
    length_all = tokens.shape[1]
    unit_rows = length_all // UNITS
    width = tokens.shape[2]

    def to_packed(rows, order_row):
        return jnp.take(rows.reshape(UNITS, unit_rows, width), order_row, axis=0).reshape(length_all, width)

    def to_arrival(rows, order_row):
        blocks = rows.reshape(UNITS, unit_rows, width)
        placed = jnp.zeros_like(blocks).at[order_row].set(blocks)
        return placed.reshape(length_all, width)

    def one_group(totals, group_items):
        group_rows, length_row, group_back, order_row = group_items
        order_row = order_row.astype(jnp.int32)
        segment_all = segment_ids(length_row, length_all)
        packed_rows = to_packed(group_rows, order_row).astype(jnp.float32)
        packed_back = to_packed(group_back, order_row).astype(jnp.float32)
        result, pull_back = jax.vjp(lambda weights, inputs: forward(weights, inputs, segment_all), params, packed_rows)
        weight_grads, row_grads = pull_back(packed_back)
        totals = tuple((running + addend for running, addend in zip(totals, weight_grads)))
        return (totals, (to_arrival(result.astype(jnp.bfloat16), order_row), to_arrival(row_grads.astype(jnp.bfloat16), order_row)))
    zero_grads = tuple((jnp.zeros(param.shape, jnp.float32) for param in params))
    totals, (outputs, input_grads) = lax.scan(one_group, zero_grads, (tokens, lengths, cotangent, block_order))
    return (outputs, input_grads, totals[0], totals[1], totals[2], totals[3], totals[4], totals[5], totals[6], totals[7], totals[8], totals[9], totals[10], totals[11], totals[12])
```

```python
import jax
import jax.numpy as jnp
import numpy as np
from jax import lax
from jax.sharding import Mesh, PartitionSpec as P
from jax.experimental import pallas as pl
from jax.experimental.pallas import tpu as pltpu

HD = 64
LOG2E = 1.4426950408889634
LN2 = 0.6931471805599453
BIG = 1e30
TQ = 512
STEP = 512
BSTEP = 512
NT = (((1,), (1,)), ((), ()))
NN = (((1,), (0,)), ((), ()))
TN = (((0,), (0,)), ((), ()))


def mxu(a, b, dims):
    return lax.dot_general(a, b, dims, preferred_element_type=jnp.float32)


def lanes(rows):
    return lax.broadcasted_iota(jnp.int32, (rows, 128), 1)


def seg_rows(segs_ref, base_block, rows):
    place = lax.broadcasted_iota(jnp.int32, (rows, 128), 0)
    out = jnp.zeros((rows, 128), jnp.int32)
    for b in range(rows // 128):
        s = segs_ref[base_block + b]
        out = jnp.where(place >= b * 128, s, out)
    return out


def split3(v):
    hi = v.astype(jnp.bfloat16).astype(jnp.float32)
    mid = (v - hi).astype(jnp.bfloat16).astype(jnp.float32)
    low = v - hi - mid
    return hi, mid, low


def both_heads(pair_rows):
    lane = lanes(pair_rows.shape[0])
    zero = jnp.zeros_like(pair_rows)
    return jnp.concatenate(
        [jnp.where(lane < HD, pair_rows, zero), jnp.where(lane < HD, zero, pair_rows)], axis=0
    )


def fill_keys(segs_ref, k_own, k_far, v_own, v_far, k_aug, v_aug):
    half = k_own.shape[0]
    step = 512
    for part, (k_in, v_in) in enumerate(((k_own, v_own), (k_far, v_far))):
        for at in range(0, half, step):
            row = part * half + at
            k_aug[row : row + step, :128] = k_in[at : at + step, :]
            v_aug[row : row + step, :128] = v_in[at : at + step, :]
    total = 2 * half
    for at in range(0, total, step):
        lane = lanes(step)
        seg = seg_rows(segs_ref, at // 128, step)
        hot = (lane == seg) | ((lane >= 64) & (lane < 67))
        k_aug[at : at + step, 128:] = jnp.where(hot, 1.0, 0.0).astype(jnp.bfloat16)
        v_aug[at : at + step, 128:] = jnp.ones((step, 128), jnp.bfloat16)


def fwd_body(segs_ref, q_own, q_far, k_own, k_far, v_own, v_far, o_own, o_far, lse_ref, k_aug, v_aug):
    i = pl.program_id(1)
    n_half = pl.num_programs(1) // 2
    total = k_aug.shape[0]

    @pl.when(i == 0)
    def _():
        fill_keys(segs_ref, k_own, k_far, v_own, v_far, k_aug, v_aug)

    pair_rows = jnp.where(i < n_half, q_own[...], q_far[...])
    lane = lanes(TQ)
    seg = seg_rows(segs_ref, i * (TQ // 128), TQ)
    off = jnp.where((lane < 16) & (lane != seg), -BIG, 0.0).astype(jnp.bfloat16)
    q_aug = jnp.concatenate([both_heads(pair_rows), jnp.concatenate([off, off], axis=0)], axis=1)
    step = STEP
    top = None
    acc = None
    for at in range(0, total, step):
        s = mxu(q_aug, k_aug[at : at + step, :], NT)
        here = jnp.max(s, axis=1, keepdims=True)
        new_top = here if top is None else jnp.maximum(top, here)
        p = jnp.exp2(s - new_top).astype(jnp.bfloat16)
        add = mxu(p, v_aug[at : at + step, :], NN)
        acc = add if acc is None else acc * jnp.exp2(top - new_top) + add
        top = new_top
    both = jnp.where(lane < HD, acc[:TQ, :128], acc[TQ:, :128])
    sums = jnp.where(lane < HD, acc[:TQ, 128:], acc[TQ:, 128:])
    tops = jnp.where(lane < HD, top[:TQ], top[TQ:])
    out = (both / sums).astype(jnp.bfloat16)
    lse_ref[...] = tops + jnp.log2(sums)

    @pl.when(i < n_half)
    def _():
        o_own[...] = out

    @pl.when(i >= n_half)
    def _():
        o_far[...] = out


def pair_specs(half, n_half, parts):
    own_q = lambda at: pl.BlockSpec((TQ, 128), lambda h, i, *_: (jnp.minimum(i, n_half - 1), at * parts + h))
    far_q = lambda at: pl.BlockSpec((TQ, 128), lambda h, i, *_: (jnp.maximum(i - n_half, 0), at * parts + h))
    whole = lambda at: pl.BlockSpec((half, 128), lambda h, i, *_: (0, at * parts + h))
    return own_q, far_q, whole


def attention(segs, own, far):
    half, width = own.shape
    parts = width // 3 // 128
    n_half = half // TQ
    own_q, far_q, whole = pair_specs(half, n_half, parts)
    return pl.pallas_call(
        fwd_body,
        grid_spec=pltpu.PrefetchScalarGridSpec(
            num_scalar_prefetch=1,
            grid=(parts, 2 * n_half),
            in_specs=[own_q(0), far_q(0), whole(1), whole(1), whole(2), whole(2)],
            out_specs=[own_q(0), far_q(0), pl.BlockSpec((TQ, 128), lambda h, i, *_: (i, h))],
            scratch_shapes=[
                pltpu.VMEM((2 * half, 256), jnp.bfloat16),
                pltpu.VMEM((2 * half, 256), jnp.bfloat16),
            ],
        ),
        out_shape=[
            jax.ShapeDtypeStruct((half, parts * 128), jnp.bfloat16),
            jax.ShapeDtypeStruct((half, parts * 128), jnp.bfloat16),
            jax.ShapeDtypeStruct((2 * half, parts * 128), jnp.float32),
        ],
        compiler_params=pltpu.CompilerParams(dimension_semantics=("arbitrary", "arbitrary"), vmem_limit_bytes=50 << 20),
        cost_estimate=pl.CostEstimate(flops=2 * 4 * half * half * 4 * 64 * 2 * parts, bytes_accessed=half * width * 4, transcendentals=8 * half * half * parts),
    )(segs, own, far, own, far, own, far)


def bwd_body(segs_ref, q_own, q_far, k_own, k_far, v_own, v_far, o_own, o_far, d_own, d_far, lse_ref,
             dq_own, dq_far, dk_own, dk_far, dv_own, dv_far, k_aug, v_aug, dk_acc, dv_acc):
    i = pl.program_id(1)
    n = pl.num_programs(1)
    n_half = n // 2
    total = k_aug.shape[0]
    half = total // 2

    @pl.when(i == 0)
    def _():
        fill_keys(segs_ref, k_own, k_far, v_own, v_far, k_aug, v_aug)
        dk_acc[...] = jnp.zeros_like(dk_acc)
        dv_acc[...] = jnp.zeros_like(dv_acc)

    near = i < n_half
    q_rows = jnp.where(near, q_own[...], q_far[...])
    d_rows = jnp.where(near, d_own[...], d_far[...])
    o_rows = jnp.where(near, o_own[...], o_far[...])
    lane = lanes(TQ)
    seg = seg_rows(segs_ref, i * (TQ // 128), TQ)
    off = jnp.where((lane < 16) & (lane != seg), -BIG, 0.0)
    prod = d_rows.astype(jnp.float32) * o_rows.astype(jnp.float32)
    q_side, d_side = [], []
    for head in range(2):
        mine = (lane < HD) if head == 0 else (lane >= HD)
        dot_row = jnp.sum(jnp.where(mine, prod, 0.0), axis=1, keepdims=True)
        lse = jnp.broadcast_to(lse_ref[:, head * HD : head * HD + 1], (TQ, 128))
        h, m, l = split3(-lse)
        q_side.append(jnp.where(lane == 64, h, jnp.where(lane == 65, m, jnp.where(lane == 66, l, off))).astype(jnp.bfloat16))
        h, m, l = split3(-jnp.broadcast_to(dot_row, (TQ, 128)))
        d_side.append(jnp.where(lane == 64, h, jnp.where(lane == 65, m, jnp.where(lane == 66, l, 0.0))).astype(jnp.bfloat16))
    q2 = both_heads(q_rows)
    d2 = both_heads(d_rows)
    q_aug = jnp.concatenate([q2, jnp.concatenate(q_side, axis=0)], axis=1)
    d_aug = jnp.concatenate([d2, jnp.concatenate(d_side, axis=0)], axis=1)
    step = BSTEP
    dq = None
    for at in range(0, total, step):
        keys = k_aug[at : at + step, :]
        p = jnp.exp2(mxu(q_aug, keys, NT))
        dp = mxu(d_aug, v_aug[at : at + step, :], NT)
        ds = (p * dp).astype(jnp.bfloat16)
        dv_acc[at : at + step, :] += mxu(p.astype(jnp.bfloat16), d2, TN)
        dk_acc[at : at + step, :] += mxu(ds, q2, TN)
        add = mxu(ds, keys[:, :128], NN)
        dq = add if dq is None else dq + add
    out = (jnp.where(lane < HD, dq[:TQ], dq[TQ:]) * (HD ** -0.5)).astype(jnp.bfloat16)

    @pl.when(near)
    def _():
        dq_own[...] = out

    @pl.when(i >= n_half)
    def _():
        dq_far[...] = out

    @pl.when(i == n - 1)
    def _():
        dk_own[...] = (dk_acc[:half, :] * LN2).astype(jnp.bfloat16)
        dk_far[...] = (dk_acc[half:, :] * LN2).astype(jnp.bfloat16)
        dv_own[...] = dv_acc[:half, :].astype(jnp.bfloat16)
        dv_far[...] = dv_acc[half:, :].astype(jnp.bfloat16)


def attention_back(segs, own, far, o_own, o_far, d_own, d_far, lse):
    half, width = own.shape
    parts = width // 3 // 128
    n_half = half // TQ
    own_q, far_q, whole = pair_specs(half, n_half, parts)
    one = jax.ShapeDtypeStruct((half, parts * 128), jnp.bfloat16)
    return pl.pallas_call(
        bwd_body,
        grid_spec=pltpu.PrefetchScalarGridSpec(
            num_scalar_prefetch=1,
            grid=(parts, 2 * n_half),
            in_specs=[own_q(0), far_q(0), whole(1), whole(1), whole(2), whole(2),
                      own_q(0), far_q(0), own_q(0), far_q(0), pl.BlockSpec((TQ, 128), lambda h, i, *_: (i, h))],
            out_specs=[own_q(0), far_q(0), whole(0), whole(0), whole(0), whole(0)],
            scratch_shapes=[
                pltpu.VMEM((2 * half, 256), jnp.bfloat16),
                pltpu.VMEM((2 * half, 256), jnp.bfloat16),
                pltpu.VMEM((2 * half, 128), jnp.float32),
                pltpu.VMEM((2 * half, 128), jnp.float32),
            ],
        ),
        out_shape=[one] * 6,
        compiler_params=pltpu.CompilerParams(dimension_semantics=("arbitrary", "arbitrary"), vmem_limit_bytes=50 << 20),
        cost_estimate=pl.CostEstimate(flops=5 * 4 * half * half * 4 * 64 * 2 * parts, bytes_accessed=half * width * 8, transcendentals=8 * half * half * parts),
    )(segs, own, far, own, far, own, far, o_own, o_far, d_own, d_far, lse)


D = 768
UNITS = 16
norm_eps = 1e-12
bf16 = jnp.bfloat16
f32 = jnp.float32


def shift(n, k):
    return [(i, (i + k) % n) for i in range(n)]


class Plan:
    def __init__(self, seq, fsdp):
        rest = fsdp // 2
        dims = []
        while rest > 1:
            want = 4 if len(dims) % 2 == 0 and rest % 4 == 0 else 2
            dims.append(want)
            rest //= want
        self.dims = [seq] + dims + [2]
        self.names = ["s"] + ["r%d" % i for i in range(len(dims))] + ["c"]
        count = len(self.dims)
        self.stages = ([1] if dims else []) + [0] + list(range(2, count - 1)) + [count - 1]
        self.total = seq * fsdp

    def places(self, sign):
        shape = [self.dims[a] for a in reversed(self.stages)]
        grid = np.indices(self.dims).reshape(len(self.dims), -1)
        flat = jnp.zeros((self.total,), jnp.int32)
        if sign < 0:
            for a in reversed(self.stages):
                n = self.dims[a]
                off = (lax.axis_index(self.names[a]) - jnp.asarray(grid[a], jnp.int32)) % n
                flat = flat * n + off
            return flat
        offs = np.indices(shape).reshape(len(shape), -1)
        by_axis = {a: offs[j] for j, a in enumerate(reversed(self.stages))}
        for a in range(len(self.dims)):
            n = self.dims[a]
            flat = flat * n + (lax.axis_index(self.names[a]) + jnp.asarray(by_axis[a], jnp.int32)) % n
        return flat


def gather_all(plan, shard):
    buf = shard[None]
    for a in plan.stages:
        n = plan.dims[a]
        if n == 1:
            continue
        parts = [buf] + [lax.ppermute(buf, plan.names[a], shift(n, k)) for k in range(1, n)]
        buf = jnp.concatenate(parts, axis=0)
    return jnp.take(buf, plan.places(-1), axis=0)


def reduce_all(plan, grads):
    buf = jnp.take(grads, plan.places(1), axis=0)
    for a in reversed(plan.stages):
        n = plan.dims[a]
        size = buf.shape[0] // n
        keep = buf[:size].astype(f32)
        for k in range(1, n):
            got = lax.ppermute(buf[k * size : (k + 1) * size].astype(bf16), plan.names[a], shift(n, k))
            keep = keep + got.astype(f32)
        buf = keep if a == plan.stages[0] else keep.astype(bf16)
    return buf[0]


def norm_stats(rows):
    mean = jnp.mean(rows, axis=-1, keepdims=True)
    centered = rows - mean
    var = jnp.mean(centered * centered, axis=-1, keepdims=True)
    rstd = lax.rsqrt(var + norm_eps)
    return centered * rstd, rstd


def norm_back(grad, unit, rstd, gain):
    eg = grad * gain
    mean_eg = jnp.mean(eg, axis=-1, keepdims=True)
    mean_en = jnp.mean(eg * unit, axis=-1, keepdims=True)
    return (eg - mean_eg - unit * mean_en) * rstd


def dot(a, b, dims=NN):
    return lax.dot_general(a, b, dims, preferred_element_type=f32)


def swap_pair(x):
    return lax.ppermute(x, "c", [(0, 1), (1, 0)])


def relocate(x):
    return lax.ppermute(x, ("s", "c"), [(0, 0), (1, 2), (2, 1), (3, 3)])


def pick(pair, at):
    return lax.dynamic_index_in_dim(pair, at, 0, keepdims=False)


def local(plan, tokens, lengths, block_order, qkv_weight, query_bias, value_bias, out_weight, out_bias,
          norm1_gain, norm1_shift, in_weight, in_bias, down_weight, down_bias, norm2_gain, norm2_shift, cotangent):
    half = tokens.shape[1]
    me = lax.axis_index("c")
    rows_dev = qkv_weight.shape[0]
    ff_dev = down_weight.shape[0]
    ff_cols = in_weight.shape[1] // D
    width = D // 2
    count = plan.total

    tok = relocate(tokens[0])
    ends = jnp.cumsum(lengths[0])
    unit = 2 * half // UNITS
    seg_packed = jnp.sum((jnp.arange(UNITS)[:, None] * unit >= ends[None, :]).astype(jnp.int32), axis=1)
    hit = block_order[0][:, None] == jnp.arange(UNITS)[None, :]
    seg_here = jnp.sum(jnp.where(hit, seg_packed[:, None], 0), axis=0)
    seg_pair = swap_pair(seg_here)
    segs = jnp.where(lax.axis_index("s") == me, seg_here, seg_pair)
    segs = jnp.roll(segs.reshape(2, UNITS // 2), me, axis=0).reshape(UNITS)

    smalls = (query_bias, value_bias, out_bias, norm1_gain, norm1_shift, in_bias, down_bias, norm2_gain, norm2_shift)
    small_row = jnp.concatenate(smalls)
    small_size = small_row.shape[0]
    small_rows = jnp.zeros((8, D), bf16).at[0, :small_size].set(small_row)
    first = jnp.concatenate([qkv_weight[:, j * D : (j + 1) * D] for j in range(3)] + [small_rows], axis=0)
    second = jnp.concatenate([out_weight] + [in_weight[:, j * D : (j + 1) * D] for j in range(ff_cols)] + [down_weight], axis=0)
    first_all = gather_all(plan, first)
    second_all = gather_all(plan, second)
    small_all = first_all[:, 3 * rows_dev, :small_size]
    small_full = []
    at = 0
    for piece in smalls:
        size = piece.shape[0]
        small_full.append(small_all[:, at : at + size].reshape(count * size).astype(f32))
        at += size
    bias_q, bias_v, bias_o, gain1, shift1, bias_in, bias_down, gain2, shift2 = small_full

    def rows_of(buf, start, size):
        return buf[:, start : start + size].reshape(count * size, D)

    w_qkv = jnp.stack([rows_of(first_all, j * rows_dev, rows_dev) for j in range(3)])
    w_heads = jnp.stack([jnp.concatenate([w_qkv[j][:, c * width : (c + 1) * width] for j in range(3)], axis=1) for c in range(2)])
    bias_heads = jnp.stack([jnp.concatenate([bias_q[c * width : (c + 1) * width], jnp.zeros((width,), f32), bias_v[c * width : (c + 1) * width]]) for c in range(2)])
    fold = jnp.concatenate([jnp.full((width,), LOG2E * HD ** -0.5, f32), jnp.ones((2 * width,), f32)])
    w_mine, w_far = pick(w_heads, me), pick(w_heads, 1 - me)
    send = ((dot(tok, w_far) + pick(bias_heads, 1 - me)) * fold).astype(bf16)
    far = swap_pair(send)
    own = ((dot(tok, w_mine) + pick(bias_heads, me)) * fold).astype(bf16)
    o_own, o_far, lse = attention(segs, own, far)
    o_got = swap_pair(o_far)
    w_out = rows_of(second_all, 0, rows_dev)
    w_in = jnp.concatenate([rows_of(second_all, (1 + j) * rows_dev, rows_dev) for j in range(ff_cols)], axis=1)
    w_down = rows_of(second_all, (1 + ff_cols) * rows_dev, ff_dev)
    w_out_pair = w_out.reshape(2, width, D)
    out_mine, out_far = pick(w_out_pair, me), pick(w_out_pair, 1 - me)
    attn_out = dot(o_own, out_mine) + dot(o_got, out_far) + bias_o
    unit1, rstd1 = norm_stats(tok.astype(f32) + attn_out)
    hidden = unit1 * gain1 + shift1
    low = hidden.astype(bf16)
    inner = dot(low, w_in) + bias_in
    phi = 0.5 * (1.0 + lax.erf(inner * (0.5 ** 0.5)))
    act = (inner * phi).astype(bf16)
    slope = phi + inner * (jnp.exp(-0.5 * inner * inner) * 0.3989422804014327)
    unit2, rstd2 = norm_stats(hidden + dot(act, w_down) + bias_down)
    out_rows = (unit2 * gain2 + shift2).astype(bf16)
    output = relocate(out_rows)

    back = relocate(cotangent[0]).astype(f32)
    g_gain2 = jnp.sum(back * unit2, axis=0)
    g_shift2 = jnp.sum(back, axis=0)
    resid2 = norm_back(back, unit2, rstd2, gain2)
    branch = resid2.astype(bf16)
    g_bdown = jnp.sum(branch.astype(f32), axis=0)
    g_down = dot(act, branch, TN).astype(bf16)
    inner_grad = (dot(branch, w_down, NT) * slope).astype(bf16)
    g_bin = jnp.sum(inner_grad.astype(f32), axis=0)
    g_in = dot(low, inner_grad, TN).astype(bf16)
    blocks = [g_in[:, j * D : (j + 1) * D].reshape(count, rows_dev, D) for j in range(ff_cols)]
    ffn_sum = reduce_all(plan, jnp.concatenate(blocks + [g_down.reshape(count, ff_dev, D)], axis=1))
    hidden_grad = resid2 + dot(inner_grad, w_in, NT)
    g_gain1 = jnp.sum(hidden_grad * unit1, axis=0)
    g_shift1 = jnp.sum(hidden_grad, axis=0)
    resid1 = norm_back(hidden_grad, unit1, rstd1, gain1)
    attn_grad = resid1.astype(bf16)
    g_bout = jnp.sum(attn_grad.astype(f32), axis=0)
    d_far = dot(attn_grad, out_far, NT).astype(bf16)
    d_got = swap_pair(d_far)
    d_own = dot(attn_grad, out_mine, NT).astype(bf16)
    g_out_mine = dot(o_own, attn_grad, TN).astype(bf16)
    g_out_far = dot(o_got, attn_grad, TN).astype(bf16)
    g_out = jnp.stack([jnp.where(me == 0, g_out_mine, g_out_far), jnp.where(me == 0, g_out_far, g_out_mine)]).reshape(D, D)
    pieces = attention_back(segs, own, far, o_own, o_far, d_own, d_got, lse)
    back_own = jnp.concatenate(pieces[0::2], axis=1)
    back_got = swap_pair(jnp.concatenate(pieces[1::2], axis=1))
    sums_own = jnp.sum(back_own.astype(f32), axis=0)
    sums_got = jnp.sum(back_got.astype(f32), axis=0)

    def order_heads(mine, other):
        return jnp.where(me == 0, mine, other), jnp.where(me == 0, other, mine)

    lo, hi = order_heads(sums_own, sums_got)
    g_bq = jnp.concatenate([lo[:width], hi[:width]])
    g_bv = jnp.concatenate([lo[2 * width :], hi[2 * width :]])
    g_lo, g_hi = order_heads(dot(tok, back_own, TN).astype(bf16), dot(tok, back_got, TN).astype(bf16))
    g_parts = [jnp.concatenate([g_lo[:, j * width : (j + 1) * width], g_hi[:, j * width : (j + 1) * width]], axis=1).reshape(count, rows_dev, D) for j in range(3)]
    small_grads = (g_bq, g_bv, g_bout, g_gain1, g_shift1, g_bin, g_bdown, g_gain2, g_shift2)
    small_back = jnp.concatenate([g.reshape(count, -1) for g in small_grads], axis=1).astype(bf16)
    small_back = jnp.zeros((count, 8, D), bf16).at[:, 0, :small_size].set(small_back)
    attn_sum = reduce_all(plan, jnp.concatenate(g_parts + [g_out.reshape(count, rows_dev, D), small_back], axis=1))
    packed_grad = (resid1 + dot(back_own, w_mine, NT) + dot(back_got, w_far, NT)).astype(bf16)
    input_grad = relocate(packed_grad)

    out_qkv = jnp.concatenate([attn_sum[j * rows_dev : (j + 1) * rows_dev] for j in range(3)], axis=1)
    out_out = attn_sum[3 * rows_dev : 4 * rows_dev]
    out_in = jnp.concatenate([ffn_sum[j * rows_dev : (j + 1) * rows_dev] for j in range(ff_cols)], axis=1)
    out_down = ffn_sum[ff_cols * rows_dev :]
    line = attn_sum[4 * rows_dev]
    small_out = []
    at = 0
    for piece in smalls:
        small_out.append(line[at : at + piece.shape[0]])
        at += piece.shape[0]
    s = small_out
    return (output[None], input_grad[None], out_qkv, s[0], s[1], out_out, s[2], s[3], s[4], out_in, s[5], out_down, s[6], s[7], s[8])


def solution(mesh):
    plan = Plan(mesh.shape["seq"], mesh.shape["fsdp"])
    inner_mesh = Mesh(mesh.devices.reshape(plan.dims), tuple(plan.names))
    groups = tuple(plan.names[1:])
    every = tuple(plan.names)
    rows = P(groups, "s", None)
    table = P(groups, None)
    mat = P(every, None)
    vec = P(every)
    placed = (rows, table, table, mat, vec, vec, mat, vec, vec, vec, mat, vec, mat, vec, vec, vec, rows)
    outs = (rows, rows, mat, vec, vec, mat, vec, vec, vec, mat, vec, mat, vec, vec, vec)

    def run(*args):
        return local(plan, *args)

    return jax.shard_map(run, mesh=inner_mesh, in_specs=placed, out_specs=outs, check_vma=False)
```

```python
import jax
import jax.numpy as jnp
import numpy as np
from jax import lax
from jax.sharding import Mesh, PartitionSpec as P
from jax.experimental import pallas as pl
from jax.experimental.pallas import tpu as pltpu

D = 768
HALF = D // 2
HD = 64
UNITS = 16
SLOTS = 16
ROWS = D // SLOTS
PAIRS = HALF // 128
LOG2E = 1.4426950408889634
LN2 = 0.6931471805599453
BIG = 1e30
TQ = 512
STEP = 512
TM = 256
norm_eps = 1e-12
bf16 = jnp.bfloat16
f32 = jnp.float32
NT = (((1,), (1,)), ((), ()))
NN = (((1,), (0,)), ((), ()))
TN = (((0,), (0,)), ((), ()))
VMEM_CAP = 58 << 20


def mxu(a, b, dims=NN):
    return lax.dot_general(a, b, dims, preferred_element_type=f32)


def shape(size, kind=bf16):
    return jax.ShapeDtypeStruct(size, kind)


def params(axes=1):
    return pltpu.CompilerParams(dimension_semantics=("arbitrary",) * axes, vmem_limit_bytes=VMEM_CAP)


def cost(flops, moved):
    return pl.CostEstimate(flops=int(flops), bytes_accessed=int(moved), transcendentals=0)


def tie(value, *others):
    return lax.optimization_barrier((value,) + others)[0]


def lanes(rows):
    return lax.broadcasted_iota(jnp.int32, (rows, 128), 1)


def seg_rows(segs_ref, base_block, rows):
    place = lax.broadcasted_iota(jnp.int32, (rows, 128), 0)
    out = jnp.zeros((rows, 128), jnp.int32)
    for b in range(rows // 128):
        out = jnp.where(place >= b * 128, segs_ref[base_block + b], out)
    return out


def split3(v):
    hi = v.astype(bf16).astype(f32)
    mid = (v - hi).astype(bf16).astype(f32)
    return hi, mid, v - hi - mid


def both_heads(pair_rows):
    lane = lanes(pair_rows.shape[0])
    zero = jnp.zeros_like(pair_rows)
    first = jnp.where(lane < HD, pair_rows, zero)
    return jnp.concatenate([first, jnp.where(lane < HD, zero, pair_rows)], axis=0)


def fill_keys(segs_ref, k_in, v_in, k_aug, v_aug):
    for at in range(0, k_in.shape[0], STEP):
        rows = slice(at, at + STEP)
        lane = lanes(STEP)
        hot = (lane == seg_rows(segs_ref, at // 128, STEP)) | ((lane >= 64) & (lane < 67))
        k_aug[rows, :128] = k_in[rows, :]
        k_aug[rows, 128:] = jnp.where(hot, 1.0, 0.0).astype(bf16)
        v_aug[rows, :128] = v_in[rows, :]
        v_aug[rows, 128:] = jnp.ones((STEP, 128), bf16)


def attend_body(segs_ref, q_in, k_in, v_in, *refs):
    o_own, o_far, lse_ref, k_aug, v_aug = refs[-5:]
    i = pl.program_id(1)
    n_half = pl.num_programs(1) // 2

    @pl.when(i == 0)
    def _():
        fill_keys(segs_ref, k_in, v_in, k_aug, v_aug)

    lane = lanes(TQ)
    seg = seg_rows(segs_ref, i * (TQ // 128), TQ)
    off = jnp.where((lane < 16) & (lane != seg), -BIG, 0.0).astype(bf16)
    q_aug = jnp.concatenate([both_heads(q_in[...]), jnp.concatenate([off, off], axis=0)], axis=1)
    top = None
    acc = None
    for at in range(0, k_aug.shape[0], STEP):
        s = mxu(q_aug, k_aug[at : at + STEP, :], NT)
        here = jnp.max(s, axis=1, keepdims=True)
        new_top = here if top is None else jnp.maximum(top, here)
        p = jnp.exp2(s - new_top).astype(bf16)
        add = mxu(p, v_aug[at : at + STEP, :])
        acc = add if acc is None else acc * jnp.exp2(top - new_top) + add
        top = new_top
    both = jnp.where(lane < HD, acc[:TQ, :128], acc[TQ:, :128])
    sums = jnp.where(lane < HD, acc[:TQ, 128:], acc[TQ:, 128:])
    tops = jnp.where(lane < HD, top[:TQ], top[TQ:])
    out = (both / sums).astype(bf16)
    lse_ref[...] = tops + jnp.log2(sums)

    @pl.when(i < n_half)
    def _():
        o_own[...] = out

    @pl.when(i >= n_half)
    def _():
        o_far[...] = out


def anyspec():
    return pl.BlockSpec(memory_space=pl.ANY)


def pair_specs(n_half, first):
    own = pl.BlockSpec((TQ, 128), lambda h, i, *_: (jnp.minimum(i, n_half - 1), first + h))
    far = pl.BlockSpec((TQ, 128), lambda h, i, *_: (jnp.maximum(i - n_half, 0), first + h))
    return own, far


def attention(segs, qkv, first, count, prev):
    total = qkv.shape[0]
    half = total // 2
    n_half = half // TQ
    own, far = pair_specs(n_half, first)
    row = pl.BlockSpec((TQ, 128), lambda h, i, *_: (i, first + h))
    whole = lambda part: pl.BlockSpec((total, 128), lambda h, i, *_: (0, part * PAIRS + first + h))
    prev = () if prev is None else tuple(prev)
    return pl.pallas_call(
        attend_body,
        grid_spec=pltpu.PrefetchScalarGridSpec(
            num_scalar_prefetch=1,
            grid=(count, 2 * n_half),
            in_specs=[row, whole(1), whole(2)] + [anyspec()] * len(prev),
            out_specs=[own, far, row],
            scratch_shapes=[pltpu.VMEM((total, 256), bf16), pltpu.VMEM((total, 256), bf16)],
        ),
        out_shape=[shape((half, HALF)), shape((half, HALF)), shape((total, HALF), f32)],
        input_output_aliases={4 + j: j for j in range(len(prev))},
        compiler_params=params(2),
        cost_estimate=cost(count * total * total * 2048, total * 128 * 2 * 8),
    )(segs, qkv, qkv, qkv, *prev)


def attend_back_body(segs_ref, q_in, k_in, v_in, o_own, o_far, d_own, d_far, lse_ref, *refs):
    dq_out, dk_out, dv_out, k_aug, v_aug, dk_acc, dv_acc = refs[-7:]
    i = pl.program_id(1)
    n = pl.num_programs(1)

    @pl.when(i == 0)
    def _():
        fill_keys(segs_ref, k_in, v_in, k_aug, v_aug)
        dk_acc[...] = jnp.zeros_like(dk_acc)
        dv_acc[...] = jnp.zeros_like(dv_acc)

    near = i < n // 2
    d_rows = jnp.where(near, d_own[...], d_far[...])
    o_rows = jnp.where(near, o_own[...], o_far[...])
    lane = lanes(TQ)
    seg = seg_rows(segs_ref, i * (TQ // 128), TQ)
    off = jnp.where((lane < 16) & (lane != seg), -BIG, 0.0)
    prod = d_rows.astype(f32) * o_rows.astype(f32)
    q_side, d_side = [], []
    for head in range(2):
        mine = (lane < HD) if head == 0 else (lane >= HD)
        dot_row = jnp.sum(jnp.where(mine, prod, 0.0), axis=1, keepdims=True)
        lse = jnp.broadcast_to(lse_ref[:, head * HD : head * HD + 1], (TQ, 128))
        for side, value, rest in ((q_side, -lse, off), (d_side, -jnp.broadcast_to(dot_row, (TQ, 128)), 0.0)):
            h, m, l = split3(value)
            cols = jnp.where(lane == 64, h, jnp.where(lane == 65, m, jnp.where(lane == 66, l, rest)))
            side.append(cols.astype(bf16))
    q2 = both_heads(q_in[...])
    d2 = both_heads(d_rows)
    q_aug = jnp.concatenate([q2, jnp.concatenate(q_side, axis=0)], axis=1)
    d_aug = jnp.concatenate([d2, jnp.concatenate(d_side, axis=0)], axis=1)
    dq = None
    for at in range(0, k_aug.shape[0], STEP):
        rows = slice(at, at + STEP)
        keys = k_aug[rows, :]
        p = jnp.exp2(mxu(q_aug, keys, NT))
        ds = (p * mxu(d_aug, v_aug[rows, :], NT)).astype(bf16)
        dv_acc[rows, :] += mxu(p.astype(bf16), d2, TN)
        dk_acc[rows, :] += mxu(ds, q2, TN)
        add = mxu(ds, keys[:, :128])
        dq = add if dq is None else dq + add
    dq_out[...] = (jnp.where(lane < HD, dq[:TQ], dq[TQ:]) * (HD ** -0.5)).astype(bf16)

    @pl.when(i == n - 1)
    def _():
        dk_out[...] = (dk_acc[...] * LN2).astype(bf16)
        dv_out[...] = dv_acc[...].astype(bf16)


def attention_back(segs, qkv, o_own, o_far, d_own, d_far, lse, first, count, prev):
    total = qkv.shape[0]
    half = total // 2
    n_half = half // TQ
    own, far = pair_specs(n_half, first)
    row = pl.BlockSpec((TQ, 128), lambda h, i, *_: (i, first + h))
    whole = lambda part: pl.BlockSpec((total, 128), lambda h, i, *_: (0, part * PAIRS + first + h))
    prev = () if prev is None else tuple(prev)
    return pl.pallas_call(
        attend_back_body,
        grid_spec=pltpu.PrefetchScalarGridSpec(
            num_scalar_prefetch=1,
            grid=(count, 2 * n_half),
            in_specs=[row, whole(1), whole(2), own, far, own, far, row] + [anyspec()] * len(prev),
            out_specs=[row, whole(0), whole(0)],
            scratch_shapes=[
                pltpu.VMEM((total, 256), bf16),
                pltpu.VMEM((total, 256), bf16),
                pltpu.VMEM((total, 128), f32),
                pltpu.VMEM((total, 128), f32),
            ],
        ),
        out_shape=[shape((total, HALF))] * 3,
        input_output_aliases={9 + j: j for j in range(len(prev))},
        compiler_params=params(2),
        cost_estimate=cost(count * total * total * 5120, total * 128 * 2 * 12),
    )(segs, qkv, qkv, qkv, o_own, o_far, d_own, d_far, lse, *prev)


def each_slot(pieces):
    at = 0
    for ref in pieces:
        for slot in range(ref.shape[0]):
            yield at, ref, slot
            at += 1


def wait_for(dst, sem):
    pltpu.make_async_copy(dst, dst, sem).wait()


def proj_body(info, t_own, t_got, bias, *refs):
    pieces, (out, w_out, w, sem) = refs[:-4], refs[-4:]
    i = pl.program_id(0)

    @pl.when(i == 0)
    def _():
        for at, ref, slot in each_slot(pieces):
            rows = pl.ds(pl.multiple_of(info[1 + at] * ROWS, ROWS), ROWS)
            for j in range(3):
                src = ref.at[slot, j * ROWS : (j + 1) * ROWS, :]
                pltpu.make_async_copy(src, w.at[rows, j * HALF : (j + 1) * HALF], sem).start()
        wait_for(w, sem)

    tile = jnp.where(i < pl.num_programs(0) // 2, t_own[...], t_got[...])
    for j in range(3):
        cols = slice(j * HALF, (j + 1) * HALF)
        part = mxu(tile, w[:, cols]) + bias[0:1, cols]
        if j == 0:
            part = part * (LOG2E * HD ** -0.5)
        out[:, cols] = part.astype(bf16)
    w_out[...] = w[...]


def project(info, t_own, t_got, bias, pieces):
    half = t_own.shape[0]
    tile = 512
    n_half = half // tile
    own = pl.BlockSpec((tile, D), lambda i, *_: (jnp.minimum(i, n_half - 1), 0))
    got = pl.BlockSpec((tile, D), lambda i, *_: (jnp.maximum(i - n_half, 0), 0))
    return pl.pallas_call(
        proj_body,
        grid_spec=pltpu.PrefetchScalarGridSpec(
            num_scalar_prefetch=1,
            grid=(2 * n_half,),
            in_specs=[own, got, pl.BlockSpec((1, 3 * HALF), lambda i, *_: (0, 0))] + [anyspec()] * len(pieces),
            out_specs=[
                pl.BlockSpec((tile, 3 * HALF), lambda i, *_: (i, 0)),
                pl.BlockSpec((D, 3 * HALF), lambda i, *_: (0, 0)),
            ],
            scratch_shapes=[pltpu.VMEM((D, 3 * HALF), bf16), pltpu.SemaphoreType.DMA],
        ),
        out_shape=[shape((2 * half, 3 * HALF)), shape((D, 3 * HALF))],
        compiler_params=params(),
        cost_estimate=cost(half * D * D * 6, half * D * 12),
    )(info, t_own, t_got, bias, *pieces)


def norm_stats(rows):
    mean = jnp.mean(rows, axis=-1, keepdims=True)
    centered = rows - mean
    var = jnp.mean(centered * centered, axis=-1, keepdims=True)
    rstd = lax.rsqrt(var + norm_eps)
    return centered * rstd, rstd


def norm_back(grad, unit, rstd, gain):
    eg = grad * gain
    mean_eg = jnp.mean(eg, axis=-1, keepdims=True)
    mean_en = jnp.mean(eg * unit, axis=-1, keepdims=True)
    return (eg - mean_eg - unit * mean_en) * rstd


def mid_body(info, tok, o_own, o_got, back, vecs, bias_in, *refs):
    n_out = 10
    outs, scratch = refs[-n_out - 5 : -5], refs[-5:]
    pieces = refs[: -n_out - 5]
    own_pieces, far_pieces = pieces[: len(pieces) // 2], pieces[len(pieces) // 2 :]
    out_rows, act_out, ig_out, low_out, branch_out, attn_out, resid_out, d_own, d_far, sums = outs
    w_out, w_in, w_down, slope, sems = scratch
    ff_cols = w_in.shape[1] // D
    me = info[0]

    @pl.when(pl.program_id(0) == 0)
    def _():
        for kind in range(3):
            for here, part in ((me, own_pieces), (1 - me, far_pieces)):
                for at, ref, slot in each_slot(part):
                    chip = info[1 + at]
                    lane0 = pl.multiple_of(here * HALF, HALF)
                    rows = pl.ds(pl.multiple_of(chip * ROWS, ROWS), ROWS)
                    if kind == 0:
                        pltpu.make_async_copy(ref.at[slot, 0:ROWS, :], w_out.at[rows, pl.ds(lane0, HALF)], sems.at[0]).start()
                    elif kind == 1:
                        for j in range(ff_cols):
                            src = ref.at[slot, (1 + j) * ROWS : (2 + j) * ROWS, :]
                            dst = w_in.at[rows, pl.ds(pl.multiple_of(lane0 + j * D, HALF), HALF)]
                            pltpu.make_async_copy(src, dst, sems.at[1]).start()
                    else:
                        size = ROWS * ff_cols
                        src = ref.at[slot, (1 + ff_cols) * ROWS : (1 + 2 * ff_cols) * ROWS, :]
                        dst = w_down.at[pl.ds(pl.multiple_of(chip * size, size), size), pl.ds(lane0, HALF)]
                        pltpu.make_async_copy(src, dst, sems.at[2]).start()
        sums[...] = jnp.zeros_like(sums)
        wait_for(w_out, sems.at[0])

    bias_o, gain1, shift1 = vecs[0:1, :], vecs[1:2, :], vecs[2:3, :]
    bias_d, gain2, shift2 = vecs[3:4, :], vecs[4:5, :], vecs[5:6, :]
    mine = w_out[pl.ds(pl.multiple_of(me * HALF, HALF), HALF), :]
    other = w_out[pl.ds(pl.multiple_of((1 - me) * HALF, HALF), HALF), :]
    resid = tok[...].astype(f32) + mxu(o_own[...], mine) + mxu(o_got[...], other) + bias_o
    unit1, rstd1 = norm_stats(resid)
    hidden = unit1 * gain1 + shift1
    low = hidden.astype(bf16)
    low_out[...] = low

    @pl.when(pl.program_id(0) == 0)
    def _():
        wait_for(w_in, sems.at[1])
        wait_for(w_down, sems.at[2])

    branch = bias_d
    for j in range(ff_cols):
        cols = slice(j * D, (j + 1) * D)
        inner = mxu(low, w_in[:, cols]) + bias_in[:, cols]
        phi = 0.5 + 0.5 * lax.erf(inner * (0.5 ** 0.5))
        act = (inner * phi).astype(bf16)
        act_out[:, cols] = act
        slope[:, cols] = phi + inner * (jnp.exp2(inner * inner * (-0.5 * LOG2E)) * 0.3989422804014327)
        branch = branch + mxu(act, w_down[cols, :])
    unit2, rstd2 = norm_stats(hidden + branch)
    out_rows[...] = (unit2 * gain2 + shift2).astype(bf16)
    grad = back[...].astype(f32)
    resid2 = norm_back(grad, unit2, rstd2, gain2)
    low_branch = resid2.astype(bf16)
    branch_out[...] = low_branch
    hidden_grad = resid2
    for j in range(ff_cols):
        cols = slice(j * D, (j + 1) * D)
        ig = (mxu(low_branch, w_down[cols, :], NT) * slope[:, cols]).astype(bf16)
        ig_out[:, cols] = ig
        hidden_grad = hidden_grad + mxu(ig, w_in[:, cols], NT)
        sums[3 + j : 4 + j, :] += jnp.sum(ig.astype(f32), axis=0, keepdims=True)
    resid1 = norm_back(hidden_grad, unit1, rstd1, gain1)
    resid_out[...] = resid1
    attn_grad = resid1.astype(bf16)
    attn_out[...] = attn_grad
    d_own[...] = mxu(attn_grad, mine, NT).astype(bf16)
    d_far[...] = mxu(attn_grad, other, NT).astype(bf16)
    rows = (
        (0, attn_grad.astype(f32)),
        (1, hidden_grad * unit1),
        (2, hidden_grad),
        (3 + ff_cols, low_branch.astype(f32)),
        (4 + ff_cols, grad * unit2),
        (5 + ff_cols, grad),
    )
    for at, value in rows:
        sums[at : at + 1, :] += jnp.sum(value, axis=0, keepdims=True)


def middle(info, tok, o_own, o_got, back, vecs, bias_in, own_pieces, far_pieces):
    half = tok.shape[0]
    ff = bias_in.shape[1]
    wide = pl.BlockSpec((TM, D), lambda i, *_: (i, 0))
    thin = pl.BlockSpec((TM, HALF), lambda i, *_: (i, 0))
    full = pl.BlockSpec((TM, ff), lambda i, *_: (i, 0))
    fixed = lambda rows, cols: pl.BlockSpec((rows, cols), lambda i, *_: (0, 0))
    pieces = tuple(own_pieces) + tuple(far_pieces)
    return pl.pallas_call(
        mid_body,
        grid_spec=pltpu.PrefetchScalarGridSpec(
            num_scalar_prefetch=1,
            grid=(half // TM,),
            in_specs=[wide, thin, thin, wide, fixed(8, D), fixed(1, ff)] + [anyspec()] * len(pieces),
            out_specs=[wide, full, full, wide, wide, wide, wide, thin, thin, fixed(16, D)],
            scratch_shapes=[
                pltpu.VMEM((D, D), bf16),
                pltpu.VMEM((D, ff), bf16),
                pltpu.VMEM((ff, D), bf16),
                pltpu.VMEM((TM, ff), f32),
                pltpu.SemaphoreType.DMA((3,)),
            ],
        ),
        out_shape=[
            shape((half, D)),
            shape((half, ff)),
            shape((half, ff)),
            shape((half, D)),
            shape((half, D)),
            shape((half, D)),
            shape((half, D), f32),
            shape((half, HALF)),
            shape((half, HALF)),
            shape((16, D), f32),
        ],
        compiler_params=params(),
        cost_estimate=cost(half * D * (D + 2 * ff) * 4, half * D * 40),
    )(info, tok, o_own, o_got, back, vecs, bias_in, *pieces)


def wgrad_body(info, act, ig, low, branch, o_own, o_got, attn_grad, keep, send, res_in, res_down, res_out, sems):
    j = pl.program_id(0)
    n = pl.num_programs(0)
    me = info[0]
    par = lax.rem(j, 2)
    down_rows = ROWS * n
    per_step = SLOTS // n

    @pl.when(j == 0)
    def _():
        for at, dst in ((0, send), (1, keep)):
            half_at = me if at == 1 else 1 - me
            lane = pl.ds(pl.multiple_of(half_at * HALF, HALF), HALF)
            grad = attn_grad[:, lane]
            for here, rows in ((me, o_own), (1 - me, o_got)):
                spot = pl.ds(pl.multiple_of(here * HALF, HALF), HALF)
                res_out[at, spot, :] = mxu(rows[...], grad, TN).astype(bf16)
            for chip in range(SLOTS):
                src = res_out.at[at, chip * ROWS : (chip + 1) * ROWS, :]
                pltpu.make_async_copy(src, dst.at[info[1 + chip], 0:ROWS, :], sems.at[2]).start()

    for at, dst in ((0, send), (1, keep)):
        half_at = me if at == 1 else 1 - me
        lane = pl.ds(pl.multiple_of(half_at * HALF, HALF), HALF)
        res_in[par, at] = mxu(low[...], ig[:, lane], TN).astype(bf16)
        for chip in range(SLOTS):
            src = res_in.at[par, at, chip * ROWS : (chip + 1) * ROWS, :]
            spot = pl.ds(pl.multiple_of((1 + j) * ROWS, ROWS), ROWS)
            pltpu.make_async_copy(src, dst.at[info[1 + chip], spot, :], sems.at[par]).start()
        res_down[par, at] = mxu(act[...], branch[:, lane], TN).astype(bf16)
        for q in range(per_step):
            src = res_down.at[par, at, q * down_rows : (q + 1) * down_rows, :]
            slot = info[1 + j * per_step + q]
            pltpu.make_async_copy(src, dst.at[slot, ROWS * (1 + n) : ROWS * (1 + 2 * n), :], sems.at[par]).start()

    def settle(which):
        wait_for(res_in.at[which], sems.at[which])
        wait_for(res_down.at[which], sems.at[which])

    @pl.when(j > 0)
    def _():
        settle(1 - par)

    @pl.when(j == n - 1)
    def _():
        settle(par)
        wait_for(res_out, sems.at[2])


def weight_grads(info, act, ig, low, branch, o_own, o_got, attn_grad):
    half, ff = act.shape
    n = ff // D
    strip = pl.BlockSpec((half, D), lambda j, *_: (0, j))
    fixed = lambda cols: pl.BlockSpec((half, cols), lambda j, *_: (0, 0))
    size = (SLOTS, ROWS * (1 + 2 * n), HALF)
    return pl.pallas_call(
        wgrad_body,
        grid_spec=pltpu.PrefetchScalarGridSpec(
            num_scalar_prefetch=1,
            grid=(n,),
            in_specs=[strip, strip, fixed(D), fixed(D), fixed(HALF), fixed(HALF), fixed(D)],
            out_specs=[anyspec(), anyspec()],
            scratch_shapes=[
                pltpu.VMEM((2, 2, D, HALF), bf16),
                pltpu.VMEM((2, 2, D, HALF), bf16),
                pltpu.VMEM((2, D, HALF), bf16),
                pltpu.SemaphoreType.DMA((3,)),
            ],
        ),
        out_shape=[shape(size), shape(size)],
        compiler_params=params(),
        cost_estimate=cost(half * D * (D + 2 * ff) * 2, half * ff * 8),
    )(info, act, ig, low, branch, o_own, o_got, attn_grad)


def qkv_grad_body(info, small, t_own, t_got, dq, dk, dv, out, t_all, d_all, res, res_small, sems):
    half = t_own.shape[0]
    pltpu.make_async_copy(t_own, t_all.at[0:half, :], sems.at[0]).start()
    pltpu.make_async_copy(t_got, t_all.at[half:, :], sems.at[0]).start()
    for j, src in enumerate((dq, dk, dv)):
        pltpu.make_async_copy(src, d_all.at[j], sems.at[1 + j]).start()
    wait_for(t_all, sems.at[0])
    res_small[...] = small[...].astype(bf16)
    row = lax.broadcasted_iota(jnp.int32, (16, HALF), 0)
    for j in range(3):
        wait_for(d_all.at[j], sems.at[1 + j])
        grads = d_all[j]
        res[j] = mxu(t_all[...], grads, TN).astype(bf16)
        for chip in range(SLOTS):
            src = res.at[j, chip * ROWS : (chip + 1) * ROWS, :]
            pltpu.make_async_copy(src, out.at[info[1 + chip], j * ROWS : (j + 1) * ROWS, :], sems.at[4]).start()
        if j != 1:
            total = jnp.sum(grads.astype(f32), axis=0, keepdims=True)
            place = 14 if j == 0 else 15
            res_small[...] = jnp.where(row == place, total, res_small[...].astype(f32)).astype(bf16)
    for slot in range(SLOTS):
        pltpu.make_async_copy(res_small, out.at[slot, 3 * ROWS : 3 * ROWS + 16, :], sems.at[5]).start()
    wait_for(res, sems.at[4])
    for slot in range(SLOTS):
        pltpu.make_async_copy(res_small, out.at[slot, 3 * ROWS : 3 * ROWS + 16, :], sems.at[5]).wait()


def qkv_grads(info, small, t_own, t_got, dq, dk, dv):
    total = dq.shape[0]
    return pl.pallas_call(
        qkv_grad_body,
        grid_spec=pltpu.PrefetchScalarGridSpec(
            num_scalar_prefetch=1,
            grid=(),
            in_specs=[pl.BlockSpec(memory_space=pltpu.VMEM)] + [anyspec()] * 5,
            out_specs=anyspec(),
            scratch_shapes=[
                pltpu.VMEM((total, D), bf16),
                pltpu.VMEM((3, total, HALF), bf16),
                pltpu.VMEM((3, D, HALF), bf16),
                pltpu.VMEM((16, HALF), bf16),
                pltpu.SemaphoreType.DMA((6,)),
            ],
        ),
        out_shape=shape((SLOTS, 3 * ROWS + 16, HALF)),
        compiler_params=pltpu.CompilerParams(vmem_limit_bytes=VMEM_CAP),
        cost_estimate=cost(total * D * HALF * 6, total * D * 5),
    )(info, small, t_own, t_got, dq, dk, dv)


def input_back_body(*refs):
    w = refs[0]
    dq, dk, dv = refs[1:4]
    out = refs[-1]
    total = None
    for j, part in enumerate((dq, dk, dv)):
        add = mxu(part[...], w[:, j * HALF : (j + 1) * HALF], NT)
        total = add if total is None else total + add
    for extra in refs[4:-1]:
        total = total + extra[...].astype(f32)
    out[...] = total.astype(bf16)


def input_back(w, dq, dk, dv, far, extras):
    half = dq.shape[0] // 2
    tile = 512
    base = half // tile if far else 0
    part = pl.BlockSpec((tile, HALF), lambda i: (base + i, 0))
    row = pl.BlockSpec((tile, D), lambda i: (i, 0))
    return pl.pallas_call(
        input_back_body,
        grid=(half // tile,),
        in_specs=[pl.BlockSpec((D, 3 * HALF), lambda i: (0, 0)), part, part, part] + [row] * len(extras),
        out_specs=row,
        out_shape=shape((half, D)),
        compiler_params=params(),
        cost_estimate=cost(half * D * HALF * 6, half * D * 8),
    )(w, dq, dk, dv, *extras)


def shift(n, k):
    return [(i, (i + k) % n) for i in range(n)]


class Plan:
    def __init__(self, seq, fsdp):
        rest = fsdp // 2
        dims = []
        while rest > 1:
            want = 4 if len(dims) % 2 == 0 and rest % 4 == 0 else 2
            dims.append(want)
            rest //= want
        self.dims = [seq] + dims + [2]
        self.names = ["s"] + ["r%d" % i for i in range(len(dims))] + ["c"]
        self.chips = seq * fsdp // 2
        self.direct = self.dims == [2, 4, 2, 2]
        self.stages = ([1] if dims else []) + [0] + list(range(2, len(dims) + 1))

    def at(self, a):
        return lax.axis_index(self.names[a])

    def chip_table(self, sign):
        if not self.direct:
            return jnp.arange(SLOTS, dtype=jnp.int32)
        spots = []
        for dx, dy in ((0, 0), (1, 0), (0, 1), (1, 1)):
            spots += [(dx, dy, z) for z in range(4)]
        dx, dy, dz = (jnp.asarray(v, jnp.int32) for v in zip(*spots))
        return ((self.at(0) + sign * dx) % 2) * 8 + ((self.at(1) + sign * dz) % 4) * 2 + (self.at(2) + sign * dy) % 2

    def slot_table(self, sign):
        table = self.chip_table(sign)
        hit = table[:, None] == jnp.arange(SLOTS, dtype=jnp.int32)[None, :]
        return jnp.sum(jnp.where(hit, jnp.arange(SLOTS, dtype=jnp.int32)[:, None], 0), axis=0)

    def places(self, sign):
        grid = np.indices(self.dims[:-1]).reshape(len(self.dims) - 1, -1)
        flat = jnp.zeros((self.chips,), jnp.int32)
        if sign < 0:
            for a in reversed(self.stages):
                n = self.dims[a]
                flat = flat * n + (self.at(a) - jnp.asarray(grid[a], jnp.int32)) % n
            return flat
        sizes = [self.dims[a] for a in reversed(self.stages)]
        offs = np.indices(sizes).reshape(len(sizes), -1)
        by_axis = {a: offs[j] for j, a in enumerate(reversed(self.stages))}
        for a in range(len(self.dims) - 1):
            n = self.dims[a]
            flat = flat * n + (self.at(a) + jnp.asarray(by_axis[a], jnp.int32)) % n
        return flat

    def send(self, x, a, k=1):
        return lax.ppermute(x, self.names[a], shift(self.dims[a], k))


def gather_chips(plan, unit):
    buf = unit[None]
    for a in plan.stages:
        n = plan.dims[a]
        if n > 1:
            buf = jnp.concatenate([buf] + [plan.send(buf, a, k) for k in range(1, n)], axis=0)
    return jnp.take(buf, plan.places(-1), axis=0, mode="clip")


def reduce_chips(plan, grads):
    buf = jnp.take(grads, plan.places(1), axis=0, mode="clip")
    for a in reversed(plan.stages):
        n = plan.dims[a]
        size = buf.shape[0] // n
        keep = buf[:size].astype(f32)
        for k in range(1, n):
            keep = keep + plan.send(buf[k * size : (k + 1) * size].astype(bf16), a, k).astype(f32)
        buf = keep if a == plan.stages[0] else keep.astype(bf16)
    return buf[0]


def regroup(buf, sizes, count):
    n, _, w = buf.shape
    parts = []
    at = 0
    for size in sizes:
        parts.append(buf[:, at : at + size].reshape(count, n * size // count, w))
        at += size
    return jnp.concatenate(parts, axis=1)


def gather_z(plan, unit):
    return jnp.concatenate([unit[None]] + [plan.send(unit, 1, k)[None] for k in range(1, 4)], axis=0)


def swap_pair(x):
    return lax.ppermute(x, "c", [(0, 1), (1, 0)])


def relocate(x):
    return lax.ppermute(x, ("s", "c"), [(0, 0), (1, 2), (2, 1), (3, 3)])


def half_of(x, at):
    return lax.dynamic_slice_in_dim(x, at * HALF, HALF, axis=x.ndim - 1)


def chip_units(me, mine, got, sizes):
    low = jnp.where(me == 0, mine, got)
    high = jnp.where(me == 0, got, mine)
    parts = []
    at = 0
    for size in sizes:
        parts += [low[at : at + size], high[at : at + size]]
        at += size
    return jnp.concatenate(parts, axis=0)


def own_rows(me, total, sizes):
    first, second = [], []
    at = 0
    for size in sizes:
        first.append(total[at : at + size])
        second.append(total[at + size : at + 2 * size])
        at += 2 * size
    first = jnp.concatenate(first, axis=0)
    second = jnp.concatenate(second, axis=0)
    return jnp.where(me == 0, first, second), jnp.where(me == 0, second, first)


def local(plan, tokens, lengths, block_order, qkv_weight, query_bias, value_bias, out_weight, out_bias,
          norm1_gain, norm1_shift, in_weight, in_bias, down_weight, down_bias, norm2_gain, norm2_shift, cotangent):
    half = tokens.shape[1]
    me = plan.at(len(plan.dims) - 1)
    rows_dev = qkv_weight.shape[0]
    ff_dev = down_weight.shape[0]
    ff_cols = in_weight.shape[1] // D
    me32 = me.astype(jnp.int32)
    pull = jnp.concatenate([me32[None], plan.chip_table(-1)])
    push = jnp.concatenate([me32[None], plan.slot_table(1)])

    sizes1 = [rows_dev] * 3
    sizes2 = [rows_dev] * (1 + ff_cols) + [ff_dev]
    first = jnp.concatenate([qkv_weight[:, j * D : (j + 1) * D] for j in range(3)], axis=0)
    second = jnp.concatenate([out_weight] + [in_weight[:, j * D : (j + 1) * D] for j in range(ff_cols)] + [down_weight], axis=0)
    smalls = (query_bias, value_bias, out_bias, norm1_gain, norm1_shift, in_bias, down_bias, norm2_gain, norm2_shift)
    line = jnp.concatenate(smalls)
    both = jnp.concatenate([first, second], axis=0)
    got = swap_pair(half_of(both, 1 - me))
    mine = half_of(both, me)
    cut = 3 * rows_dev
    unit1 = chip_units(me, mine[:cut], got[:cut], sizes1)
    unit2 = chip_units(me, mine[cut:], got[cut:], sizes2)
    line_got = swap_pair(line)
    line_unit = jnp.stack([jnp.where(me == 0, line, line_got), jnp.where(me == 0, line_got, line)])

    tok = relocate(tokens[0])
    if plan.direct:
        z1 = gather_z(plan, unit1)
        x1, y1 = plan.send(z1, 0), plan.send(z1, 2)
        pieces1 = [z1, x1, y1, plan.send(y1[0:2], 0), plan.send(x1[2:4], 2)]
        z2 = gather_z(plan, tie(unit2, z1))
    else:
        pieces1 = [regroup(gather_chips(plan, unit1), [2 * r for r in sizes1], SLOTS)]
        pieces2 = [regroup(gather_chips(plan, unit2), [2 * r for r in sizes2], SLOTS)]
        far2 = [swap_pair(p) for p in pieces2]
    lines = gather_chips(plan, line_unit).reshape(2 * plan.chips, line.shape[0])
    vectors = []
    at = 0
    for piece in smalls:
        size = piece.shape[0]
        vectors.append(lines[:, at : at + size].reshape(2 * plan.chips * size).astype(f32))
        at += size
    bias_q, bias_v, bias_o, gain1, shift1, bias_in, bias_d, gain2, shift2 = vectors
    bias_qkv = jnp.concatenate([half_of(bias_q, me), jnp.zeros((HALF,), f32), half_of(bias_v, me)])[None]
    zero = jnp.zeros((D,), f32)
    vecs = jnp.stack([bias_o, gain1, shift1, bias_d, gain2, shift2, zero, zero])

    ends = jnp.cumsum(lengths[0])
    unit_rows = 2 * half // UNITS
    seg_packed = jnp.sum((jnp.arange(UNITS)[:, None] * unit_rows >= ends[None, :]).astype(jnp.int32), axis=1)
    hit = block_order[0][:, None] == jnp.arange(UNITS)[None, :]
    seg_here = jnp.sum(jnp.where(hit, seg_packed[:, None], 0), axis=0)
    segs = jnp.where(plan.at(0) == me, seg_here, swap_pair(seg_here))
    segs = jnp.where(me == 0, segs, jnp.roll(segs, UNITS // 2))

    tok_got = swap_pair(tok)
    qkv, w_qkv = project(pull, tok, tok_got, bias_qkv, pieces1)
    back = relocate(tie(cotangent[0], pieces1[-1]))
    if plan.direct:
        qkv = tie(qkv, z2)
        x2, y2 = plan.send(z2, 0), plan.send(z2, 2)
        z2_far = swap_pair(z2)
    att = attention(segs, qkv, 0, 2, None)
    if plan.direct:
        y2_cut, x2_cut = lax.optimization_barrier((y2[0:2], x2[2:4], att[0]))[:2]
        d2a, d2b = plan.send(y2_cut, 0), plan.send(x2_cut, 2)
        x2_far, y2_far = swap_pair(x2), swap_pair(y2)
        att = lax.optimization_barrier(tuple(att) + (y2_cut, x2_cut))[:3]
    o_own, o_far, lse = attention(segs, qkv, 2, PAIRS - 2, att)
    o_got = swap_pair(o_far)
    if plan.direct:
        pieces2 = [z2, x2, y2, d2a, d2b]
        far2 = [z2_far, x2_far, y2_far, swap_pair(d2a), swap_pair(d2b)]
    (out_rows, act, ig, low, branch, attn_grad, resid1, d_own, d_far, sums) = middle(
        pull, tok, o_own, o_got, back, vecs, bias_in[None], pieces2, far2)
    d_got = swap_pair(d_far)
    sum_got = swap_pair(half_of(sums, 1 - me))
    small = half_of(sums, me) + sum_got
    keep, give = weight_grads(push, act, ig, low, branch, o_own, o_got, attn_grad)
    back_args = (o_own, o_far, d_own, d_got, lse)
    if plan.direct:
        got_g = swap_pair(give)
        g0 = attention_back(segs, tie(qkv, give), *back_args, 0, 1, None)
        output = relocate(tie(out_rows, give))

        def both_sums(lo, hi):
            return keep[lo:hi].astype(f32) + got_g[lo:hi].astype(f32)

        step1 = both_sums(12, 16).astype(bf16)
        sx, sy = lax.optimization_barrier((step1[:2], step1[2:], g0[0]))[:2]
        rx, ry = plan.send(sx, 0), plan.send(sy, 2)
        g0 = lax.optimization_barrier(tuple(g0) + (sx, sy))[:3]
        g1 = attention_back(segs, qkv, *back_args, 1, 1, g0)
        rx, ry = lax.optimization_barrier((rx, ry, g1[0]))[:2]
        send_x = jnp.concatenate([both_sums(4, 6), both_sums(6, 8) + ry.astype(f32)], axis=0).astype(bf16)
        send_y = jnp.concatenate([both_sums(8, 10) + rx.astype(f32), both_sums(10, 12)], axis=0).astype(bf16)
        px, py = plan.send(send_x, 0), plan.send(send_y, 2)
        g1 = lax.optimization_barrier(tuple(g1) + (send_x, send_y))[:3]
        dq, dk, dv = attention_back(segs, qkv, *back_args, 2, PAIRS - 2, g1)
        px, py = lax.optimization_barrier((px, py, dq))[:2]
        z_sum = both_sums(0, 4) + px.astype(f32) + py.astype(f32)
        z_low = z_sum[1:].astype(bf16)
        ffn = z_sum[0]
        for k in range(1, 4):
            ffn = ffn + plan.send(z_low[k - 1], 1, k).astype(f32)
        dq = tie(dq, z_low)
    else:
        output = relocate(out_rows)
        dq, dk, dv = attention_back(segs, qkv, *back_args, 0, PAIRS, None)
        summed = (keep.astype(f32) + swap_pair(give).astype(f32)).astype(bf16)
        scale = plan.chips // SLOTS
        units = regroup_back(summed, [ROWS] * (1 + ff_cols) + [ROWS * ff_cols], scale)
        ffn = reduce_chips(plan, units)
    tail = qkv_grads(push, small, tok, tok_got, dq, dk, dv)
    if plan.direct:
        rx, ry = plan.send(tail[12:14], 0), plan.send(tail[14:16], 2)
        far_back = swap_pair(input_back(w_qkv, dq, dk, dv, True, ()))
        send_x = jnp.concatenate([tail[4:6], (tail[6:8].astype(f32) + ry.astype(f32)).astype(bf16)], axis=0)
        send_y = jnp.concatenate([(tail[8:10].astype(f32) + rx.astype(f32)).astype(bf16), tail[10:12]], axis=0)
        px, py = plan.send(send_x, 0), plan.send(send_y, 2)
        packed = input_back(w_qkv, dq, dk, dv, False, (resid1, far_back))
        input_grad = relocate(packed)
        z_sum = tail[0:4].astype(f32) + px.astype(f32) + py.astype(f32)
        z_low = z_sum[1:].astype(bf16)
        qkv_sum = z_sum[0]
        for k in range(1, 4):
            qkv_sum = qkv_sum + plan.send(z_low[k - 1], 1, k).astype(f32)
    else:
        far_back = swap_pair(input_back(w_qkv, dq, dk, dv, True, ()))
        input_grad = relocate(input_back(w_qkv, dq, dk, dv, False, (resid1, far_back)))
        units = regroup_back(tail[:, : 3 * ROWS], [ROWS] * 3, scale)
        extra = jnp.broadcast_to(tail[0:1, 3 * ROWS :], (plan.chips, 16, HALF))
        qkv_sum = reduce_chips(plan, jnp.concatenate([units, extra], axis=1))

    small_sum = qkv_sum[6 * rows_dev :]
    sizes = sizes1 + sizes2
    total = jnp.concatenate([qkv_sum[: 6 * rows_dev], ffn], axis=0)
    mine, other = own_rows(me, total, sizes)
    got = swap_pair(jnp.concatenate([other, small_sum], axis=0))
    count = mine.shape[0]
    mine = jnp.concatenate([mine, small_sum], axis=0)
    full = jnp.concatenate([jnp.where(me == 0, mine, got), jnp.where(me == 0, got, mine)], axis=1)
    take = lambda at, size: full[at : at + size]
    out_qkv = jnp.concatenate([take(j * rows_dev, rows_dev) for j in range(3)], axis=1)
    out_out = take(3 * rows_dev, rows_dev)
    out_in = jnp.concatenate([take((4 + j) * rows_dev, rows_dev) for j in range(ff_cols)], axis=1)
    out_down = take((4 + ff_cols) * rows_dev, ff_dev)
    small_full = full[count:]
    device = plan.at(0)
    for a in range(1, len(plan.dims)):
        device = device * plan.dims[a] + plan.at(a)
    order = (14, 15, 0, 1, 2, 3, 3 + ff_cols, 4 + ff_cols, 5 + ff_cols)
    outs = []
    for piece, row in zip(smalls, order):
        size = piece.shape[0]
        span = small_full[row : row + size * 2 * plan.chips // D].reshape(-1)
        outs.append(lax.dynamic_slice_in_dim(span, device * size, size))
    s = outs
    return (output[None], input_grad[None], out_qkv, s[0], s[1], out_out, s[2], s[3], s[4], out_in, s[5], out_down, s[6], s[7], s[8])


def regroup_back(buf, sizes, scale):
    n, _, w = buf.shape
    parts = []
    at = 0
    for size in sizes:
        parts.append(buf[:, at : at + size].reshape(n * scale, size // scale, w))
        at += size
    return jnp.concatenate(parts, axis=1)


def solution(mesh):
    plan = Plan(mesh.shape["seq"], mesh.shape["fsdp"])
    inner_mesh = Mesh(mesh.devices.reshape(plan.dims), tuple(plan.names))
    groups = tuple(plan.names[1:])
    every = tuple(plan.names)
    rows = P(groups, "s", None)
    table = P(groups, None)
    mat = P(every, None)
    vec = P(every)
    placed = (rows, table, table, mat, vec, vec, mat, vec, vec, vec, mat, vec, mat, vec, vec, vec, rows)
    outs = (rows, rows, mat, vec, vec, mat, vec, vec, vec, mat, vec, mat, vec, vec, vec)

    def run(*args):
        return local(plan, *args)

    return jax.shard_map(run, mesh=inner_mesh, in_specs=placed, out_specs=outs, check_vma=False)
```

```python
import functools

import jax
import jax.numpy as jnp
import numpy as np
from jax import lax
from jax.sharding import Mesh, PartitionSpec as P
from jax.experimental import pallas as pl
from jax.experimental.pallas import tpu as pltpu

D = 768
HALF = D // 2
HD = 64
UNITS = 16
SLOTS = 16
ROWS = D // SLOTS
PAIRS = HALF // 128
LOG2E = 1.4426950408889634
LN2 = 0.6931471805599453
BIG = 1e30
TQ = 512
STEP = 512
TM = 256
norm_eps = 1e-12
bf16 = jnp.bfloat16
f32 = jnp.float32
NT = (((1,), (1,)), ((), ()))
NN = (((1,), (0,)), ((), ()))
TN = (((0,), (0,)), ((), ()))
VMEM_CAP = 58 << 20


def mxu(a, b, dims=NN):
    return lax.dot_general(a, b, dims, preferred_element_type=f32)


def shape(size, kind=bf16):
    return jax.ShapeDtypeStruct(size, kind)


def params(axes=1):
    return pltpu.CompilerParams(dimension_semantics=("arbitrary",) * axes, vmem_limit_bytes=VMEM_CAP)


def cost(flops, moved):
    return pl.CostEstimate(flops=int(flops), bytes_accessed=int(moved), transcendentals=0)


def tie(value, *others):
    return lax.optimization_barrier((value,) + others)[0]


def lanes(rows):
    return lax.broadcasted_iota(jnp.int32, (rows, 128), 1)


def seg_rows(segs_ref, base_block, rows):
    place = lax.broadcasted_iota(jnp.int32, (rows, 128), 0)
    out = jnp.zeros((rows, 128), jnp.int32)
    for b in range(rows // 128):
        out = jnp.where(place >= b * 128, segs_ref[base_block + b], out)
    return out


def split3(v):
    hi = v.astype(bf16).astype(f32)
    mid = (v - hi).astype(bf16).astype(f32)
    return hi, mid, v - hi - mid


def both_heads(pair_rows):
    lane = lanes(pair_rows.shape[0])
    zero = jnp.zeros_like(pair_rows)
    first = jnp.where(lane < HD, pair_rows, zero)
    return jnp.concatenate([first, jnp.where(lane < HD, zero, pair_rows)], axis=0)


def fill_keys(segs_ref, k_in, v_in, k_aug, v_aug):
    for at in range(0, k_in.shape[0], STEP):
        rows = slice(at, at + STEP)
        lane = lanes(STEP)
        hot = (lane == seg_rows(segs_ref, at // 128, STEP)) | ((lane >= 64) & (lane < 67))
        k_aug[rows, :128] = k_in[rows, :]
        k_aug[rows, 128:] = jnp.where(hot, 1.0, 0.0).astype(bf16)
        v_aug[rows, :128] = v_in[rows, :]
        v_aug[rows, 128:] = jnp.ones((STEP, 128), bf16)


def attend_body(segs_ref, q_in, k_in, v_in, *refs):
    o_own, o_far, lse_ref, k_aug, v_aug = refs[-5:]
    i = pl.program_id(1)
    n_half = pl.num_programs(1) // 2

    @pl.when(i == 0)
    def _():
        fill_keys(segs_ref, k_in, v_in, k_aug, v_aug)

    lane = lanes(TQ)
    seg = seg_rows(segs_ref, i * (TQ // 128), TQ)
    off = jnp.where((lane < 16) & (lane != seg), -BIG, 0.0).astype(bf16)
    q_aug = jnp.concatenate([both_heads(q_in[...]), jnp.concatenate([off, off], axis=0)], axis=1)
    top = None
    acc = None
    for at in range(0, k_aug.shape[0], STEP):
        s = mxu(q_aug, k_aug[at : at + STEP, :], NT)
        here = jnp.max(s, axis=1, keepdims=True)
        new_top = here if top is None else jnp.maximum(top, here)
        p = jnp.exp2(s - new_top).astype(bf16)
        add = mxu(p, v_aug[at : at + STEP, :])
        acc = add if acc is None else acc * jnp.exp2(top - new_top) + add
        top = new_top
    both = jnp.where(lane < HD, acc[:TQ, :128], acc[TQ:, :128])
    sums = jnp.where(lane < HD, acc[:TQ, 128:], acc[TQ:, 128:])
    tops = jnp.where(lane < HD, top[:TQ], top[TQ:])
    out = (both / sums).astype(bf16)
    lse_ref[...] = tops + jnp.log2(sums)

    @pl.when(i < n_half)
    def _():
        o_own[...] = out

    @pl.when(i >= n_half)
    def _():
        o_far[...] = out


def anyspec():
    return pl.BlockSpec(memory_space=pl.ANY)


def pair_specs(n_half, first):
    own = pl.BlockSpec((TQ, 128), lambda h, i, *_: (jnp.minimum(i, n_half - 1), first + h))
    far = pl.BlockSpec((TQ, 128), lambda h, i, *_: (jnp.maximum(i - n_half, 0), first + h))
    return own, far


def attention(segs, qkv, first, count, prev):
    total = qkv.shape[0]
    half = total // 2
    n_half = half // TQ
    own, far = pair_specs(n_half, first)
    row = pl.BlockSpec((TQ, 128), lambda h, i, *_: (i, first + h))
    whole = lambda part: pl.BlockSpec((total, 128), lambda h, i, *_: (0, part * PAIRS + first + h))
    prev = () if prev is None else tuple(prev)
    return pl.pallas_call(
        attend_body,
        grid_spec=pltpu.PrefetchScalarGridSpec(
            num_scalar_prefetch=1,
            grid=(count, 2 * n_half),
            in_specs=[row, whole(1), whole(2)] + [anyspec()] * len(prev),
            out_specs=[own, far, row],
            scratch_shapes=[pltpu.VMEM((total, 256), bf16), pltpu.VMEM((total, 256), bf16)],
        ),
        out_shape=[shape((half, HALF)), shape((half, HALF)), shape((total, HALF), f32)],
        input_output_aliases={4 + j: j for j in range(len(prev))},
        compiler_params=params(2),
        cost_estimate=cost(count * total * total * 2048, total * 128 * 2 * 8),
    )(segs, qkv, qkv, qkv, *prev)


def attend_back_body(segs_ref, q_in, k_in, v_in, o_own, o_far, d_own, d_far, lse_ref, *refs):
    dq_out, dk_out, dv_out, k_aug, v_aug, dk_acc, dv_acc = refs[-7:]
    i = pl.program_id(1)
    n = pl.num_programs(1)

    @pl.when(i == 0)
    def _():
        fill_keys(segs_ref, k_in, v_in, k_aug, v_aug)
        dk_acc[...] = jnp.zeros_like(dk_acc)
        dv_acc[...] = jnp.zeros_like(dv_acc)

    near = i < n // 2
    d_rows = jnp.where(near, d_own[...], d_far[...])
    o_rows = jnp.where(near, o_own[...], o_far[...])
    lane = lanes(TQ)
    seg = seg_rows(segs_ref, i * (TQ // 128), TQ)
    off = jnp.where((lane < 16) & (lane != seg), -BIG, 0.0)
    prod = d_rows.astype(f32) * o_rows.astype(f32)
    q_side, d_side = [], []
    for head in range(2):
        mine = (lane < HD) if head == 0 else (lane >= HD)
        dot_row = jnp.sum(jnp.where(mine, prod, 0.0), axis=1, keepdims=True)
        lse = jnp.broadcast_to(lse_ref[:, head * HD : head * HD + 1], (TQ, 128))
        for side, value, rest in ((q_side, -lse, off), (d_side, -jnp.broadcast_to(dot_row, (TQ, 128)), 0.0)):
            h, m, l = split3(value)
            cols = jnp.where(lane == 64, h, jnp.where(lane == 65, m, jnp.where(lane == 66, l, rest)))
            side.append(cols.astype(bf16))
    q2 = both_heads(q_in[...])
    d2 = both_heads(d_rows)
    q_aug = jnp.concatenate([q2, jnp.concatenate(q_side, axis=0)], axis=1)
    d_aug = jnp.concatenate([d2, jnp.concatenate(d_side, axis=0)], axis=1)
    dq = None
    for at in range(0, k_aug.shape[0], STEP):
        rows = slice(at, at + STEP)
        keys = k_aug[rows, :]
        p = jnp.exp2(mxu(q_aug, keys, NT))
        ds = (p * mxu(d_aug, v_aug[rows, :], NT)).astype(bf16)
        dv_acc[rows, :] += mxu(p.astype(bf16), d2, TN)
        dk_acc[rows, :] += mxu(ds, q2, TN)
        add = mxu(ds, keys[:, :128])
        dq = add if dq is None else dq + add
    dq_out[...] = (jnp.where(lane < HD, dq[:TQ], dq[TQ:]) * (HD ** -0.5)).astype(bf16)

    @pl.when(i == n - 1)
    def _():
        dk_out[...] = (dk_acc[...] * LN2).astype(bf16)
        dv_out[...] = dv_acc[...].astype(bf16)


def attention_back(segs, qkv, o_own, o_far, d_own, d_far, lse, first, count, prev):
    total = qkv.shape[0]
    half = total // 2
    n_half = half // TQ
    own, far = pair_specs(n_half, first)
    row = pl.BlockSpec((TQ, 128), lambda h, i, *_: (i, first + h))
    whole = lambda part: pl.BlockSpec((total, 128), lambda h, i, *_: (0, part * PAIRS + first + h))
    prev = () if prev is None else tuple(prev)
    return pl.pallas_call(
        attend_back_body,
        grid_spec=pltpu.PrefetchScalarGridSpec(
            num_scalar_prefetch=1,
            grid=(count, 2 * n_half),
            in_specs=[row, whole(1), whole(2), own, far, own, far, row] + [anyspec()] * len(prev),
            out_specs=[row, whole(0), whole(0)],
            scratch_shapes=[
                pltpu.VMEM((total, 256), bf16),
                pltpu.VMEM((total, 256), bf16),
                pltpu.VMEM((total, 128), f32),
                pltpu.VMEM((total, 128), f32),
            ],
        ),
        out_shape=[shape((total, HALF))] * 3,
        input_output_aliases={9 + j: j for j in range(len(prev))},
        compiler_params=params(2),
        cost_estimate=cost(count * total * total * 5120, total * 128 * 2 * 12),
    )(segs, qkv, qkv, qkv, o_own, o_far, d_own, d_far, lse, *prev)


def pack_body(info, qkv, w_out, w_in, w_down, small, mine, give):
    me = info[0]
    for half_at, dst in ((me, mine), (1 - me, give)):
        slab = 0

        def cols(base):
            return pl.ds(pl.multiple_of(base + half_at * HALF, 128), HALF)

        for j in range(3):
            dst[slab] = qkv[:, cols(j * D)]
            slab += 1
        dst[slab] = jnp.zeros(dst.shape[1:], bf16)
        dst[slab, :, 0:128] = small[...]
        dst[slab + 1] = w_out[:, cols(0)]
        slab += 2
        for j in range(w_in.shape[1] // D):
            dst[slab] = w_in[:, cols(j * D)]
            slab += 1
        for j in range(w_down.shape[0]):
            dst[slab] = w_down[j, :, cols(0)]
            slab += 1


def combine_body(info, mine, got, unit1, unit2):
    me = info[0]
    n = unit2.shape[0] // 2
    wide = n // 2
    unit1[6] = jnp.zeros(unit1.shape[1:], bf16)
    for at, src in ((me, mine), (1 - me, got)):
        for j in range(3):
            unit1[2 * j + at] = src[j]
        for j in range(wide + 1):
            unit2[2 * j + at] = src[4 + j]
        for j in range(wide):
            unit2[2 * (wide + 1) + at * wide + j] = src[5 + wide + j]
    unit1[6, :, 0:128] = mine[3, :, 0:128]
    unit1[6, :, 128:256] = got[3, :, 0:128]


def whole_call(body, ins, outs, *args):
    return pl.pallas_call(
        body,
        grid_spec=pltpu.PrefetchScalarGridSpec(
            num_scalar_prefetch=1,
            grid=(),
            in_specs=[pl.BlockSpec(memory_space=pltpu.VMEM)] * ins,
            out_specs=[pl.BlockSpec(memory_space=pltpu.VMEM)] * len(outs),
        ),
        out_shape=[shape(o) for o in outs],
        cost_estimate=cost(0, 2 << 20),
    )(*args)


def each_slot(pieces):
    at = 0
    for ref in pieces:
        for slot in range(ref.shape[0]):
            yield at, ref, slot
            at += 1


def wait_for(dst, sem):
    pltpu.make_async_copy(dst, dst, sem).wait()


def proj_body(info, t_own, t_got, bias, *refs):
    pieces, (out, w_out, w, sem) = refs[:-4], refs[-4:]
    i = pl.program_id(0)

    @pl.when(i == 0)
    def _():
        for at, ref, slot in each_slot(pieces):
            rows = pl.ds(pl.multiple_of(info[1 + at] * ROWS, ROWS), ROWS)
            for j in range(3):
                src = ref.at[slot, j * ROWS : (j + 1) * ROWS, :]
                pltpu.make_async_copy(src, w.at[rows, j * HALF : (j + 1) * HALF], sem).start()
        wait_for(w, sem)

    tile = jnp.where(i < pl.num_programs(0) // 2, t_own[...], t_got[...])
    for j in range(3):
        cols = slice(j * HALF, (j + 1) * HALF)
        part = mxu(tile, w[:, cols]) + bias[0:1, cols]
        if j == 0:
            part = part * (LOG2E * HD ** -0.5)
        out[:, cols] = part.astype(bf16)
    w_out[...] = w[...]


def project(info, t_own, t_got, bias, pieces):
    half = t_own.shape[0]
    tile = 512
    n_half = half // tile
    own = pl.BlockSpec((tile, D), lambda i, *_: (jnp.minimum(i, n_half - 1), 0))
    got = pl.BlockSpec((tile, D), lambda i, *_: (jnp.maximum(i - n_half, 0), 0))
    return pl.pallas_call(
        proj_body,
        grid_spec=pltpu.PrefetchScalarGridSpec(
            num_scalar_prefetch=1,
            grid=(2 * n_half,),
            in_specs=[own, got, pl.BlockSpec((1, 3 * HALF), lambda i, *_: (0, 0))] + [anyspec()] * len(pieces),
            out_specs=[
                pl.BlockSpec((tile, 3 * HALF), lambda i, *_: (i, 0)),
                pl.BlockSpec((D, 3 * HALF), lambda i, *_: (0, 0)),
            ],
            scratch_shapes=[pltpu.VMEM((D, 3 * HALF), bf16), pltpu.SemaphoreType.DMA],
        ),
        out_shape=[shape((2 * half, 3 * HALF)), shape((D, 3 * HALF))],
        compiler_params=params(),
        cost_estimate=cost(half * D * D * 6, half * D * 12),
    )(info, t_own, t_got, bias, *pieces)


def norm_stats(rows):
    mean = jnp.mean(rows, axis=-1, keepdims=True)
    centered = rows - mean
    var = jnp.mean(centered * centered, axis=-1, keepdims=True)
    rstd = lax.rsqrt(var + norm_eps)
    return centered * rstd, rstd


def norm_back(grad, unit, rstd, gain):
    eg = grad * gain
    mean_eg = jnp.mean(eg, axis=-1, keepdims=True)
    mean_en = jnp.mean(eg * unit, axis=-1, keepdims=True)
    return (eg - mean_eg - unit * mean_en) * rstd


def mid_body(info, tok, o_own, o_got, back, vecs, bias_in, *refs):
    n_out = 10
    outs, scratch = refs[-n_out - 5 : -5], refs[-5:]
    pieces = refs[: -n_out - 5]
    own_pieces, far_pieces = pieces[: len(pieces) // 2], pieces[len(pieces) // 2 :]
    out_rows, act_out, ig_out, low_out, branch_out, attn_out, resid_out, d_own, d_far, sums = outs
    w_out, w_in, w_down, slope, sems = scratch
    ff_cols = w_in.shape[1] // D
    me = info[0]

    @pl.when(pl.program_id(0) == 0)
    def _():
        for kind in range(3):
            for here, part in ((me, own_pieces), (1 - me, far_pieces)):
                for at, ref, slot in each_slot(part):
                    chip = info[1 + at]
                    lane0 = pl.multiple_of(here * HALF, HALF)
                    rows = pl.ds(pl.multiple_of(chip * ROWS, ROWS), ROWS)
                    if kind == 0:
                        pltpu.make_async_copy(ref.at[slot, 0:ROWS, :], w_out.at[rows, pl.ds(lane0, HALF)], sems.at[0]).start()
                    elif kind == 1:
                        for j in range(ff_cols):
                            src = ref.at[slot, (1 + j) * ROWS : (2 + j) * ROWS, :]
                            dst = w_in.at[rows, pl.ds(pl.multiple_of(lane0 + j * D, HALF), HALF)]
                            pltpu.make_async_copy(src, dst, sems.at[1]).start()
                    else:
                        size = ROWS * ff_cols
                        src = ref.at[slot, (1 + ff_cols) * ROWS : (1 + 2 * ff_cols) * ROWS, :]
                        dst = w_down.at[pl.ds(pl.multiple_of(chip * size, size), size), pl.ds(lane0, HALF)]
                        pltpu.make_async_copy(src, dst, sems.at[2]).start()
        sums[...] = jnp.zeros_like(sums)
        wait_for(w_out, sems.at[0])

    bias_o, gain1, shift1 = vecs[0:1, :], vecs[1:2, :], vecs[2:3, :]
    bias_d, gain2, shift2 = vecs[3:4, :], vecs[4:5, :], vecs[5:6, :]
    mine = w_out[pl.ds(pl.multiple_of(me * HALF, HALF), HALF), :]
    other = w_out[pl.ds(pl.multiple_of((1 - me) * HALF, HALF), HALF), :]
    resid = tok[...].astype(f32) + mxu(o_own[...], mine) + mxu(o_got[...], other) + bias_o
    unit1, rstd1 = norm_stats(resid)
    hidden = unit1 * gain1 + shift1
    low = hidden.astype(bf16)
    low_out[...] = low

    @pl.when(pl.program_id(0) == 0)
    def _():
        wait_for(w_in, sems.at[1])
        wait_for(w_down, sems.at[2])

    branch = bias_d
    for j in range(ff_cols):
        cols = slice(j * D, (j + 1) * D)
        inner = mxu(low, w_in[:, cols]) + bias_in[:, cols]
        phi = 0.5 + 0.5 * lax.erf(inner * (0.5 ** 0.5))
        act = (inner * phi).astype(bf16)
        act_out[:, cols] = act
        slope[:, cols] = phi + inner * (jnp.exp2(inner * inner * (-0.5 * LOG2E)) * 0.3989422804014327)
        branch = branch + mxu(act, w_down[cols, :])
    unit2, rstd2 = norm_stats(hidden + branch)
    out_rows[...] = (unit2 * gain2 + shift2).astype(bf16)
    grad = back[...].astype(f32)
    resid2 = norm_back(grad, unit2, rstd2, gain2)
    low_branch = resid2.astype(bf16)
    branch_out[...] = low_branch
    hidden_grad = resid2
    for j in range(ff_cols):
        cols = slice(j * D, (j + 1) * D)
        ig = (mxu(low_branch, w_down[cols, :], NT) * slope[:, cols]).astype(bf16)
        ig_out[:, cols] = ig
        hidden_grad = hidden_grad + mxu(ig, w_in[:, cols], NT)
        sums[3 + j : 4 + j, :] += jnp.sum(ig.astype(f32), axis=0, keepdims=True)
    resid1 = norm_back(hidden_grad, unit1, rstd1, gain1)
    resid_out[...] = resid1
    attn_grad = resid1.astype(bf16)
    attn_out[...] = attn_grad
    d_own[...] = mxu(attn_grad, mine, NT).astype(bf16)
    d_far[...] = mxu(attn_grad, other, NT).astype(bf16)
    rows = (
        (0, attn_grad.astype(f32)),
        (1, hidden_grad * unit1),
        (2, hidden_grad),
        (3 + ff_cols, low_branch.astype(f32)),
        (4 + ff_cols, grad * unit2),
        (5 + ff_cols, grad),
    )
    for at, value in rows:
        sums[at : at + 1, :] += jnp.sum(value, axis=0, keepdims=True)


def middle(info, tok, o_own, o_got, back, vecs, bias_in, own_pieces, far_pieces):
    half = tok.shape[0]
    ff = bias_in.shape[1]
    wide = pl.BlockSpec((TM, D), lambda i, *_: (i, 0))
    thin = pl.BlockSpec((TM, HALF), lambda i, *_: (i, 0))
    full = pl.BlockSpec((TM, ff), lambda i, *_: (i, 0))
    fixed = lambda rows, cols: pl.BlockSpec((rows, cols), lambda i, *_: (0, 0))
    pieces = tuple(own_pieces) + tuple(far_pieces)
    return pl.pallas_call(
        mid_body,
        grid_spec=pltpu.PrefetchScalarGridSpec(
            num_scalar_prefetch=1,
            grid=(half // TM,),
            in_specs=[wide, thin, thin, wide, fixed(8, D), fixed(1, ff)] + [anyspec()] * len(pieces),
            out_specs=[wide, full, full, wide, wide, wide, wide, thin, thin, fixed(16, D)],
            scratch_shapes=[
                pltpu.VMEM((D, D), bf16),
                pltpu.VMEM((D, ff), bf16),
                pltpu.VMEM((ff, D), bf16),
                pltpu.VMEM((TM, ff), f32),
                pltpu.SemaphoreType.DMA((3,)),
            ],
        ),
        out_shape=[
            shape((half, D)),
            shape((half, ff)),
            shape((half, ff)),
            shape((half, D)),
            shape((half, D)),
            shape((half, D)),
            shape((half, D), f32),
            shape((half, HALF)),
            shape((half, HALF)),
            shape((16, D), f32),
        ],
        compiler_params=params(),
        cost_estimate=cost(half * D * (D + 2 * ff) * 4, half * D * 40),
    )(info, tok, o_own, o_got, back, vecs, bias_in, *pieces)


def wgrad_body(own, info, act, ig, low, branch, o_own, o_got, attn_grad, dst, res_in, res_down, res_out, sems):
    j = pl.program_id(0)
    n = pl.num_programs(0)
    me = info[0]
    par = lax.rem(j, 2)
    down_rows = ROWS * n
    per_step = SLOTS // n
    half_at = me if own else 1 - me
    lane = pl.ds(pl.multiple_of(half_at * HALF, HALF), HALF)

    @pl.when(j == 0)
    def _():
        grad = attn_grad[:, lane]
        for here, rows in ((me, o_own), (1 - me, o_got)):
            spot = pl.ds(pl.multiple_of(here * HALF, HALF), HALF)
            res_out[spot, :] = mxu(rows[...], grad, TN).astype(bf16)
        for chip in range(SLOTS):
            src = res_out.at[chip * ROWS : (chip + 1) * ROWS, :]
            pltpu.make_async_copy(src, dst.at[info[1 + chip], 0:ROWS, :], sems.at[2]).start()

    res_in[par] = mxu(low[...], ig[:, lane], TN).astype(bf16)
    for chip in range(SLOTS):
        src = res_in.at[par, chip * ROWS : (chip + 1) * ROWS, :]
        spot = pl.ds(pl.multiple_of((1 + j) * ROWS, ROWS), ROWS)
        pltpu.make_async_copy(src, dst.at[info[1 + chip], spot, :], sems.at[par]).start()
    res_down[par] = mxu(act[...], branch[:, lane], TN).astype(bf16)
    for q in range(per_step):
        src = res_down.at[par, q * down_rows : (q + 1) * down_rows, :]
        slot = info[1 + j * per_step + q]
        pltpu.make_async_copy(src, dst.at[slot, ROWS * (1 + n) : ROWS * (1 + 2 * n), :], sems.at[par]).start()

    def settle(which):
        wait_for(res_in.at[which], sems.at[which])
        wait_for(res_down.at[which], sems.at[which])

    @pl.when(j > 0)
    def _():
        settle(1 - par)

    @pl.when(j == n - 1)
    def _():
        settle(par)
        wait_for(res_out, sems.at[2])


def weight_grads(own, info, act, ig, low, branch, o_own, o_got, attn_grad):
    half, ff = act.shape
    n = ff // D
    strip = pl.BlockSpec((half, D), lambda j, *_: (0, j))
    fixed = lambda cols: pl.BlockSpec((half, cols), lambda j, *_: (0, 0))
    return pl.pallas_call(
        functools.partial(wgrad_body, own),
        grid_spec=pltpu.PrefetchScalarGridSpec(
            num_scalar_prefetch=1,
            grid=(n,),
            in_specs=[strip, strip, fixed(D), fixed(D), fixed(HALF), fixed(HALF), fixed(D)],
            out_specs=anyspec(),
            scratch_shapes=[
                pltpu.VMEM((2, D, HALF), bf16),
                pltpu.VMEM((2, D, HALF), bf16),
                pltpu.VMEM((D, HALF), bf16),
                pltpu.SemaphoreType.DMA((3,)),
            ],
        ),
        out_shape=shape((SLOTS, ROWS * (1 + 2 * n), HALF)),
        compiler_params=params(),
        cost_estimate=cost(half * D * (D + 2 * ff), half * ff * 8),
    )(info, act, ig, low, branch, o_own, o_got, attn_grad)


def qkv_grad_body(info, small, t_own, t_got, dq, dk, dv, out, t_all, d_all, res, res_small, sems):
    half = t_own.shape[0]
    pltpu.make_async_copy(t_own, t_all.at[0:half, :], sems.at[0]).start()
    pltpu.make_async_copy(t_got, t_all.at[half:, :], sems.at[0]).start()
    for j, src in enumerate((dq, dk, dv)):
        pltpu.make_async_copy(src, d_all.at[j], sems.at[1 + j]).start()
    wait_for(t_all, sems.at[0])
    res_small[...] = small[...].astype(bf16)
    row = lax.broadcasted_iota(jnp.int32, (16, HALF), 0)
    for j in range(3):
        wait_for(d_all.at[j], sems.at[1 + j])
        grads = d_all[j]
        res[j] = mxu(t_all[...], grads, TN).astype(bf16)
        for chip in range(SLOTS):
            src = res.at[j, chip * ROWS : (chip + 1) * ROWS, :]
            pltpu.make_async_copy(src, out.at[info[1 + chip], j * ROWS : (j + 1) * ROWS, :], sems.at[4]).start()
        if j != 1:
            total = jnp.sum(grads.astype(f32), axis=0, keepdims=True)
            place = 14 if j == 0 else 15
            res_small[...] = jnp.where(row == place, total, res_small[...].astype(f32)).astype(bf16)
    for slot in range(SLOTS):
        pltpu.make_async_copy(res_small, out.at[slot, 3 * ROWS : 3 * ROWS + 16, :], sems.at[5]).start()
    wait_for(res, sems.at[4])
    for slot in range(SLOTS):
        pltpu.make_async_copy(res_small, out.at[slot, 3 * ROWS : 3 * ROWS + 16, :], sems.at[5]).wait()


def qkv_grads(info, small, t_own, t_got, dq, dk, dv):
    total = dq.shape[0]
    return pl.pallas_call(
        qkv_grad_body,
        grid_spec=pltpu.PrefetchScalarGridSpec(
            num_scalar_prefetch=1,
            grid=(),
            in_specs=[pl.BlockSpec(memory_space=pltpu.VMEM)] + [anyspec()] * 5,
            out_specs=anyspec(),
            scratch_shapes=[
                pltpu.VMEM((total, D), bf16),
                pltpu.VMEM((3, total, HALF), bf16),
                pltpu.VMEM((3, D, HALF), bf16),
                pltpu.VMEM((16, HALF), bf16),
                pltpu.SemaphoreType.DMA((6,)),
            ],
        ),
        out_shape=shape((SLOTS, 3 * ROWS + 16, HALF)),
        compiler_params=pltpu.CompilerParams(vmem_limit_bytes=VMEM_CAP),
        cost_estimate=cost(total * D * HALF * 6, total * D * 5),
    )(info, small, t_own, t_got, dq, dk, dv)


def input_back_body(*refs):
    w = refs[0]
    dq, dk, dv = refs[1:4]
    out = refs[-1]
    total = None
    for j, part in enumerate((dq, dk, dv)):
        add = mxu(part[...], w[:, j * HALF : (j + 1) * HALF], NT)
        total = add if total is None else total + add
    for extra in refs[4:-1]:
        total = total + extra[...].astype(f32)
    out[...] = total.astype(bf16)


def input_back(w, dq, dk, dv, far, extras):
    half = dq.shape[0] // 2
    tile = 512
    base = half // tile if far else 0
    part = pl.BlockSpec((tile, HALF), lambda i: (base + i, 0))
    row = pl.BlockSpec((tile, D), lambda i: (i, 0))
    return pl.pallas_call(
        input_back_body,
        grid=(half // tile,),
        in_specs=[pl.BlockSpec((D, 3 * HALF), lambda i: (0, 0)), part, part, part] + [row] * len(extras),
        out_specs=row,
        out_shape=shape((half, D)),
        compiler_params=params(),
        cost_estimate=cost(half * D * HALF * 6, half * D * 8),
    )(w, dq, dk, dv, *extras)


def shift(n, k):
    return [(i, (i + k) % n) for i in range(n)]


class Plan:
    def __init__(self, seq, fsdp):
        rest = fsdp // 2
        dims = []
        while rest > 1:
            want = 4 if len(dims) % 2 == 0 and rest % 4 == 0 else 2
            dims.append(want)
            rest //= want
        self.dims = [seq] + dims + [2]
        self.names = ["s"] + ["r%d" % i for i in range(len(dims))] + ["c"]
        self.chips = seq * fsdp // 2
        self.direct = self.dims == [2, 4, 2, 2]
        self.stages = ([1] if dims else []) + [0] + list(range(2, len(dims) + 1))

    def at(self, a):
        return lax.axis_index(self.names[a])

    def chip_table(self, sign):
        if not self.direct:
            return jnp.arange(SLOTS, dtype=jnp.int32)
        spots = []
        for dx, dy in ((0, 0), (1, 0), (0, 1), (1, 1)):
            spots += [(dx, dy, z) for z in range(4)]
        dx, dy, dz = (jnp.asarray(v, jnp.int32) for v in zip(*spots))
        return ((self.at(0) + sign * dx) % 2) * 8 + ((self.at(1) + sign * dz) % 4) * 2 + (self.at(2) + sign * dy) % 2

    def slot_table(self, sign):
        table = self.chip_table(sign)
        hit = table[:, None] == jnp.arange(SLOTS, dtype=jnp.int32)[None, :]
        return jnp.sum(jnp.where(hit, jnp.arange(SLOTS, dtype=jnp.int32)[:, None], 0), axis=0)

    def places(self, sign):
        grid = np.indices(self.dims[:-1]).reshape(len(self.dims) - 1, -1)
        flat = jnp.zeros((self.chips,), jnp.int32)
        if sign < 0:
            for a in reversed(self.stages):
                n = self.dims[a]
                flat = flat * n + (self.at(a) - jnp.asarray(grid[a], jnp.int32)) % n
            return flat
        sizes = [self.dims[a] for a in reversed(self.stages)]
        offs = np.indices(sizes).reshape(len(sizes), -1)
        by_axis = {a: offs[j] for j, a in enumerate(reversed(self.stages))}
        for a in range(len(self.dims) - 1):
            n = self.dims[a]
            flat = flat * n + (self.at(a) + jnp.asarray(by_axis[a], jnp.int32)) % n
        return flat

    def send(self, x, a, k=1):
        return lax.ppermute(x, self.names[a], shift(self.dims[a], k))


def gather_chips(plan, unit):
    buf = unit[None]
    for a in plan.stages:
        n = plan.dims[a]
        if n > 1:
            buf = jnp.concatenate([buf] + [plan.send(buf, a, k) for k in range(1, n)], axis=0)
    return jnp.take(buf, plan.places(-1), axis=0, mode="clip")


def reduce_chips(plan, grads):
    buf = jnp.take(grads, plan.places(1), axis=0, mode="clip")
    for a in reversed(plan.stages):
        n = plan.dims[a]
        size = buf.shape[0] // n
        keep = buf[:size].astype(f32)
        for k in range(1, n):
            keep = keep + plan.send(buf[k * size : (k + 1) * size].astype(bf16), a, k).astype(f32)
        buf = keep if a == plan.stages[0] else keep.astype(bf16)
    return buf[0]


def regroup(buf, sizes, count):
    n, _, w = buf.shape
    parts = []
    at = 0
    for size in sizes:
        parts.append(buf[:, at : at + size].reshape(count, n * size // count, w))
        at += size
    return jnp.concatenate(parts, axis=1)


def gather_z(plan, unit):
    return jnp.concatenate([unit[None]] + [plan.send(unit, 1, k)[None] for k in range(1, 4)], axis=0)


def swap_pair(x):
    return lax.ppermute(x, "c", [(0, 1), (1, 0)])


def cross(x):
    return lax.ppermute(x, ("s", "c"), [(1, 2), (2, 1)])


def together(*values):
    return lax.optimization_barrier(values)


def half_of(x, at):
    return lax.dynamic_slice_in_dim(x, at * HALF, HALF, axis=x.ndim - 1)


def chip_units(me, mine, got, sizes):
    low = jnp.where(me == 0, mine, got)
    high = jnp.where(me == 0, got, mine)
    parts = []
    at = 0
    for size in sizes:
        parts += [low[at : at + size], high[at : at + size]]
        at += size
    return jnp.concatenate(parts, axis=0)


def own_rows(me, total, sizes):
    first, second = [], []
    at = 0
    for size in sizes:
        first.append(total[at : at + size])
        second.append(total[at + size : at + 2 * size])
        at += 2 * size
    first = jnp.concatenate(first, axis=0)
    second = jnp.concatenate(second, axis=0)
    return jnp.where(me == 0, first, second), jnp.where(me == 0, second, first)


def local(plan, tokens, lengths, block_order, qkv_weight, query_bias, value_bias, out_weight, out_bias,
          norm1_gain, norm1_shift, in_weight, in_bias, down_weight, down_bias, norm2_gain, norm2_shift, cotangent):
    half = tokens.shape[1]
    me = plan.at(len(plan.dims) - 1)
    stays = plan.at(0) == me
    rows_dev = qkv_weight.shape[0]
    ff_dev = down_weight.shape[0]
    ff_cols = in_weight.shape[1] // D
    me32 = me.astype(jnp.int32)
    pull = jnp.concatenate([me32[None], plan.chip_table(-1)])
    push = jnp.concatenate([me32[None], plan.slot_table(1)])
    sizes1 = [rows_dev] * 3
    sizes2 = [rows_dev] * (1 + ff_cols) + [ff_dev]
    smalls = (query_bias, value_bias, out_bias, norm1_gain, norm1_shift, in_bias, down_bias, norm2_gain, norm2_shift)
    unit_rows = 2 * half // UNITS

    def settle_rows(x, got):
        return jnp.where(stays, x, got)

    tok = settle_rows(tokens[0], cross(tokens[0]))
    if plan.direct:
        counts = [(lengths[0] // unit_rows).astype(bf16), block_order[0].astype(bf16)]
        lines = [jnp.pad(v, (0, 128 - v.shape[0])) for v in smalls + tuple(counts)]
        lines += [jnp.zeros((128,), bf16)] * (rows_dev - len(lines))
        slabs = 5 + 2 * ff_cols
        slab = (slabs, rows_dev, HALF)
        mine, give = whole_call(pack_body, 5, (slab, slab), pull, qkv_weight, out_weight, in_weight,
                                down_weight.reshape(ff_cols, rows_dev, D), jnp.stack(lines))
        got = swap_pair(give)
        unit1, unit2 = whole_call(combine_body, 2, ((7, rows_dev, HALF), (2 + 4 * ff_cols, rows_dev, HALF)), pull, mine, got)
        unit1 = unit1.reshape(7 * rows_dev, HALF)
        unit2 = unit2.reshape(-1, HALF)
        other = got[3, len(smalls) : len(smalls) + 2, :UNITS].astype(jnp.int32)
        counts_here = jnp.where(stays, lengths[0] // unit_rows, other[0])
        order_here = jnp.where(stays, block_order[0], other[1])

        z1 = gather_z(plan, unit1)
        unit2, z1 = together(unit2, z1)
        x1, y1 = plan.send(z1, 0), plan.send(z1, 2)
        z2_parts = [unit2] + [plan.send(unit2, 1, k) for k in range(1, 4)]
        cot, x1, y1 = together(cotangent[0], x1, y1)
        d1a, d1b = plan.send(y1[0:2], 0), plan.send(x1[2:4], 2)
        cot_got = cross(cot)
        pieces1 = [z1, x1, y1, d1a, d1b]
        tail_rows = [p[:, 6 * rows_dev : 6 * rows_dev + 16, 0:256] for p in pieces1]
        table = jnp.take(jnp.concatenate(tail_rows, axis=0), plan.slot_table(-1), axis=0, mode="clip")
        table = table.reshape(plan.chips, 16, 2, 128)
        table = jnp.where(me == 0, table, table[:, :, ::-1])
        vectors = [table[:, i, :, : v.shape[0]].reshape(-1).astype(f32) for i, v in enumerate(smalls)]
    else:
        first = jnp.concatenate([qkv_weight[:, j * D : (j + 1) * D] for j in range(3)], axis=0)
        second = jnp.concatenate([out_weight] + [in_weight[:, j * D : (j + 1) * D] for j in range(ff_cols)] + [down_weight], axis=0)
        line = jnp.concatenate(smalls)
        both = jnp.concatenate([first, second], axis=0)
        got = swap_pair(half_of(both, 1 - me))
        mine = half_of(both, me)
        cut = 3 * rows_dev
        unit1 = chip_units(me, mine[:cut], got[:cut], sizes1)
        unit2 = chip_units(me, mine[cut:], got[cut:], sizes2)
        line_got = swap_pair(line)
        line_unit = jnp.stack([jnp.where(me == 0, line, line_got), jnp.where(me == 0, line_got, line)])
        pieces1 = [regroup(gather_chips(plan, unit1), [2 * r for r in sizes1], SLOTS)]
        pieces2 = [regroup(gather_chips(plan, unit2), [2 * r for r in sizes2], SLOTS)]
        far2 = [swap_pair(p) for p in pieces2]
        lines = gather_chips(plan, line_unit).reshape(2 * plan.chips, line.shape[0])
        vectors = []
        at = 0
        for piece in smalls:
            size = piece.shape[0]
            vectors.append(lines[:, at : at + size].reshape(2 * plan.chips * size).astype(f32))
            at += size
        counts_here = jnp.where(stays, lengths[0], swap_pair(lengths[0])) // unit_rows
        order_here = jnp.where(stays, block_order[0], swap_pair(block_order[0]))
        cot_got = cross(cotangent[0])
    bias_q, bias_v, bias_o, gain1, shift1, bias_in, bias_d, gain2, shift2 = vectors
    bias_qkv = jnp.concatenate([half_of(bias_q, me), jnp.zeros((HALF,), f32), half_of(bias_v, me)])[None]
    zero = jnp.zeros((D,), f32)
    vecs = jnp.stack([bias_o, gain1, shift1, bias_d, gain2, shift2, zero, zero])

    spot = jnp.arange(UNITS)
    ends = jnp.sum(jnp.where(spot[None, :] <= spot[:, None], counts_here[None, :], 0), axis=1)
    seg_packed = jnp.sum((spot[:, None] >= ends[None, :]).astype(jnp.int32), axis=1)
    hit = order_here[:, None] == spot[None, :]
    segs = jnp.sum(jnp.where(hit, seg_packed[:, None], 0), axis=0)
    segs = jnp.where(me == 0, segs, jnp.roll(segs, UNITS // 2))

    tok_got = swap_pair(tok)
    qkv, w_qkv = project(pull, tok, tok_got, bias_qkv, pieces1)
    if plan.direct:
        *z2_parts, qkv = together(*z2_parts, qkv)
        z2 = jnp.stack(z2_parts)
        x2, y2 = plan.send(z2, 0), plan.send(z2, 2)
        z2_far = swap_pair(z2)
        att = attention(segs, qkv, 0, 2, None)
        x2, y2, cot_got, *att = together(x2, y2, cot_got, *att)
        d2a, d2b = plan.send(y2[0:2], 0), plan.send(x2[2:4], 2)
        x2_far, y2_far = swap_pair(x2), swap_pair(y2)
    else:
        att = attention(segs, qkv, 0, 2, None)
    back = settle_rows(cotangent[0], cot_got)
    o_own, o_far, lse = attention(segs, qkv, 2, PAIRS - 2, att)
    o_got = swap_pair(o_far)
    if plan.direct:
        pieces2 = [z2, x2, y2, d2a, d2b]
        far2 = [z2_far, x2_far, y2_far, swap_pair(d2a), swap_pair(d2b)]
    (out_rows, act, ig, low, branch, attn_grad, resid1, d_own, d_far, sums) = middle(
        pull, tok, o_own, o_got, back, vecs, bias_in[None], pieces2, far2)
    d_got = swap_pair(d_far)
    out_got = cross(out_rows)
    sum_got = swap_pair(half_of(sums, 1 - me))
    grad_args = (low, branch, o_own, o_got)
    give = weight_grads(False, push, act, ig, *grad_args, attn_grad)
    give, attn_grad = together(give, attn_grad)
    got_g = swap_pair(give)
    keep = weight_grads(True, push, act, ig, *grad_args, attn_grad)
    back_args = (o_own, o_far, d_own, d_got, lse)
    if plan.direct:

        def both_sums(lo, hi):
            return keep[lo:hi].astype(f32) + got_g[lo:hi].astype(f32)

        step1 = both_sums(12, 16).astype(bf16)
        sx, sy, qkv_back, out_got = together(step1[:2], step1[2:], qkv, out_got)
        rx, ry = plan.send(sx, 0), plan.send(sy, 2)
        g = attention_back(segs, qkv_back, *back_args, 0, 1, None)
        rx, ry, sum_got, *g = together(rx, ry, sum_got, *g)
        send_x = jnp.concatenate([both_sums(4, 6), both_sums(6, 8) + ry.astype(f32)], axis=0).astype(bf16)
        send_y = jnp.concatenate([both_sums(8, 10) + rx.astype(f32), both_sums(10, 12)], axis=0).astype(bf16)
        send_x, send_y, *g = together(send_x, send_y, *g)
        px, py = plan.send(send_x, 0), plan.send(send_y, 2)
        g = attention_back(segs, qkv_back, *back_args, 1, 1, g)
        px, py, *g = together(px, py, *g)
        z_sum = both_sums(0, 4) + px.astype(f32) + py.astype(f32)
        z_low, ffn, *g = together(z_sum[1:].astype(bf16), z_sum[0], *g)
        z_got = [plan.send(z_low[k - 1], 1, k) for k in range(1, 4)]
        g = attention_back(segs, qkv_back, *back_args, 2, PAIRS - 2, g)
        *z_got, dq, dk, dv = together(*z_got, *g)
        for part in z_got:
            ffn = ffn + part.astype(f32)
    else:
        dq, dk, dv = attention_back(segs, qkv, *back_args, 0, PAIRS, None)
        summed = (keep.astype(f32) + got_g.astype(f32)).astype(bf16)
        scale = plan.chips // SLOTS
        units = regroup_back(summed, [ROWS] * (1 + ff_cols) + [ROWS * ff_cols], scale)
        ffn = reduce_chips(plan, units)
    output = settle_rows(out_rows, out_got)
    small = half_of(sums, me) + sum_got
    tail = qkv_grads(push, small, tok, tok_got, dq, dk, dv)
    if plan.direct:
        rx, ry = plan.send(tail[12:14], 0), plan.send(tail[14:16], 2)
        far_back = input_back(w_qkv, dq, dk, dv, True, ())
        rx, ry, far_back = together(rx, ry, far_back)
        far_back = swap_pair(far_back)
        send_x = jnp.concatenate([tail[4:6], (tail[6:8].astype(f32) + ry.astype(f32)).astype(bf16)], axis=0)
        send_y = jnp.concatenate([(tail[8:10].astype(f32) + rx.astype(f32)).astype(bf16), tail[10:12]], axis=0)
        px, py = plan.send(send_x, 0), plan.send(send_y, 2)
        packed = input_back(w_qkv, dq, dk, dv, False, (resid1, far_back))
        px, py, packed = together(px, py, packed)
        packed_got = cross(packed)
        z_sum = tail[0:4].astype(f32) + px.astype(f32) + py.astype(f32)
        z_low = z_sum[1:].astype(bf16)
        qkv_sum = z_sum[0]
        packed_got, *z_got = together(packed_got, *[plan.send(z_low[k - 1], 1, k) for k in range(1, 4)])
        for part in z_got:
            qkv_sum = qkv_sum + part.astype(f32)
    else:
        far_back = swap_pair(input_back(w_qkv, dq, dk, dv, True, ()))
        packed = input_back(w_qkv, dq, dk, dv, False, (resid1, far_back))
        packed_got = cross(packed)
        units = regroup_back(tail[:, : 3 * ROWS], [ROWS] * 3, scale)
        extra = jnp.broadcast_to(tail[0:1, 3 * ROWS :], (plan.chips, 16, HALF))
        qkv_sum = reduce_chips(plan, jnp.concatenate([units, extra], axis=1))
    input_grad = settle_rows(packed, packed_got)

    small_sum = qkv_sum[6 * rows_dev :]
    sizes = sizes1 + sizes2
    total = jnp.concatenate([qkv_sum[: 6 * rows_dev], ffn], axis=0)
    mine, other = own_rows(me, total, sizes)
    got = swap_pair(jnp.concatenate([other, small_sum], axis=0))
    count = mine.shape[0]
    mine = jnp.concatenate([mine, small_sum], axis=0)
    full = jnp.concatenate([jnp.where(me == 0, mine, got), jnp.where(me == 0, got, mine)], axis=1)
    take = lambda at, size: full[at : at + size]
    out_qkv = jnp.concatenate([take(j * rows_dev, rows_dev) for j in range(3)], axis=1)
    out_out = take(3 * rows_dev, rows_dev)
    out_in = jnp.concatenate([take((4 + j) * rows_dev, rows_dev) for j in range(ff_cols)], axis=1)
    out_down = take((4 + ff_cols) * rows_dev, ff_dev)
    small_full = full[count:]
    device = plan.at(0)
    for a in range(1, len(plan.dims)):
        device = device * plan.dims[a] + plan.at(a)
    order = (14, 15, 0, 1, 2, 3, 3 + ff_cols, 4 + ff_cols, 5 + ff_cols)
    wide_row = 3
    thin = lax.dynamic_slice_in_dim(small_full, device * rows_dev, rows_dev, axis=1)
    span = small_full[wide_row : wide_row + ff_cols].reshape(-1)
    s = [lax.dynamic_slice_in_dim(span, device * ff_dev, ff_dev) if row == wide_row and piece is in_bias else thin[row]
         for piece, row in zip(smalls, order)]
    return (output[None], input_grad[None], out_qkv, s[0], s[1], out_out, s[2], s[3], s[4], out_in, s[5], out_down, s[6], s[7], s[8])


def regroup_back(buf, sizes, scale):
    n, _, w = buf.shape
    parts = []
    at = 0
    for size in sizes:
        parts.append(buf[:, at : at + size].reshape(n * scale, size // scale, w))
        at += size
    return jnp.concatenate(parts, axis=1)


def solution(mesh):
    plan = Plan(mesh.shape["seq"], mesh.shape["fsdp"])
    inner_mesh = Mesh(mesh.devices.reshape(plan.dims), tuple(plan.names))
    groups = tuple(plan.names[1:])
    every = tuple(plan.names)
    rows = P(groups, "s", None)
    table = P(groups, None)
    mat = P(every, None)
    vec = P(every)
    placed = (rows, table, table, mat, vec, vec, mat, vec, vec, vec, mat, vec, mat, vec, vec, vec, rows)
    outs = (rows, rows, mat, vec, vec, mat, vec, vec, vec, mat, vec, mat, vec, vec, vec)

    def run(*args):
        return local(plan, *args)

    return jax.shard_map(run, mesh=inner_mesh, in_specs=placed, out_specs=outs, check_vma=False)
```

```python
import functools

import jax
import jax.numpy as jnp
import numpy as np
from jax import lax
from jax.sharding import Mesh, PartitionSpec as P
from jax.experimental import pallas as pl
from jax.experimental.pallas import tpu as pltpu

D = 768
HALF = D // 2
HD = 64
UNITS = 16
SLOTS = 16
ROWS = D // SLOTS
PAIRS = HALF // 128
LOG2E = 1.4426950408889634
LN2 = 0.6931471805599453
BIG = 1e30
TQ = 1024
TQ_BACK = 512
STEP = 256
STEP_BACK = 1024
TM = 256
norm_eps = 1e-12
bf16 = jnp.bfloat16
f32 = jnp.float32
NT = (((1,), (1,)), ((), ()))
NN = (((1,), (0,)), ((), ()))
TN = (((0,), (0,)), ((), ()))
VMEM_CAP = 58 << 20


def mxu(a, b, dims=NN):
    return lax.dot_general(a, b, dims, preferred_element_type=f32)


def shape(size, kind=bf16):
    return jax.ShapeDtypeStruct(size, kind)


def params(axes=1):
    return pltpu.CompilerParams(dimension_semantics=("arbitrary",) * axes, vmem_limit_bytes=VMEM_CAP)


def cost(flops, moved):
    return pl.CostEstimate(flops=int(flops), bytes_accessed=int(moved), transcendentals=0)


def tie(value, *others):
    return lax.optimization_barrier((value,) + others)[0]


def lanes(rows):
    return lax.broadcasted_iota(jnp.int32, (rows, 128), 1)


def seg_rows(segs_ref, base_block, rows):
    place = lax.broadcasted_iota(jnp.int32, (rows, 128), 0)
    out = jnp.zeros((rows, 128), jnp.int32)
    for b in range(rows // 128):
        out = jnp.where(place >= b * 128, segs_ref[base_block + b], out)
    return out


def split3(v):
    hi = v.astype(bf16).astype(f32)
    mid = (v - hi).astype(bf16).astype(f32)
    return hi, mid, v - hi - mid


def both_heads(pair_rows):
    lane = lanes(pair_rows.shape[0])
    zero = jnp.zeros_like(pair_rows)
    first = jnp.where(lane < HD, pair_rows, zero)
    return jnp.concatenate([first, jnp.where(lane < HD, zero, pair_rows)], axis=0)


def fill_keys(segs_ref, k_in, v_in, k_aug, v_aug):
    for at in range(0, k_in.shape[0], STEP):
        rows = slice(at, at + STEP)
        lane = lanes(STEP)
        hot = (lane == seg_rows(segs_ref, at // 128, STEP)) | ((lane >= 64) & (lane < 67))
        k_aug[rows, :128] = k_in[rows, :]
        k_aug[rows, 128:] = jnp.where(hot, 1.0, 0.0).astype(bf16)
        v_aug[rows, :128] = v_in[rows, :]
        v_aug[rows, 128:] = jnp.ones((STEP, 128), bf16)


def attend_body(segs_ref, q_in, k_in, v_in, *refs):
    o_own, o_far, lse_ref, k_aug, v_aug = refs[-5:]
    i = pl.program_id(1)
    n_half = pl.num_programs(1) // 2

    @pl.when(i == 0)
    def _():
        fill_keys(segs_ref, k_in, v_in, k_aug, v_aug)

    lane = lanes(TQ)
    seg = seg_rows(segs_ref, i * (TQ // 128), TQ)
    off = jnp.where((lane < 16) & (lane != seg), -BIG, 0.0).astype(bf16)
    q_aug = jnp.concatenate([both_heads(q_in[...]), jnp.concatenate([off, off], axis=0)], axis=1)
    top = None
    acc = None
    for at in range(0, k_aug.shape[0], STEP):
        s = mxu(q_aug, k_aug[at : at + STEP, :], NT)
        here = jnp.max(s, axis=1, keepdims=True)
        new_top = here if top is None else jnp.maximum(top, here)
        p = jnp.exp2(s - new_top).astype(bf16)
        add = mxu(p, v_aug[at : at + STEP, :])
        acc = add if acc is None else acc * jnp.exp2(top - new_top) + add
        top = new_top
    both = jnp.where(lane < HD, acc[:TQ, :128], acc[TQ:, :128])
    sums = jnp.where(lane < HD, acc[:TQ, 128:], acc[TQ:, 128:])
    tops = jnp.where(lane < HD, top[:TQ], top[TQ:])
    out = (both / sums).astype(bf16)
    lse_ref[...] = tops + jnp.log2(sums)

    @pl.when(i < n_half)
    def _():
        o_own[...] = out

    @pl.when(i >= n_half)
    def _():
        o_far[...] = out


def anyspec():
    return pl.BlockSpec(memory_space=pl.ANY)


def pair_specs(n_half, first, rows):
    own = pl.BlockSpec((rows, 128), lambda h, i, *_: (jnp.minimum(i, n_half - 1), first + h))
    far = pl.BlockSpec((rows, 128), lambda h, i, *_: (jnp.maximum(i - n_half, 0), first + h))
    return own, far


def attention(segs, qkv, first, count, prev):
    total = qkv.shape[0]
    half = total // 2
    n_half = half // TQ
    own, far = pair_specs(n_half, first, TQ)
    row = pl.BlockSpec((TQ, 128), lambda h, i, *_: (i, first + h))
    whole = lambda part: pl.BlockSpec((total, 128), lambda h, i, *_: (0, part * PAIRS + first + h))
    prev = () if prev is None else tuple(prev)
    return pl.pallas_call(
        attend_body,
        grid_spec=pltpu.PrefetchScalarGridSpec(
            num_scalar_prefetch=1,
            grid=(count, 2 * n_half),
            in_specs=[row, whole(1), whole(2)] + [anyspec()] * len(prev),
            out_specs=[own, far, row],
            scratch_shapes=[pltpu.VMEM((total, 256), bf16), pltpu.VMEM((total, 256), bf16)],
        ),
        out_shape=[shape((half, HALF)), shape((half, HALF)), shape((total, HALF), f32)],
        input_output_aliases={4 + j: j for j in range(len(prev))},
        compiler_params=params(2),
        cost_estimate=cost(count * total * total * 2048, total * 128 * 2 * 8),
    )(segs, qkv, qkv, qkv, *prev)


def attend_back_body(segs_ref, q_in, k_in, v_in, o_own, o_far, d_own, d_far, lse_ref, *refs):
    dq_out, dk_out, dv_out, k_aug, v_aug, dk_acc, dv_acc, k_turn = refs[-8:]
    i = pl.program_id(1)
    n = pl.num_programs(1)

    @pl.when(i == 0)
    def _():
        fill_keys(segs_ref, k_in, v_in, k_aug, v_aug)
        k_turn[...] = k_in[...].T
        dk_acc[...] = jnp.zeros_like(dk_acc)
        dv_acc[...] = jnp.zeros_like(dv_acc)

    near = i < n // 2
    d_rows = jnp.where(near, d_own[...], d_far[...])
    o_rows = jnp.where(near, o_own[...], o_far[...])
    lane = lanes(TQ_BACK)
    seg = seg_rows(segs_ref, i * (TQ_BACK // 128), TQ_BACK)
    off = jnp.where((lane < 16) & (lane != seg), -BIG, 0.0)
    prod = d_rows.astype(f32) * o_rows.astype(f32)
    q_side, d_side = [], []
    for head in range(2):
        mine = (lane < HD) if head == 0 else (lane >= HD)
        dot_row = jnp.sum(jnp.where(mine, prod, 0.0), axis=1, keepdims=True)
        lse = jnp.broadcast_to(lse_ref[:, head * HD : head * HD + 1], (TQ_BACK, 128))
        for side, value, rest in ((q_side, -lse, off), (d_side, -jnp.broadcast_to(dot_row, (TQ_BACK, 128)), 0.0)):
            h, m, l = split3(value)
            cols = jnp.where(lane == 64, h, jnp.where(lane == 65, m, jnp.where(lane == 66, l, rest)))
            side.append(cols.astype(bf16))
    q2 = both_heads(q_in[...])
    d2 = both_heads(d_rows)
    q_aug = jnp.concatenate([q2, jnp.concatenate(q_side, axis=0)], axis=1)
    d_aug = jnp.concatenate([d2, jnp.concatenate(d_side, axis=0)], axis=1)
    dq = None
    for at in range(0, k_aug.shape[0], STEP_BACK):
        rows = slice(at, at + STEP_BACK)
        p = jnp.exp2(mxu(k_aug[rows, :], q_aug, NT))
        ds = (p * mxu(v_aug[rows, :], d_aug, NT)).astype(bf16)
        dv_acc[rows, :] += mxu(p.astype(bf16), d2)
        dk_acc[rows, :] += mxu(ds, q2)
        add = mxu(k_turn[:, rows], ds)
        dq = add if dq is None else dq + add
    dq = jnp.concatenate([dq[:HD, :TQ_BACK], dq[HD:, TQ_BACK:]], axis=0) * (HD ** -0.5)
    dq_out[...] = dq.T.astype(bf16)

    @pl.when(i == n - 1)
    def _():
        dk_out[...] = (dk_acc[...] * LN2).astype(bf16)
        dv_out[...] = dv_acc[...].astype(bf16)


def attention_back(segs, qkv, o_own, o_far, d_own, d_far, lse, first, count, prev):
    total = qkv.shape[0]
    half = total // 2
    n_half = half // TQ_BACK
    own, far = pair_specs(n_half, first, TQ_BACK)
    row = pl.BlockSpec((TQ_BACK, 128), lambda h, i, *_: (i, first + h))
    whole = lambda part: pl.BlockSpec((total, 128), lambda h, i, *_: (0, part * PAIRS + first + h))
    prev = () if prev is None else tuple(prev)
    return pl.pallas_call(
        attend_back_body,
        grid_spec=pltpu.PrefetchScalarGridSpec(
            num_scalar_prefetch=1,
            grid=(count, 2 * n_half),
            in_specs=[row, whole(1), whole(2), own, far, own, far, row] + [anyspec()] * len(prev),
            out_specs=[row, whole(0), whole(0)],
            scratch_shapes=[
                pltpu.VMEM((total, 256), bf16),
                pltpu.VMEM((total, 256), bf16),
                pltpu.VMEM((total, 128), f32),
                pltpu.VMEM((total, 128), f32),
                pltpu.VMEM((128, total), bf16),
            ],
        ),
        out_shape=[shape((total, HALF))] * 3,
        input_output_aliases={9 + j: j for j in range(len(prev))},
        compiler_params=params(2),
        cost_estimate=cost(count * total * total * 5120, total * 128 * 2 * 12),
    )(segs, qkv, qkv, qkv, o_own, o_far, d_own, d_far, lse, *prev)


def pack_body(qkv, w_out, w_in, w_down, *refs):
    lines, (mine, give) = refs[:-2], refs[-2:]
    me = lax.axis_index("c")
    for half_at, dst in ((me, mine), (1 - me, give)):
        slab = 0

        def cols(base):
            return pl.ds(pl.multiple_of(base + half_at * HALF, 128), HALF)

        for j in range(3):
            dst[slab] = qkv[:, cols(j * D)]
            slab += 1
        dst[slab] = jnp.zeros(dst.shape[1:], bf16)
        for i, line in enumerate(lines):
            value = line[...].astype(f32)
            dst[slab, i : i + 1, 0 : value.shape[1]] = value.astype(bf16)
        dst[slab + 1] = w_out[:, cols(0)]
        slab += 2
        for j in range(w_in.shape[1] // D):
            dst[slab] = w_in[:, cols(j * D)]
            slab += 1
        for j in range(w_down.shape[0]):
            dst[slab] = w_down[j, :, cols(0)]
            slab += 1


def combine_body(mine, got, unit1, unit2):
    me = lax.axis_index("c")
    n = unit2.shape[0] // 2
    wide = n // 2
    unit1[6] = jnp.zeros(unit1.shape[1:], bf16)
    for at, src in ((me, mine), (1 - me, got)):
        for j in range(3):
            unit1[2 * j + at] = src[j]
        for j in range(wide + 1):
            unit2[2 * j + at] = src[4 + j]
        for j in range(wide):
            unit2[2 * (wide + 1) + at * wide + j] = src[5 + wide + j]
    unit1[6, :, 0:128] = mine[3, :, 0:128]
    unit1[6, :, 128:256] = got[3, :, 0:128]


def whole_call(body, outs, *args):
    return pl.pallas_call(
        body,
        in_specs=[pl.BlockSpec(memory_space=pltpu.VMEM)] * len(args),
        out_specs=[pl.BlockSpec(memory_space=pltpu.VMEM)] * len(outs),
        out_shape=[shape(o) for o in outs],
        cost_estimate=cost(0, 2 << 20),
    )(*args)


def each_slot(pieces):
    at = 0
    for ref in pieces:
        for slot in range(ref.shape[0]):
            yield at, ref, slot
            at += 1


def wait_for(dst, sem):
    pltpu.make_async_copy(dst, dst, sem).wait()


def proj_body(info, t_own, t_got, bias, *refs):
    pieces, (out, w_out, w, sem) = refs[:-4], refs[-4:]
    i = pl.program_id(0)

    @pl.when(i == 0)
    def _():
        for at, ref, slot in each_slot(pieces):
            rows = pl.ds(pl.multiple_of(info[1 + at] * ROWS, ROWS), ROWS)
            for j in range(3):
                src = ref.at[slot, j * ROWS : (j + 1) * ROWS, :]
                pltpu.make_async_copy(src, w.at[rows, j * HALF : (j + 1) * HALF], sem).start()
        wait_for(w, sem)

    tile = jnp.where(i < pl.num_programs(0) // 2, t_own[...], t_got[...])
    for j in range(3):
        cols = slice(j * HALF, (j + 1) * HALF)
        part = mxu(tile, w[:, cols]) + bias[0:1, cols]
        if j == 0:
            part = part * (LOG2E * HD ** -0.5)
        out[:, cols] = part.astype(bf16)
    w_out[...] = w[...]


def project(info, t_own, t_got, bias, pieces):
    half = t_own.shape[0]
    tile = 512
    n_half = half // tile
    own = pl.BlockSpec((tile, D), lambda i, *_: (jnp.minimum(i, n_half - 1), 0))
    got = pl.BlockSpec((tile, D), lambda i, *_: (jnp.maximum(i - n_half, 0), 0))
    return pl.pallas_call(
        proj_body,
        grid_spec=pltpu.PrefetchScalarGridSpec(
            num_scalar_prefetch=1,
            grid=(2 * n_half,),
            in_specs=[own, got, pl.BlockSpec((1, 3 * HALF), lambda i, *_: (0, 0))] + [anyspec()] * len(pieces),
            out_specs=[
                pl.BlockSpec((tile, 3 * HALF), lambda i, *_: (i, 0)),
                pl.BlockSpec((D, 3 * HALF), lambda i, *_: (0, 0)),
            ],
            scratch_shapes=[pltpu.VMEM((D, 3 * HALF), bf16), pltpu.SemaphoreType.DMA],
        ),
        out_shape=[shape((2 * half, 3 * HALF)), shape((D, 3 * HALF))],
        compiler_params=params(),
        cost_estimate=cost(half * D * D * 6, half * D * 12),
    )(info, t_own, t_got, bias, *pieces)


def norm_stats(rows):
    mean = jnp.mean(rows, axis=-1, keepdims=True)
    centered = rows - mean
    var = jnp.mean(centered * centered, axis=-1, keepdims=True)
    rstd = lax.rsqrt(var + norm_eps)
    return centered * rstd, rstd


def norm_back(grad, unit, rstd, gain):
    eg = grad * gain
    mean_eg = jnp.mean(eg, axis=-1, keepdims=True)
    mean_en = jnp.mean(eg * unit, axis=-1, keepdims=True)
    return (eg - mean_eg - unit * mean_en) * rstd


def mid_body(info, tok, o_own, o_got, back, back_got, vecs, bias_in, *refs):
    n_out = 10
    outs, scratch = refs[-n_out - 5 : -5], refs[-5:]
    pieces = refs[: -n_out - 5]
    own_pieces, far_pieces = pieces[: len(pieces) // 2], pieces[len(pieces) // 2 :]
    out_rows, act_out, ig_out, low_out, branch_out, attn_out, resid_out, d_own, d_far, sums = outs
    w_out, w_in, w_down, slope, sems = scratch
    ff_cols = w_in.shape[1] // D
    me = info[0]

    @pl.when(pl.program_id(0) == 0)
    def _():
        for kind in range(3):
            for here, part in ((me, own_pieces), (1 - me, far_pieces)):
                for at, ref, slot in each_slot(part):
                    chip = info[1 + at]
                    lane0 = pl.multiple_of(here * HALF, HALF)
                    rows = pl.ds(pl.multiple_of(chip * ROWS, ROWS), ROWS)
                    if kind == 0:
                        pltpu.make_async_copy(ref.at[slot, 0:ROWS, :], w_out.at[rows, pl.ds(lane0, HALF)], sems.at[0]).start()
                    elif kind == 1:
                        for j in range(ff_cols):
                            src = ref.at[slot, (1 + j) * ROWS : (2 + j) * ROWS, :]
                            dst = w_in.at[rows, pl.ds(pl.multiple_of(lane0 + j * D, HALF), HALF)]
                            pltpu.make_async_copy(src, dst, sems.at[1]).start()
                    else:
                        size = ROWS * ff_cols
                        src = ref.at[slot, (1 + ff_cols) * ROWS : (1 + 2 * ff_cols) * ROWS, :]
                        dst = w_down.at[pl.ds(pl.multiple_of(chip * size, size), size), pl.ds(lane0, HALF)]
                        pltpu.make_async_copy(src, dst, sems.at[2]).start()
        sums[...] = jnp.zeros_like(sums)
        wait_for(w_out, sems.at[0])

    bias_o, gain1, shift1 = vecs[0:1, :], vecs[1:2, :], vecs[2:3, :]
    bias_d, gain2, shift2 = vecs[3:4, :], vecs[4:5, :], vecs[5:6, :]
    mine = w_out[pl.ds(pl.multiple_of(me * HALF, HALF), HALF), :]
    other = w_out[pl.ds(pl.multiple_of((1 - me) * HALF, HALF), HALF), :]
    resid = tok[...].astype(f32) + mxu(o_own[...], mine) + mxu(o_got[...], other) + bias_o
    unit1, rstd1 = norm_stats(resid)
    hidden = unit1 * gain1 + shift1
    low = hidden.astype(bf16)
    low_out[...] = low

    @pl.when(pl.program_id(0) == 0)
    def _():
        wait_for(w_in, sems.at[1])
        wait_for(w_down, sems.at[2])

    branch = bias_d
    for j in range(ff_cols):
        cols = slice(j * D, (j + 1) * D)
        inner = mxu(low, w_in[:, cols]) + bias_in[:, cols]
        phi = 0.5 + 0.5 * lax.erf(inner * (0.5 ** 0.5))
        act = (inner * phi).astype(bf16)
        act_out[:, cols] = act
        slope[:, cols] = phi + inner * (jnp.exp2(inner * inner * (-0.5 * LOG2E)) * 0.3989422804014327)
        branch = branch + mxu(act, w_down[cols, :])
    unit2, rstd2 = norm_stats(hidden + branch)
    out_rows[...] = (unit2 * gain2 + shift2).astype(bf16)
    grad = jnp.where(info[1 + SLOTS] == 1, back[...], back_got[...]).astype(f32)
    resid2 = norm_back(grad, unit2, rstd2, gain2)
    low_branch = resid2.astype(bf16)
    branch_out[...] = low_branch
    hidden_grad = resid2
    for j in range(ff_cols):
        cols = slice(j * D, (j + 1) * D)
        ig = (mxu(low_branch, w_down[cols, :], NT) * slope[:, cols]).astype(bf16)
        ig_out[:, cols] = ig
        hidden_grad = hidden_grad + mxu(ig, w_in[:, cols], NT)
        sums[3 + j : 4 + j, :] += jnp.sum(ig.astype(f32), axis=0, keepdims=True)
    resid1 = norm_back(hidden_grad, unit1, rstd1, gain1)
    resid_out[...] = resid1
    attn_grad = resid1.astype(bf16)
    attn_out[...] = attn_grad
    d_own[...] = mxu(attn_grad, mine, NT).astype(bf16)
    d_far[...] = mxu(attn_grad, other, NT).astype(bf16)
    rows = (
        (0, attn_grad.astype(f32)),
        (1, hidden_grad * unit1),
        (2, hidden_grad),
        (3 + ff_cols, low_branch.astype(f32)),
        (4 + ff_cols, grad * unit2),
        (5 + ff_cols, grad),
    )
    for at, value in rows:
        sums[at : at + 1, :] += jnp.sum(value, axis=0, keepdims=True)


def middle(info, tok, o_own, o_got, back, back_got, vecs, bias_in, own_pieces, far_pieces):
    half = tok.shape[0]
    ff = bias_in.shape[1]
    wide = pl.BlockSpec((TM, D), lambda i, *_: (i, 0))
    thin = pl.BlockSpec((TM, HALF), lambda i, *_: (i, 0))
    full = pl.BlockSpec((TM, ff), lambda i, *_: (i, 0))
    fixed = lambda rows, cols: pl.BlockSpec((rows, cols), lambda i, *_: (0, 0))
    pieces = tuple(own_pieces) + tuple(far_pieces)
    return pl.pallas_call(
        mid_body,
        grid_spec=pltpu.PrefetchScalarGridSpec(
            num_scalar_prefetch=1,
            grid=(half // TM,),
            in_specs=[wide, thin, thin, wide, wide, fixed(8, D), fixed(1, ff)] + [anyspec()] * len(pieces),
            out_specs=[wide, full, full, wide, wide, wide, wide, thin, thin, fixed(16, D)],
            scratch_shapes=[
                pltpu.VMEM((D, D), bf16),
                pltpu.VMEM((D, ff), bf16),
                pltpu.VMEM((ff, D), bf16),
                pltpu.VMEM((TM, ff), f32),
                pltpu.SemaphoreType.DMA((3,)),
            ],
        ),
        out_shape=[
            shape((half, D)),
            shape((half, ff)),
            shape((half, ff)),
            shape((half, D)),
            shape((half, D)),
            shape((half, D)),
            shape((half, D), f32),
            shape((half, HALF)),
            shape((half, HALF)),
            shape((16, D), f32),
        ],
        compiler_params=params(),
        cost_estimate=cost(half * D * (D + 2 * ff) * 4, half * D * 40),
    )(info, tok, o_own, o_got, back, back_got, vecs, bias_in, *pieces)


def wgrad_body(own, info, act, ig, low, branch, o_own, o_got, attn_grad, dst, res_in, res_down, res_out, sems):
    j = pl.program_id(0)
    n = pl.num_programs(0)
    me = info[0]
    par = lax.rem(j, 2)
    down_rows = ROWS * n
    per_step = SLOTS // n
    half_at = me if own else 1 - me
    lane = pl.ds(pl.multiple_of(half_at * HALF, HALF), HALF)

    @pl.when(j == 0)
    def _():
        grad = attn_grad[:, lane]
        for here, rows in ((me, o_own), (1 - me, o_got)):
            spot = pl.ds(pl.multiple_of(here * HALF, HALF), HALF)
            res_out[spot, :] = mxu(rows[...], grad, TN).astype(bf16)
        for chip in range(SLOTS):
            src = res_out.at[chip * ROWS : (chip + 1) * ROWS, :]
            pltpu.make_async_copy(src, dst.at[info[1 + chip], 0:ROWS, :], sems.at[2]).start()

    res_in[par] = mxu(low[...], ig[:, lane], TN).astype(bf16)
    for chip in range(SLOTS):
        src = res_in.at[par, chip * ROWS : (chip + 1) * ROWS, :]
        spot = pl.ds(pl.multiple_of((1 + j) * ROWS, ROWS), ROWS)
        pltpu.make_async_copy(src, dst.at[info[1 + chip], spot, :], sems.at[par]).start()
    res_down[par] = mxu(act[...], branch[:, lane], TN).astype(bf16)
    for q in range(per_step):
        src = res_down.at[par, q * down_rows : (q + 1) * down_rows, :]
        slot = info[1 + j * per_step + q]
        pltpu.make_async_copy(src, dst.at[slot, ROWS * (1 + n) : ROWS * (1 + 2 * n), :], sems.at[par]).start()

    def settle(which):
        wait_for(res_in.at[which], sems.at[which])
        wait_for(res_down.at[which], sems.at[which])

    @pl.when(j > 0)
    def _():
        settle(1 - par)

    @pl.when(j == n - 1)
    def _():
        settle(par)
        wait_for(res_out, sems.at[2])


def weight_grads(own, info, act, ig, low, branch, o_own, o_got, attn_grad):
    half, ff = act.shape
    n = ff // D
    strip = pl.BlockSpec((half, D), lambda j, *_: (0, j))
    fixed = lambda cols: pl.BlockSpec((half, cols), lambda j, *_: (0, 0))
    return pl.pallas_call(
        functools.partial(wgrad_body, own),
        grid_spec=pltpu.PrefetchScalarGridSpec(
            num_scalar_prefetch=1,
            grid=(n,),
            in_specs=[strip, strip, fixed(D), fixed(D), fixed(HALF), fixed(HALF), fixed(D)],
            out_specs=anyspec(),
            scratch_shapes=[
                pltpu.VMEM((2, D, HALF), bf16),
                pltpu.VMEM((2, D, HALF), bf16),
                pltpu.VMEM((D, HALF), bf16),
                pltpu.SemaphoreType.DMA((3,)),
            ],
        ),
        out_shape=shape((SLOTS, ROWS * (1 + 2 * n), HALF)),
        compiler_params=params(),
        cost_estimate=cost(half * D * (D + 2 * ff), half * ff * 8),
    )(info, act, ig, low, branch, o_own, o_got, attn_grad)


def qkv_grad_body(info, small, t_own, t_got, dq, dk, dv, out, t_all, d_all, res, res_small, sems):
    half = t_own.shape[0]
    pltpu.make_async_copy(t_own, t_all.at[0:half, :], sems.at[0]).start()
    pltpu.make_async_copy(t_got, t_all.at[half:, :], sems.at[0]).start()
    for j, src in enumerate((dq, dk, dv)):
        pltpu.make_async_copy(src, d_all.at[j], sems.at[1 + j]).start()
    wait_for(t_all, sems.at[0])
    res_small[...] = small[...].astype(bf16)
    row = lax.broadcasted_iota(jnp.int32, (16, HALF), 0)
    for j in range(3):
        wait_for(d_all.at[j], sems.at[1 + j])
        grads = d_all[j]
        res[j] = mxu(t_all[...], grads, TN).astype(bf16)
        for chip in range(SLOTS):
            src = res.at[j, chip * ROWS : (chip + 1) * ROWS, :]
            pltpu.make_async_copy(src, out.at[info[1 + chip], j * ROWS : (j + 1) * ROWS, :], sems.at[4]).start()
        if j != 1:
            total = jnp.sum(grads.astype(f32), axis=0, keepdims=True)
            place = 14 if j == 0 else 15
            res_small[...] = jnp.where(row == place, total, res_small[...].astype(f32)).astype(bf16)
    for slot in range(SLOTS):
        pltpu.make_async_copy(res_small, out.at[slot, 3 * ROWS : 3 * ROWS + 16, :], sems.at[5]).start()
    wait_for(res, sems.at[4])
    for slot in range(SLOTS):
        pltpu.make_async_copy(res_small, out.at[slot, 3 * ROWS : 3 * ROWS + 16, :], sems.at[5]).wait()


def qkv_grads(info, small, t_own, t_got, dq, dk, dv):
    total = dq.shape[0]
    return pl.pallas_call(
        qkv_grad_body,
        grid_spec=pltpu.PrefetchScalarGridSpec(
            num_scalar_prefetch=1,
            grid=(),
            in_specs=[pl.BlockSpec(memory_space=pltpu.VMEM)] + [anyspec()] * 5,
            out_specs=anyspec(),
            scratch_shapes=[
                pltpu.VMEM((total, D), bf16),
                pltpu.VMEM((3, total, HALF), bf16),
                pltpu.VMEM((3, D, HALF), bf16),
                pltpu.VMEM((16, HALF), bf16),
                pltpu.SemaphoreType.DMA((6,)),
            ],
        ),
        out_shape=shape((SLOTS, 3 * ROWS + 16, HALF)),
        compiler_params=pltpu.CompilerParams(vmem_limit_bytes=VMEM_CAP),
        cost_estimate=cost(total * D * HALF * 6, total * D * 5),
    )(info, small, t_own, t_got, dq, dk, dv)


def input_back_body(*refs):
    w = refs[0]
    dq, dk, dv = refs[1:4]
    out = refs[-1]
    total = None
    for j, part in enumerate((dq, dk, dv)):
        add = mxu(part[...], w[:, j * HALF : (j + 1) * HALF], NT)
        total = add if total is None else total + add
    for extra in refs[4:-1]:
        total = total + extra[...].astype(f32)
    out[...] = total.astype(bf16)


def input_back(w, dq, dk, dv, far, extras):
    half = dq.shape[0] // 2
    tile = 512
    base = half // tile if far else 0
    part = pl.BlockSpec((tile, HALF), lambda i: (base + i, 0))
    row = pl.BlockSpec((tile, D), lambda i: (i, 0))
    return pl.pallas_call(
        input_back_body,
        grid=(half // tile,),
        in_specs=[pl.BlockSpec((D, 3 * HALF), lambda i: (0, 0)), part, part, part] + [row] * len(extras),
        out_specs=row,
        out_shape=shape((half, D)),
        compiler_params=params(),
        cost_estimate=cost(half * D * HALF * 6, half * D * 8),
    )(w, dq, dk, dv, *extras)


def shift(n, k):
    return [(i, (i + k) % n) for i in range(n)]


class Plan:
    def __init__(self, seq, fsdp):
        rest = fsdp // 2
        dims = []
        while rest > 1:
            want = 4 if len(dims) % 2 == 0 and rest % 4 == 0 else 2
            dims.append(want)
            rest //= want
        self.dims = [seq] + dims + [2]
        self.names = ["s"] + ["r%d" % i for i in range(len(dims))] + ["c"]
        self.chips = seq * fsdp // 2
        self.direct = self.dims == [2, 4, 2, 2]
        self.stages = ([1] if dims else []) + [0] + list(range(2, len(dims) + 1))

    def at(self, a):
        return lax.axis_index(self.names[a])

    def chip_table(self, sign):
        if not self.direct:
            return jnp.arange(SLOTS, dtype=jnp.int32)
        spots = []
        for dx, dy in ((0, 0), (1, 0), (0, 1), (1, 1)):
            spots += [(dx, dy, z) for z in range(4)]
        dx, dy, dz = (jnp.asarray(v, jnp.int32) for v in zip(*spots))
        return ((self.at(0) + sign * dx) % 2) * 8 + ((self.at(1) + sign * dz) % 4) * 2 + (self.at(2) + sign * dy) % 2

    def slot_table(self, sign):
        table = self.chip_table(sign)
        hit = table[:, None] == jnp.arange(SLOTS, dtype=jnp.int32)[None, :]
        return jnp.sum(jnp.where(hit, jnp.arange(SLOTS, dtype=jnp.int32)[:, None], 0), axis=0)

    def places(self, sign):
        grid = np.indices(self.dims[:-1]).reshape(len(self.dims) - 1, -1)
        flat = jnp.zeros((self.chips,), jnp.int32)
        if sign < 0:
            for a in reversed(self.stages):
                n = self.dims[a]
                flat = flat * n + (self.at(a) - jnp.asarray(grid[a], jnp.int32)) % n
            return flat
        sizes = [self.dims[a] for a in reversed(self.stages)]
        offs = np.indices(sizes).reshape(len(sizes), -1)
        by_axis = {a: offs[j] for j, a in enumerate(reversed(self.stages))}
        for a in range(len(self.dims) - 1):
            n = self.dims[a]
            flat = flat * n + (self.at(a) + jnp.asarray(by_axis[a], jnp.int32)) % n
        return flat

    def send(self, x, a, k=1):
        return lax.ppermute(x, self.names[a], shift(self.dims[a], k))


def gather_chips(plan, unit):
    buf = unit[None]
    for a in plan.stages:
        n = plan.dims[a]
        if n > 1:
            buf = jnp.concatenate([buf] + [plan.send(buf, a, k) for k in range(1, n)], axis=0)
    return jnp.take(buf, plan.places(-1), axis=0, mode="clip")


def reduce_chips(plan, grads):
    buf = jnp.take(grads, plan.places(1), axis=0, mode="clip")
    for a in reversed(plan.stages):
        n = plan.dims[a]
        size = buf.shape[0] // n
        keep = buf[:size].astype(f32)
        for k in range(1, n):
            keep = keep + plan.send(buf[k * size : (k + 1) * size].astype(bf16), a, k).astype(f32)
        buf = keep if a == plan.stages[0] else keep.astype(bf16)
    return buf[0]


def regroup(buf, sizes, count):
    n, _, w = buf.shape
    parts = []
    at = 0
    for size in sizes:
        parts.append(buf[:, at : at + size].reshape(count, n * size // count, w))
        at += size
    return jnp.concatenate(parts, axis=1)


def gather_z(plan, unit):
    return jnp.concatenate([unit[None]] + [plan.send(unit, 1, k)[None] for k in range(1, 4)], axis=0)


def swap_pair(x):
    return lax.ppermute(x, "c", [(0, 1), (1, 0)])


def cross(x):
    return lax.ppermute(x, ("s", "c"), [(1, 2), (2, 1)])


def together(*values):
    return lax.optimization_barrier(values)


def half_of(x, at):
    return lax.dynamic_slice_in_dim(x, at * HALF, HALF, axis=x.ndim - 1)


def chip_units(me, mine, got, sizes):
    low = jnp.where(me == 0, mine, got)
    high = jnp.where(me == 0, got, mine)
    parts = []
    at = 0
    for size in sizes:
        parts += [low[at : at + size], high[at : at + size]]
        at += size
    return jnp.concatenate(parts, axis=0)


def own_rows(me, total, sizes):
    first, second = [], []
    at = 0
    for size in sizes:
        first.append(total[at : at + size])
        second.append(total[at + size : at + 2 * size])
        at += 2 * size
    first = jnp.concatenate(first, axis=0)
    second = jnp.concatenate(second, axis=0)
    return jnp.where(me == 0, first, second), jnp.where(me == 0, second, first)


def local(plan, tokens, lengths, block_order, qkv_weight, query_bias, value_bias, out_weight, out_bias,
          norm1_gain, norm1_shift, in_weight, in_bias, down_weight, down_bias, norm2_gain, norm2_shift, cotangent):
    half = tokens.shape[1]
    me = plan.at(len(plan.dims) - 1)
    stays = plan.at(0) == me
    rows_dev = qkv_weight.shape[0]
    ff_dev = down_weight.shape[0]
    ff_cols = in_weight.shape[1] // D
    me32 = me.astype(jnp.int32)
    pull = jnp.concatenate([me32[None], plan.chip_table(-1), stays.astype(jnp.int32)[None]])
    push = jnp.concatenate([me32[None], plan.slot_table(1)])
    sizes1 = [rows_dev] * 3
    sizes2 = [rows_dev] * (1 + ff_cols) + [ff_dev]
    smalls = (query_bias, value_bias, out_bias, norm1_gain, norm1_shift, in_bias, down_bias, norm2_gain, norm2_shift)
    unit_rows = 2 * half // UNITS

    def settle_rows(x, got):
        return jnp.where(stays, x, got)

    tok = settle_rows(tokens[0], cross(tokens[0]))
    if plan.direct:
        lines = [v[None] for v in smalls] + [lengths, block_order]
        slab = (5 + 2 * ff_cols, rows_dev, HALF)
        mine, give = whole_call(pack_body, (slab, slab), qkv_weight, out_weight, in_weight,
                                down_weight.reshape(ff_cols, rows_dev, D), *lines)
        got = swap_pair(give)
        unit1, unit2 = whole_call(combine_body, ((7, rows_dev, HALF), (2 + 4 * ff_cols, rows_dev, HALF)), mine, got)
        unit1 = unit1.reshape(7 * rows_dev, HALF)
        unit2 = unit2.reshape(-1, HALF)
        other = got[3, len(smalls) : len(smalls) + 2, :UNITS].astype(jnp.int32)
        counts_here = jnp.where(stays, lengths[0], other[0]) // unit_rows
        order_here = jnp.where(stays, block_order[0], other[1])

        z1 = gather_z(plan, unit1)
        unit2, z1 = together(unit2, z1)
        x1, y1 = plan.send(z1, 0), plan.send(z1, 2)
        z2_parts = [unit2] + [plan.send(unit2, 1, k) for k in range(1, 4)]
        cot, x1, y1 = together(cotangent[0], x1, y1)
        d1a, d1b = plan.send(y1[0:2], 0), plan.send(x1[2:4], 2)
        cot_got = cross(cot)
        pieces1 = [z1, x1, y1, d1a, d1b]
        tail_rows = [p[:, 6 * rows_dev : 6 * rows_dev + 16, 0:256] for p in pieces1]
        table = jnp.take(jnp.concatenate(tail_rows, axis=0), plan.slot_table(-1), axis=0, mode="clip")
        table = table.reshape(plan.chips, 16, 2, 128)
        table = jnp.where(me == 0, table, table[:, :, ::-1])
        vectors = [table[:, i, :, : v.shape[0]].reshape(-1).astype(f32) for i, v in enumerate(smalls)]
    else:
        first = jnp.concatenate([qkv_weight[:, j * D : (j + 1) * D] for j in range(3)], axis=0)
        second = jnp.concatenate([out_weight] + [in_weight[:, j * D : (j + 1) * D] for j in range(ff_cols)] + [down_weight], axis=0)
        line = jnp.concatenate(smalls)
        both = jnp.concatenate([first, second], axis=0)
        got = swap_pair(half_of(both, 1 - me))
        mine = half_of(both, me)
        cut = 3 * rows_dev
        unit1 = chip_units(me, mine[:cut], got[:cut], sizes1)
        unit2 = chip_units(me, mine[cut:], got[cut:], sizes2)
        line_got = swap_pair(line)
        line_unit = jnp.stack([jnp.where(me == 0, line, line_got), jnp.where(me == 0, line_got, line)])
        pieces1 = [regroup(gather_chips(plan, unit1), [2 * r for r in sizes1], SLOTS)]
        pieces2 = [regroup(gather_chips(plan, unit2), [2 * r for r in sizes2], SLOTS)]
        far2 = [swap_pair(p) for p in pieces2]
        lines = gather_chips(plan, line_unit).reshape(2 * plan.chips, line.shape[0])
        vectors = []
        at = 0
        for piece in smalls:
            size = piece.shape[0]
            vectors.append(lines[:, at : at + size].reshape(2 * plan.chips * size).astype(f32))
            at += size
        counts_here = jnp.where(stays, lengths[0], swap_pair(lengths[0])) // unit_rows
        order_here = jnp.where(stays, block_order[0], swap_pair(block_order[0]))
        cot_got = cross(cotangent[0])
    bias_q, bias_v, bias_o, gain1, shift1, bias_in, bias_d, gain2, shift2 = vectors
    bias_qkv = jnp.concatenate([half_of(bias_q, me), jnp.zeros((HALF,), f32), half_of(bias_v, me)])[None]
    zero = jnp.zeros((D,), f32)
    vecs = jnp.stack([bias_o, gain1, shift1, bias_d, gain2, shift2, zero, zero])

    spot = jnp.arange(UNITS)
    ends = jnp.sum(jnp.where(spot[None, :] <= spot[:, None], counts_here[None, :], 0), axis=1)
    seg_packed = jnp.sum((spot[:, None] >= ends[None, :]).astype(jnp.int32), axis=1)
    hit = order_here[:, None] == spot[None, :]
    segs = jnp.sum(jnp.where(hit, seg_packed[:, None], 0), axis=0)
    segs = jnp.where(me == 0, segs, jnp.roll(segs, UNITS // 2))

    tok_got = swap_pair(tok)
    qkv, w_qkv = project(pull, tok, tok_got, bias_qkv, pieces1)
    if plan.direct:
        *z2_parts, qkv = together(*z2_parts, qkv)
        z2 = jnp.stack(z2_parts)
        x2, y2 = plan.send(z2, 0), plan.send(z2, 2)
        z2_far = swap_pair(z2)
        att = attention(segs, qkv, 0, 2, None)
        x2, y2, cot_got, *att = together(x2, y2, cot_got, *att)
        d2a, d2b = plan.send(y2[0:2], 0), plan.send(x2[2:4], 2)
        x2_far, y2_far = swap_pair(x2), swap_pair(y2)
    else:
        att = attention(segs, qkv, 0, 2, None)
    o_own, o_far, lse = attention(segs, qkv, 2, PAIRS - 2, att)
    o_got = swap_pair(o_far)
    if plan.direct:
        pieces2 = [z2, x2, y2, d2a, d2b]
        far2 = [z2_far, x2_far, y2_far, swap_pair(d2a), swap_pair(d2b)]
    (out_rows, act, ig, low, branch, attn_grad, resid1, d_own, d_far, sums) = middle(
        pull, tok, o_own, o_got, cotangent[0], cot_got, vecs, bias_in[None], pieces2, far2)
    d_got = swap_pair(d_far)
    out_got = cross(out_rows)
    sum_got = swap_pair(half_of(sums, 1 - me))
    grad_args = (low, branch, o_own, o_got)
    give = weight_grads(False, push, act, ig, *grad_args, attn_grad)
    give, attn_grad = together(give, attn_grad)
    got_g = swap_pair(give)
    keep = weight_grads(True, push, act, ig, *grad_args, attn_grad)
    back_args = (o_own, o_far, d_own, d_got, lse)
    if plan.direct:

        def both_sums(lo, hi):
            return keep[lo:hi].astype(f32) + got_g[lo:hi].astype(f32)

        step1 = both_sums(12, 16).astype(bf16)
        sx, sy, qkv_back, out_got = together(step1[:2], step1[2:], qkv, out_got)
        rx, ry = plan.send(sx, 0), plan.send(sy, 2)
        g = attention_back(segs, qkv_back, *back_args, 0, 1, None)
        rx, ry, sum_got, *g = together(rx, ry, sum_got, *g)
        send_x = jnp.concatenate([both_sums(4, 6), both_sums(6, 8) + ry.astype(f32)], axis=0).astype(bf16)
        send_y = jnp.concatenate([both_sums(8, 10) + rx.astype(f32), both_sums(10, 12)], axis=0).astype(bf16)
        send_x, send_y, *g = together(send_x, send_y, *g)
        px, py = plan.send(send_x, 0), plan.send(send_y, 2)
        g = attention_back(segs, qkv_back, *back_args, 1, 1, g)
        px, py, *g = together(px, py, *g)
        z_sum = both_sums(0, 4) + px.astype(f32) + py.astype(f32)
        z_low, ffn, *g = together(z_sum[1:].astype(bf16), z_sum[0], *g)
        z_got = [plan.send(z_low[k - 1], 1, k) for k in range(1, 4)]
        g = attention_back(segs, qkv_back, *back_args, 2, PAIRS - 2, g)
        *z_got, dq, dk, dv = together(*z_got, *g)
        for part in z_got:
            ffn = ffn + part.astype(f32)
    else:
        dq, dk, dv = attention_back(segs, qkv, *back_args, 0, PAIRS, None)
        summed = (keep.astype(f32) + got_g.astype(f32)).astype(bf16)
        scale = plan.chips // SLOTS
        units = regroup_back(summed, [ROWS] * (1 + ff_cols) + [ROWS * ff_cols], scale)
        ffn = reduce_chips(plan, units)
    small = half_of(sums, me) + sum_got
    tail = qkv_grads(push, small, tok, tok_got, dq, dk, dv)
    if plan.direct:
        rx, ry = plan.send(tail[12:14], 0), plan.send(tail[14:16], 2)
        far_back = input_back(w_qkv, dq, dk, dv, True, ())
        rx, ry, far_back = together(rx, ry, far_back)
        far_back = swap_pair(far_back)
        send_x = jnp.concatenate([tail[4:6], (tail[6:8].astype(f32) + ry.astype(f32)).astype(bf16)], axis=0)
        send_y = jnp.concatenate([(tail[8:10].astype(f32) + rx.astype(f32)).astype(bf16), tail[10:12]], axis=0)
        px, py = plan.send(send_x, 0), plan.send(send_y, 2)
        packed = input_back(w_qkv, dq, dk, dv, False, (resid1, far_back))
        px, py, packed = together(px, py, packed)
        packed_got = cross(packed)
        z_sum = tail[0:4].astype(f32) + px.astype(f32) + py.astype(f32)
        z_low = z_sum[1:].astype(bf16)
        qkv_sum = z_sum[0]
        output = settle_rows(out_rows, out_got)
        packed_got, output, *z_got = together(packed_got, output, *[plan.send(z_low[k - 1], 1, k) for k in range(1, 4)])
        for part in z_got:
            qkv_sum = qkv_sum + part.astype(f32)
    else:
        far_back = swap_pair(input_back(w_qkv, dq, dk, dv, True, ()))
        packed = input_back(w_qkv, dq, dk, dv, False, (resid1, far_back))
        packed_got = cross(packed)
        output = settle_rows(out_rows, out_got)
        units = regroup_back(tail[:, : 3 * ROWS], [ROWS] * 3, scale)
        extra = jnp.broadcast_to(tail[0:1, 3 * ROWS :], (plan.chips, 16, HALF))
        qkv_sum = reduce_chips(plan, jnp.concatenate([units, extra], axis=1))
    input_grad = settle_rows(packed, packed_got)

    small_sum = qkv_sum[6 * rows_dev :]
    sizes = sizes1 + sizes2
    total = jnp.concatenate([qkv_sum[: 6 * rows_dev], ffn], axis=0)
    mine, other = own_rows(me, total, sizes)
    got = swap_pair(jnp.concatenate([other, small_sum], axis=0))
    count = mine.shape[0]
    mine = jnp.concatenate([mine, small_sum], axis=0)
    full = jnp.concatenate([jnp.where(me == 0, mine, got), jnp.where(me == 0, got, mine)], axis=1)
    take = lambda at, size: full[at : at + size]
    out_qkv = jnp.concatenate([take(j * rows_dev, rows_dev) for j in range(3)], axis=1)
    out_out = take(3 * rows_dev, rows_dev)
    out_in = jnp.concatenate([take((4 + j) * rows_dev, rows_dev) for j in range(ff_cols)], axis=1)
    out_down = take((4 + ff_cols) * rows_dev, ff_dev)
    small_full = full[count:]
    device = plan.at(0)
    for a in range(1, len(plan.dims)):
        device = device * plan.dims[a] + plan.at(a)
    order = (14, 15, 0, 1, 2, 3, 3 + ff_cols, 4 + ff_cols, 5 + ff_cols)
    wide_row = 3
    thin = lax.dynamic_slice_in_dim(small_full, device * rows_dev, rows_dev, axis=1)
    span = small_full[wide_row : wide_row + ff_cols].reshape(-1)
    s = [lax.dynamic_slice_in_dim(span, device * ff_dev, ff_dev) if row == wide_row and piece is in_bias else thin[row]
         for piece, row in zip(smalls, order)]
    return (output[None], input_grad[None], out_qkv, s[0], s[1], out_out, s[2], s[3], s[4], out_in, s[5], out_down, s[6], s[7], s[8])


def regroup_back(buf, sizes, scale):
    n, _, w = buf.shape
    parts = []
    at = 0
    for size in sizes:
        parts.append(buf[:, at : at + size].reshape(n * scale, size // scale, w))
        at += size
    return jnp.concatenate(parts, axis=1)


def solution(mesh):
    plan = Plan(mesh.shape["seq"], mesh.shape["fsdp"])
    inner_mesh = Mesh(mesh.devices.reshape(plan.dims), tuple(plan.names))
    groups = tuple(plan.names[1:])
    every = tuple(plan.names)
    rows = P(groups, "s", None)
    table = P(groups, None)
    mat = P(every, None)
    vec = P(every)
    placed = (rows, table, table, mat, vec, vec, mat, vec, vec, vec, mat, vec, mat, vec, vec, vec, rows)
    outs = (rows, rows, mat, vec, vec, mat, vec, vec, vec, mat, vec, mat, vec, vec, vec)

    def run(*args):
        return local(plan, *args)

    return jax.shard_map(run, mesh=inner_mesh, in_specs=placed, out_specs=outs, check_vma=False)
```

```python
import jax
import jax.numpy as jnp
import numpy as np
from jax import lax
from jax.sharding import Mesh, PartitionSpec as P
from jax.experimental import pallas as pl
from jax.experimental.pallas import tpu as pltpu

D = 768
HALF = D // 2
HD = 64
UNITS = 16
SLOTS = 16
ROWS = D // SLOTS
PAIRS = HALF // 128
LOG2E = 1.4426950408889634
LN2 = 0.6931471805599453
BIG = 1e30
TQ = 1024
TQ_BACK = 512
STEP = 256
STEP_BACK = 1024
TM = 256
norm_eps = 1e-12
bf16 = jnp.bfloat16
f32 = jnp.float32
NT = (((1,), (1,)), ((), ()))
NN = (((1,), (0,)), ((), ()))
TN = (((0,), (0,)), ((), ()))
VMEM_CAP = 58 << 20


def mxu(a, b, dims=NN):
    return lax.dot_general(a, b, dims, preferred_element_type=f32)


def shape(size, kind=bf16):
    return jax.ShapeDtypeStruct(size, kind)


def params(axes=1):
    return pltpu.CompilerParams(dimension_semantics=("arbitrary",) * axes, vmem_limit_bytes=VMEM_CAP)


def cost(flops, moved):
    return pl.CostEstimate(flops=int(flops), bytes_accessed=int(moved), transcendentals=0)


def tie(value, *others):
    return lax.optimization_barrier((value,) + others)[0]


def lanes(rows):
    return lax.broadcasted_iota(jnp.int32, (rows, 128), 1)


def seg_rows(segs_ref, base_block, rows):
    place = lax.broadcasted_iota(jnp.int32, (rows, 128), 0)
    out = jnp.zeros((rows, 128), jnp.int32)
    for b in range(rows // 128):
        out = jnp.where(place >= b * 128, segs_ref[base_block + b], out)
    return out


def split3(v):
    hi = v.astype(bf16).astype(f32)
    mid = (v - hi).astype(bf16).astype(f32)
    return hi, mid, v - hi - mid


def both_heads(pair_rows):
    lane = lanes(pair_rows.shape[0])
    zero = jnp.zeros_like(pair_rows)
    first = jnp.where(lane < HD, pair_rows, zero)
    return jnp.concatenate([first, jnp.where(lane < HD, zero, pair_rows)], axis=0)


def fill_keys(segs_ref, k_in, v_in, k_aug, v_aug):
    for at in range(0, k_in.shape[0], STEP):
        rows = slice(at, at + STEP)
        lane = lanes(STEP)
        hot = (lane == seg_rows(segs_ref, at // 128, STEP)) | ((lane >= 64) & (lane < 67))
        k_aug[rows, :128] = k_in[rows, :]
        k_aug[rows, 128:] = jnp.where(hot, 1.0, 0.0).astype(bf16)
        v_aug[rows, :128] = v_in[rows, :]
        v_aug[rows, 128:] = jnp.ones((STEP, 128), bf16)


def attend_body(segs_ref, q_in, k_in, v_in, *refs):
    o_own, o_far, lse_ref, k_aug, v_aug = refs[-5:]
    i = pl.program_id(1)
    n_half = pl.num_programs(1) // 2

    @pl.when(i == 0)
    def _():
        fill_keys(segs_ref, k_in, v_in, k_aug, v_aug)

    lane = lanes(TQ)
    seg = seg_rows(segs_ref, i * (TQ // 128), TQ)
    off = jnp.where((lane < 16) & (lane != seg), -BIG, 0.0).astype(bf16)
    q_aug = jnp.concatenate([both_heads(q_in[...]), jnp.concatenate([off, off], axis=0)], axis=1)
    top = None
    acc = None
    for at in range(0, k_aug.shape[0], STEP):
        s = mxu(q_aug, k_aug[at : at + STEP, :], NT)
        here = jnp.max(s, axis=1, keepdims=True)
        new_top = here if top is None else jnp.maximum(top, here)
        p = jnp.exp2(s - new_top).astype(bf16)
        add = mxu(p, v_aug[at : at + STEP, :])
        acc = add if acc is None else acc * jnp.exp2(top - new_top) + add
        top = new_top
    both = jnp.where(lane < HD, acc[:TQ, :128], acc[TQ:, :128])
    sums = jnp.where(lane < HD, acc[:TQ, 128:], acc[TQ:, 128:])
    tops = jnp.where(lane < HD, top[:TQ], top[TQ:])
    out = (both / sums).astype(bf16)
    lse_ref[...] = tops + jnp.log2(sums)

    @pl.when(i < n_half)
    def _():
        o_own[...] = out

    @pl.when(i >= n_half)
    def _():
        o_far[...] = out


def anyspec():
    return pl.BlockSpec(memory_space=pl.ANY)


def pair_specs(n_half, first, rows):
    own = pl.BlockSpec((rows, 128), lambda h, i, *_: (jnp.minimum(i, n_half - 1), first + h))
    far = pl.BlockSpec((rows, 128), lambda h, i, *_: (jnp.maximum(i - n_half, 0), first + h))
    return own, far


def attention(segs, qkv, first, count, prev):
    total = qkv.shape[0]
    half = total // 2
    n_half = half // TQ
    own, far = pair_specs(n_half, first, TQ)
    row = pl.BlockSpec((TQ, 128), lambda h, i, *_: (i, first + h))
    whole = lambda part: pl.BlockSpec((total, 128), lambda h, i, *_: (0, part * PAIRS + first + h))
    prev = () if prev is None else tuple(prev)
    return pl.pallas_call(
        attend_body,
        grid_spec=pltpu.PrefetchScalarGridSpec(
            num_scalar_prefetch=1,
            grid=(count, 2 * n_half),
            in_specs=[row, whole(1), whole(2)] + [anyspec()] * len(prev),
            out_specs=[own, far, row],
            scratch_shapes=[pltpu.VMEM((total, 256), bf16), pltpu.VMEM((total, 256), bf16)],
        ),
        out_shape=[shape((half, HALF)), shape((half, HALF)), shape((total, HALF), f32)],
        input_output_aliases={4 + j: j for j in range(len(prev))},
        compiler_params=params(2),
        cost_estimate=cost(count * total * total * 2048, total * 128 * 2 * 8),
    )(segs, qkv, qkv, qkv, *prev)


def attend_back_body(segs_ref, q_in, k_in, v_in, o_own, o_far, d_own, d_far, lse_ref, *refs):
    dq_out, dk_out, dv_out, k_aug, v_aug, dk_acc, dv_acc, k_turn = refs[-8:]
    i = pl.program_id(1)
    n = pl.num_programs(1)

    @pl.when(i == 0)
    def _():
        fill_keys(segs_ref, k_in, v_in, k_aug, v_aug)
        k_turn[...] = k_in[...].T
        dk_acc[...] = jnp.zeros_like(dk_acc)
        dv_acc[...] = jnp.zeros_like(dv_acc)

    near = i < n // 2
    d_rows = jnp.where(near, d_own[...], d_far[...])
    o_rows = jnp.where(near, o_own[...], o_far[...])
    lane = lanes(TQ_BACK)
    seg = seg_rows(segs_ref, i * (TQ_BACK // 128), TQ_BACK)
    off = jnp.where((lane < 16) & (lane != seg), -BIG, 0.0)
    prod = d_rows.astype(f32) * o_rows.astype(f32)
    q_side, d_side = [], []
    for head in range(2):
        mine = (lane < HD) if head == 0 else (lane >= HD)
        dot_row = jnp.sum(jnp.where(mine, prod, 0.0), axis=1, keepdims=True)
        lse = jnp.broadcast_to(lse_ref[:, head * HD : head * HD + 1], (TQ_BACK, 128))
        for side, value, rest in ((q_side, -lse, off), (d_side, -jnp.broadcast_to(dot_row, (TQ_BACK, 128)), 0.0)):
            h, m, l = split3(value)
            cols = jnp.where(lane == 64, h, jnp.where(lane == 65, m, jnp.where(lane == 66, l, rest)))
            side.append(cols.astype(bf16))
    q2 = both_heads(q_in[...])
    d2 = both_heads(d_rows)
    q_aug = jnp.concatenate([q2, jnp.concatenate(q_side, axis=0)], axis=1)
    d_aug = jnp.concatenate([d2, jnp.concatenate(d_side, axis=0)], axis=1)
    dq = None
    for at in range(0, k_aug.shape[0], STEP_BACK):
        rows = slice(at, at + STEP_BACK)
        p = jnp.exp2(mxu(k_aug[rows, :], q_aug, NT))
        ds = (p * mxu(v_aug[rows, :], d_aug, NT)).astype(bf16)
        dv_acc[rows, :] += mxu(p.astype(bf16), d2)
        dk_acc[rows, :] += mxu(ds, q2)
        add = mxu(k_turn[:, rows], ds)
        dq = add if dq is None else dq + add
    dq = jnp.concatenate([dq[:HD, :TQ_BACK], dq[HD:, TQ_BACK:]], axis=0) * (HD ** -0.5)
    dq_out[...] = dq.T.astype(bf16)

    @pl.when(i == n - 1)
    def _():
        dk_out[...] = (dk_acc[...] * LN2).astype(bf16)
        dv_out[...] = dv_acc[...].astype(bf16)


def attention_back(segs, qkv, o_own, o_far, d_own, d_far, lse, first, count, prev):
    total = qkv.shape[0]
    half = total // 2
    n_half = half // TQ_BACK
    own, far = pair_specs(n_half, first, TQ_BACK)
    row = pl.BlockSpec((TQ_BACK, 128), lambda h, i, *_: (i, first + h))
    whole = lambda part: pl.BlockSpec((total, 128), lambda h, i, *_: (0, part * PAIRS + first + h))
    prev = () if prev is None else tuple(prev)
    return pl.pallas_call(
        attend_back_body,
        grid_spec=pltpu.PrefetchScalarGridSpec(
            num_scalar_prefetch=1,
            grid=(count, 2 * n_half),
            in_specs=[row, whole(1), whole(2), own, far, own, far, row] + [anyspec()] * len(prev),
            out_specs=[row, whole(0), whole(0)],
            scratch_shapes=[
                pltpu.VMEM((total, 256), bf16),
                pltpu.VMEM((total, 256), bf16),
                pltpu.VMEM((total, 128), f32),
                pltpu.VMEM((total, 128), f32),
                pltpu.VMEM((128, total), bf16),
            ],
        ),
        out_shape=[shape((total, HALF))] * 3,
        input_output_aliases={9 + j: j for j in range(len(prev))},
        compiler_params=params(2),
        cost_estimate=cost(count * total * total * 5120, total * 128 * 2 * 12),
    )(segs, qkv, qkv, qkv, o_own, o_far, d_own, d_far, lse, *prev)


def pack_body(qkv, w_out, w_in, w_down, *refs):
    lines, (mine, give) = refs[:-2], refs[-2:]
    me = lax.axis_index("c")
    for half_at, dst in ((me, mine), (1 - me, give)):
        slab = 0

        def cols(base):
            return pl.ds(pl.multiple_of(base + half_at * HALF, 128), HALF)

        for j in range(3):
            dst[slab] = qkv[:, cols(j * D)]
            slab += 1
        dst[slab] = jnp.zeros(dst.shape[1:], bf16)
        for i, line in enumerate(lines):
            value = line[...].astype(f32)
            dst[slab, i : i + 1, 0 : value.shape[1]] = value.astype(bf16)
        dst[slab + 1] = w_out[:, cols(0)]
        slab += 2
        for j in range(w_in.shape[1] // D):
            dst[slab] = w_in[:, cols(j * D)]
            slab += 1
        for j in range(w_down.shape[0]):
            dst[slab] = w_down[j, :, cols(0)]
            slab += 1


def combine_body(mine, got, unit1, unit2):
    me = lax.axis_index("c")
    n = unit2.shape[0] // 2
    wide = n // 2
    unit1[6] = jnp.zeros(unit1.shape[1:], bf16)
    for at, src in ((me, mine), (1 - me, got)):
        for j in range(3):
            unit1[2 * j + at] = src[j]
        for j in range(wide + 1):
            unit2[2 * j + at] = src[4 + j]
        for j in range(wide):
            unit2[2 * (wide + 1) + at * wide + j] = src[5 + wide + j]
    unit1[6, :, 0:128] = mine[3, :, 0:128]
    unit1[6, :, 128:256] = got[3, :, 0:128]


def whole_call(body, outs, *args):
    return pl.pallas_call(
        body,
        in_specs=[pl.BlockSpec(memory_space=pltpu.VMEM)] * len(args),
        out_specs=[pl.BlockSpec(memory_space=pltpu.VMEM)] * len(outs),
        out_shape=[shape(o) for o in outs],
        cost_estimate=cost(0, 2 << 20),
    )(*args)


def each_slot(pieces):
    at = 0
    for ref in pieces:
        for slot in range(ref.shape[0]):
            yield at, ref, slot
            at += 1


def wait_for(dst, sem):
    pltpu.make_async_copy(dst, dst, sem).wait()


def proj_body(info, t_own, t_got, bias, *refs):
    pieces, (out, w_out, w, sem) = refs[:-4], refs[-4:]
    i = pl.program_id(0)

    @pl.when(i == 0)
    def _():
        for at, ref, slot in each_slot(pieces):
            rows = pl.ds(pl.multiple_of(info[1 + at] * ROWS, ROWS), ROWS)
            for j in range(3):
                src = ref.at[slot, j * ROWS : (j + 1) * ROWS, :]
                pltpu.make_async_copy(src, w.at[rows, j * HALF : (j + 1) * HALF], sem).start()
        wait_for(w, sem)

    tile = jnp.where(i < pl.num_programs(0) // 2, t_own[...], t_got[...])
    for j in range(3):
        cols = slice(j * HALF, (j + 1) * HALF)
        part = mxu(tile, w[:, cols]) + bias[0:1, cols]
        if j == 0:
            part = part * (LOG2E * HD ** -0.5)
        out[:, cols] = part.astype(bf16)
    w_out[...] = w[...]


def project(info, t_own, t_got, bias, pieces):
    half = t_own.shape[0]
    tile = 512
    n_half = half // tile
    own = pl.BlockSpec((tile, D), lambda i, *_: (jnp.minimum(i, n_half - 1), 0))
    got = pl.BlockSpec((tile, D), lambda i, *_: (jnp.maximum(i - n_half, 0), 0))
    return pl.pallas_call(
        proj_body,
        grid_spec=pltpu.PrefetchScalarGridSpec(
            num_scalar_prefetch=1,
            grid=(2 * n_half,),
            in_specs=[own, got, pl.BlockSpec((1, 3 * HALF), lambda i, *_: (0, 0))] + [anyspec()] * len(pieces),
            out_specs=[
                pl.BlockSpec((tile, 3 * HALF), lambda i, *_: (i, 0)),
                pl.BlockSpec((D, 3 * HALF), lambda i, *_: (0, 0)),
            ],
            scratch_shapes=[pltpu.VMEM((D, 3 * HALF), bf16), pltpu.SemaphoreType.DMA],
        ),
        out_shape=[shape((2 * half, 3 * HALF)), shape((D, 3 * HALF))],
        compiler_params=params(),
        cost_estimate=cost(half * D * D * 6, half * D * 12),
    )(info, t_own, t_got, bias, *pieces)


def norm_stats(rows):
    mean = jnp.mean(rows, axis=-1, keepdims=True)
    centered = rows - mean
    var = jnp.mean(centered * centered, axis=-1, keepdims=True)
    rstd = lax.rsqrt(var + norm_eps)
    return centered * rstd, rstd


def norm_back(grad, unit, rstd, gain):
    eg = grad * gain
    mean_eg = jnp.mean(eg, axis=-1, keepdims=True)
    mean_en = jnp.mean(eg * unit, axis=-1, keepdims=True)
    return (eg - mean_eg - unit * mean_en) * rstd


def mid_body(info, tok, o_own, o_got, back, back_got, vecs, bias_in, *refs):
    n_out = 10
    outs, scratch = refs[-n_out - 5 : -5], refs[-5:]
    pieces = refs[: -n_out - 5]
    own_pieces, far_pieces = pieces[: len(pieces) // 2], pieces[len(pieces) // 2 :]
    out_rows, act_out, ig_out, low_out, branch_out, attn_out, resid_out, d_own, d_far, sums = outs
    w_out, w_in, w_down, slope, sems = scratch
    ff_cols = w_in.shape[1] // D
    me = info[0]

    @pl.when(pl.program_id(0) == 0)
    def _():
        for kind in range(3):
            for here, part in ((me, own_pieces), (1 - me, far_pieces)):
                for at, ref, slot in each_slot(part):
                    chip = info[1 + at]
                    lane0 = pl.multiple_of(here * HALF, HALF)
                    rows = pl.ds(pl.multiple_of(chip * ROWS, ROWS), ROWS)
                    if kind == 0:
                        pltpu.make_async_copy(ref.at[slot, 0:ROWS, :], w_out.at[rows, pl.ds(lane0, HALF)], sems.at[0]).start()
                    elif kind == 1:
                        for j in range(ff_cols):
                            src = ref.at[slot, (1 + j) * ROWS : (2 + j) * ROWS, :]
                            dst = w_in.at[rows, pl.ds(pl.multiple_of(lane0 + j * D, HALF), HALF)]
                            pltpu.make_async_copy(src, dst, sems.at[1]).start()
                    else:
                        size = ROWS * ff_cols
                        src = ref.at[slot, (1 + ff_cols) * ROWS : (1 + 2 * ff_cols) * ROWS, :]
                        dst = w_down.at[pl.ds(pl.multiple_of(chip * size, size), size), pl.ds(lane0, HALF)]
                        pltpu.make_async_copy(src, dst, sems.at[2]).start()
        sums[...] = jnp.zeros_like(sums)
        wait_for(w_out, sems.at[0])

    bias_o, gain1, shift1 = vecs[0:1, :], vecs[1:2, :], vecs[2:3, :]
    bias_d, gain2, shift2 = vecs[3:4, :], vecs[4:5, :], vecs[5:6, :]
    mine = w_out[pl.ds(pl.multiple_of(me * HALF, HALF), HALF), :]
    other = w_out[pl.ds(pl.multiple_of((1 - me) * HALF, HALF), HALF), :]
    resid = tok[...].astype(f32) + mxu(o_own[...], mine) + mxu(o_got[...], other) + bias_o
    unit1, rstd1 = norm_stats(resid)
    hidden = unit1 * gain1 + shift1
    low = hidden.astype(bf16)
    low_out[...] = low

    @pl.when(pl.program_id(0) == 0)
    def _():
        wait_for(w_in, sems.at[1])
        wait_for(w_down, sems.at[2])

    branch = bias_d
    for j in range(ff_cols):
        cols = slice(j * D, (j + 1) * D)
        inner = mxu(low, w_in[:, cols]) + bias_in[:, cols]
        phi = 0.5 + 0.5 * lax.erf(inner * (0.5 ** 0.5))
        act = (inner * phi).astype(bf16)
        act_out[:, cols] = act
        slope[:, cols] = phi + inner * (jnp.exp2(inner * inner * (-0.5 * LOG2E)) * 0.3989422804014327)
        branch = branch + mxu(act, w_down[cols, :])
    unit2, rstd2 = norm_stats(hidden + branch)
    out_rows[...] = (unit2 * gain2 + shift2).astype(bf16)
    grad = jnp.where(info[1 + SLOTS] == 1, back[...], back_got[...]).astype(f32)
    resid2 = norm_back(grad, unit2, rstd2, gain2)
    low_branch = resid2.astype(bf16)
    branch_out[...] = low_branch
    hidden_grad = resid2
    for j in range(ff_cols):
        cols = slice(j * D, (j + 1) * D)
        ig = (mxu(low_branch, w_down[cols, :], NT) * slope[:, cols]).astype(bf16)
        ig_out[:, cols] = ig
        hidden_grad = hidden_grad + mxu(ig, w_in[:, cols], NT)
        sums[3 + j : 4 + j, :] += jnp.sum(ig.astype(f32), axis=0, keepdims=True)
    resid1 = norm_back(hidden_grad, unit1, rstd1, gain1)
    resid_out[...] = resid1
    attn_grad = resid1.astype(bf16)
    attn_out[...] = attn_grad
    d_own[...] = mxu(attn_grad, mine, NT).astype(bf16)
    d_far[...] = mxu(attn_grad, other, NT).astype(bf16)
    rows = (
        (0, attn_grad.astype(f32)),
        (1, hidden_grad * unit1),
        (2, hidden_grad),
        (3 + ff_cols, low_branch.astype(f32)),
        (4 + ff_cols, grad * unit2),
        (5 + ff_cols, grad),
    )
    for at, value in rows:
        sums[at : at + 1, :] += jnp.sum(value, axis=0, keepdims=True)


def middle(info, tok, o_own, o_got, back, back_got, vecs, bias_in, own_pieces, far_pieces):
    half = tok.shape[0]
    ff = bias_in.shape[1]
    wide = pl.BlockSpec((TM, D), lambda i, *_: (i, 0))
    thin = pl.BlockSpec((TM, HALF), lambda i, *_: (i, 0))
    full = pl.BlockSpec((TM, ff), lambda i, *_: (i, 0))
    fixed = lambda rows, cols: pl.BlockSpec((rows, cols), lambda i, *_: (0, 0))
    pieces = tuple(own_pieces) + tuple(far_pieces)
    return pl.pallas_call(
        mid_body,
        grid_spec=pltpu.PrefetchScalarGridSpec(
            num_scalar_prefetch=1,
            grid=(half // TM,),
            in_specs=[wide, thin, thin, wide, wide, fixed(8, D), fixed(1, ff)] + [anyspec()] * len(pieces),
            out_specs=[wide, full, full, wide, wide, wide, wide, thin, thin, fixed(16, D)],
            scratch_shapes=[
                pltpu.VMEM((D, D), bf16),
                pltpu.VMEM((D, ff), bf16),
                pltpu.VMEM((ff, D), bf16),
                pltpu.VMEM((TM, ff), f32),
                pltpu.SemaphoreType.DMA((3,)),
            ],
        ),
        out_shape=[
            shape((half, D)),
            shape((half, ff)),
            shape((half, ff)),
            shape((half, D)),
            shape((half, D)),
            shape((half, D)),
            shape((half, D), f32),
            shape((half, HALF)),
            shape((half, HALF)),
            shape((16, D), f32),
        ],
        compiler_params=params(),
        cost_estimate=cost(half * D * (D + 2 * ff) * 4, half * D * 40),
    )(info, tok, o_own, o_got, back, back_got, vecs, bias_in, *pieces)


def wgrad_body(info, act, ig, low, branch, o_own, o_got, attn_grad, dst, res_in, res_down, res_out, sems):
    j = pl.program_id(0)
    n = pl.num_programs(0)
    me = info[0]
    par = lax.rem(j, 2)
    down_rows = ROWS * n
    per_step = SLOTS // n
    @pl.when(j == 0)
    def _():
        grad = attn_grad[...]
        for here, rows in ((me, o_own), (1 - me, o_got)):
            spot = pl.ds(pl.multiple_of(here * HALF, HALF), HALF)
            res_out[spot, :] = mxu(rows[...], grad, TN).astype(bf16)
        for chip in range(SLOTS):
            src = res_out.at[chip * ROWS : (chip + 1) * ROWS, :]
            pltpu.make_async_copy(src, dst.at[info[1 + chip], 0:ROWS, :], sems.at[2]).start()

    res_in[par] = mxu(low[...], ig[...], TN).astype(bf16)
    for chip in range(SLOTS):
        src = res_in.at[par, chip * ROWS : (chip + 1) * ROWS, :]
        spot = pl.ds(pl.multiple_of((1 + j) * ROWS, ROWS), ROWS)
        pltpu.make_async_copy(src, dst.at[info[1 + chip], spot, :], sems.at[par]).start()
    res_down[par] = mxu(act[...], branch[...], TN).astype(bf16)
    for q in range(per_step):
        src = res_down.at[par, q * down_rows : (q + 1) * down_rows, :]
        slot = info[1 + j * per_step + q]
        pltpu.make_async_copy(src, dst.at[slot, ROWS * (1 + n) : ROWS * (1 + 2 * n), :], sems.at[par]).start()

    def settle(which):
        wait_for(res_in.at[which], sems.at[which])
        wait_for(res_down.at[which], sems.at[which])

    @pl.when(j > 0)
    def _():
        settle(1 - par)

    @pl.when(j == n - 1)
    def _():
        settle(par)
        wait_for(res_out, sems.at[2])


def weight_grads(own, info, act, ig, low, branch, o_own, o_got, attn_grad):
    half, ff = act.shape
    n = ff // D
    strip = pl.BlockSpec((half, D), lambda j, *_: (0, j))
    fixed = lambda cols: pl.BlockSpec((half, cols), lambda j, *_: (0, 0))
    at = (lambda info: info[0]) if own else (lambda info: 1 - info[0])
    lanes_of = pl.BlockSpec((half, HALF), lambda j, info: (0, 2 * j + at(info)))
    side = pl.BlockSpec((half, HALF), lambda j, info: (0, at(info)))
    return pl.pallas_call(
        wgrad_body,
        grid_spec=pltpu.PrefetchScalarGridSpec(
            num_scalar_prefetch=1,
            grid=(n,),
            in_specs=[strip, lanes_of, fixed(D), side, fixed(HALF), fixed(HALF), side],
            out_specs=anyspec(),
            scratch_shapes=[
                pltpu.VMEM((2, D, HALF), bf16),
                pltpu.VMEM((2, D, HALF), bf16),
                pltpu.VMEM((D, HALF), bf16),
                pltpu.SemaphoreType.DMA((3,)),
            ],
        ),
        out_shape=shape((SLOTS, ROWS * (1 + 2 * n), HALF)),
        compiler_params=params(),
        cost_estimate=cost(half * D * (D + 2 * ff), half * ff * 8),
    )(info, act, ig, low, branch, o_own, o_got, attn_grad)


def qkv_grad_body(info, small, t_own, t_got, dq, dk, dv, out, t_all, d_all, res, res_small, sems):
    half = t_own.shape[0]
    pltpu.make_async_copy(t_own, t_all.at[0:half, :], sems.at[0]).start()
    pltpu.make_async_copy(t_got, t_all.at[half:, :], sems.at[0]).start()
    for j, src in enumerate((dq, dk, dv)):
        pltpu.make_async_copy(src, d_all.at[j], sems.at[1 + j]).start()
    wait_for(t_all, sems.at[0])
    res_small[...] = small[...].astype(bf16)
    row = lax.broadcasted_iota(jnp.int32, (16, HALF), 0)
    for j in range(3):
        wait_for(d_all.at[j], sems.at[1 + j])
        grads = d_all[j]
        res[j] = mxu(t_all[...], grads, TN).astype(bf16)
        for chip in range(SLOTS):
            src = res.at[j, chip * ROWS : (chip + 1) * ROWS, :]
            pltpu.make_async_copy(src, out.at[info[1 + chip], j * ROWS : (j + 1) * ROWS, :], sems.at[4]).start()
        if j != 1:
            total = jnp.sum(grads.astype(f32), axis=0, keepdims=True)
            place = 14 if j == 0 else 15
            res_small[...] = jnp.where(row == place, total, res_small[...].astype(f32)).astype(bf16)
    for slot in range(SLOTS):
        pltpu.make_async_copy(res_small, out.at[slot, 3 * ROWS : 3 * ROWS + 16, :], sems.at[5]).start()
    wait_for(res, sems.at[4])
    for slot in range(SLOTS):
        pltpu.make_async_copy(res_small, out.at[slot, 3 * ROWS : 3 * ROWS + 16, :], sems.at[5]).wait()


def qkv_grads(info, small, t_own, t_got, dq, dk, dv):
    total = dq.shape[0]
    return pl.pallas_call(
        qkv_grad_body,
        grid_spec=pltpu.PrefetchScalarGridSpec(
            num_scalar_prefetch=1,
            grid=(),
            in_specs=[pl.BlockSpec(memory_space=pltpu.VMEM)] + [anyspec()] * 5,
            out_specs=anyspec(),
            scratch_shapes=[
                pltpu.VMEM((total, D), bf16),
                pltpu.VMEM((3, total, HALF), bf16),
                pltpu.VMEM((3, D, HALF), bf16),
                pltpu.VMEM((16, HALF), bf16),
                pltpu.SemaphoreType.DMA((6,)),
            ],
        ),
        out_shape=shape((SLOTS, 3 * ROWS + 16, HALF)),
        compiler_params=pltpu.CompilerParams(vmem_limit_bytes=VMEM_CAP),
        cost_estimate=cost(total * D * HALF * 6, total * D * 5),
    )(info, small, t_own, t_got, dq, dk, dv)


def input_back_body(*refs):
    w = refs[0]
    dq, dk, dv = refs[1:4]
    out = refs[-1]
    total = None
    for j, part in enumerate((dq, dk, dv)):
        add = mxu(part[...], w[:, j * HALF : (j + 1) * HALF], NT)
        total = add if total is None else total + add
    for extra in refs[4:-1]:
        total = total + extra[...].astype(f32)
    out[...] = total.astype(bf16)


def input_back(w, dq, dk, dv, far, extras):
    half = dq.shape[0] // 2
    tile = 512
    base = half // tile if far else 0
    part = pl.BlockSpec((tile, HALF), lambda i: (base + i, 0))
    row = pl.BlockSpec((tile, D), lambda i: (i, 0))
    return pl.pallas_call(
        input_back_body,
        grid=(half // tile,),
        in_specs=[pl.BlockSpec((D, 3 * HALF), lambda i: (0, 0)), part, part, part] + [row] * len(extras),
        out_specs=row,
        out_shape=shape((half, D)),
        compiler_params=params(),
        cost_estimate=cost(half * D * HALF * 6, half * D * 8),
    )(w, dq, dk, dv, *extras)


def shift(n, k):
    return [(i, (i + k) % n) for i in range(n)]


class Plan:
    def __init__(self, seq, fsdp):
        rest = fsdp // 2
        dims = []
        while rest > 1:
            want = 4 if len(dims) % 2 == 0 and rest % 4 == 0 else 2
            dims.append(want)
            rest //= want
        self.dims = [seq] + dims + [2]
        self.names = ["s"] + ["r%d" % i for i in range(len(dims))] + ["c"]
        self.chips = seq * fsdp // 2
        self.direct = self.dims == [2, 4, 2, 2]
        self.stages = ([1] if dims else []) + [0] + list(range(2, len(dims) + 1))

    def at(self, a):
        return lax.axis_index(self.names[a])

    def chip_table(self, sign):
        if not self.direct:
            return jnp.arange(SLOTS, dtype=jnp.int32)
        spots = []
        for dx, dy in ((0, 0), (1, 0), (0, 1), (1, 1)):
            spots += [(dx, dy, z) for z in range(4)]
        dx, dy, dz = (jnp.asarray(v, jnp.int32) for v in zip(*spots))
        return ((self.at(0) + sign * dx) % 2) * 8 + ((self.at(1) + sign * dz) % 4) * 2 + (self.at(2) + sign * dy) % 2

    def slot_table(self, sign):
        table = self.chip_table(sign)
        hit = table[:, None] == jnp.arange(SLOTS, dtype=jnp.int32)[None, :]
        return jnp.sum(jnp.where(hit, jnp.arange(SLOTS, dtype=jnp.int32)[:, None], 0), axis=0)

    def places(self, sign):
        grid = np.indices(self.dims[:-1]).reshape(len(self.dims) - 1, -1)
        flat = jnp.zeros((self.chips,), jnp.int32)
        if sign < 0:
            for a in reversed(self.stages):
                n = self.dims[a]
                flat = flat * n + (self.at(a) - jnp.asarray(grid[a], jnp.int32)) % n
            return flat
        sizes = [self.dims[a] for a in reversed(self.stages)]
        offs = np.indices(sizes).reshape(len(sizes), -1)
        by_axis = {a: offs[j] for j, a in enumerate(reversed(self.stages))}
        for a in range(len(self.dims) - 1):
            n = self.dims[a]
            flat = flat * n + (self.at(a) + jnp.asarray(by_axis[a], jnp.int32)) % n
        return flat

    def send(self, x, a, k=1):
        return lax.ppermute(x, self.names[a], shift(self.dims[a], k))


def gather_chips(plan, unit):
    buf = unit[None]
    for a in plan.stages:
        n = plan.dims[a]
        if n > 1:
            buf = jnp.concatenate([buf] + [plan.send(buf, a, k) for k in range(1, n)], axis=0)
    return jnp.take(buf, plan.places(-1), axis=0, mode="clip")


def reduce_chips(plan, grads):
    buf = jnp.take(grads, plan.places(1), axis=0, mode="clip")
    for a in reversed(plan.stages):
        n = plan.dims[a]
        size = buf.shape[0] // n
        keep = buf[:size].astype(f32)
        for k in range(1, n):
            keep = keep + plan.send(buf[k * size : (k + 1) * size].astype(bf16), a, k).astype(f32)
        buf = keep if a == plan.stages[0] else keep.astype(bf16)
    return buf[0]


def regroup(buf, sizes, count):
    n, _, w = buf.shape
    parts = []
    at = 0
    for size in sizes:
        parts.append(buf[:, at : at + size].reshape(count, n * size // count, w))
        at += size
    return jnp.concatenate(parts, axis=1)


def gather_z(plan, unit):
    return jnp.concatenate([unit[None]] + [plan.send(unit, 1, k)[None] for k in range(1, 4)], axis=0)


def swap_pair(x):
    return lax.ppermute(x, "c", [(0, 1), (1, 0)])


def cross(x):
    return lax.ppermute(x, ("s", "c"), [(1, 2), (2, 1)])


def together(*values):
    return lax.optimization_barrier(values)


def half_of(x, at):
    return lax.dynamic_slice_in_dim(x, at * HALF, HALF, axis=x.ndim - 1)


def chip_units(me, mine, got, sizes):
    low = jnp.where(me == 0, mine, got)
    high = jnp.where(me == 0, got, mine)
    parts = []
    at = 0
    for size in sizes:
        parts += [low[at : at + size], high[at : at + size]]
        at += size
    return jnp.concatenate(parts, axis=0)


def own_rows(me, total, sizes):
    first, second = [], []
    at = 0
    for size in sizes:
        first.append(total[at : at + size])
        second.append(total[at + size : at + 2 * size])
        at += 2 * size
    first = jnp.concatenate(first, axis=0)
    second = jnp.concatenate(second, axis=0)
    return jnp.where(me == 0, first, second), jnp.where(me == 0, second, first)


def local(plan, tokens, lengths, block_order, qkv_weight, query_bias, value_bias, out_weight, out_bias,
          norm1_gain, norm1_shift, in_weight, in_bias, down_weight, down_bias, norm2_gain, norm2_shift, cotangent):
    half = tokens.shape[1]
    me = plan.at(len(plan.dims) - 1)
    stays = plan.at(0) == me
    rows_dev = qkv_weight.shape[0]
    ff_dev = down_weight.shape[0]
    ff_cols = in_weight.shape[1] // D
    me32 = me.astype(jnp.int32)
    pull = jnp.concatenate([me32[None], plan.chip_table(-1), stays.astype(jnp.int32)[None]])
    push = jnp.concatenate([me32[None], plan.slot_table(1)])
    sizes1 = [rows_dev] * 3
    sizes2 = [rows_dev] * (1 + ff_cols) + [ff_dev]
    smalls = (query_bias, value_bias, out_bias, norm1_gain, norm1_shift, in_bias, down_bias, norm2_gain, norm2_shift)
    unit_rows = 2 * half // UNITS

    def stacked(vectors):
        bias_o, gain1, shift1, wide, bias_d, gain2, shift2 = vectors[2:]
        zero = jnp.zeros((D,), f32)
        return jnp.stack([bias_o, gain1, shift1, bias_d, gain2, shift2, zero, zero]), wide[None]

    def settle_rows(x, got):
        return jnp.where(stays, x, got)

    tok = settle_rows(tokens[0], cross(tokens[0]))
    tok_got = swap_pair(tok)
    if plan.direct:
        lines = [v[None] for v in smalls] + [lengths, block_order]
        slab = (5 + 2 * ff_cols, rows_dev, HALF)
        mine, give = whole_call(pack_body, (slab, slab), qkv_weight, out_weight, in_weight,
                                down_weight.reshape(ff_cols, rows_dev, D), *lines)
        got = swap_pair(give)
        unit1, unit2 = whole_call(combine_body, ((7, rows_dev, HALF), (2 + 4 * ff_cols, rows_dev, HALF)), mine, got)
        unit1 = unit1.reshape(7 * rows_dev, HALF)
        unit2 = unit2.reshape(-1, HALF)
        other = got[3, len(smalls) : len(smalls) + 2, :UNITS].astype(jnp.int32)
        counts_here = jnp.where(stays, lengths[0], other[0]) // unit_rows
        order_here = jnp.where(stays, block_order[0], other[1])

        z1 = gather_z(plan, unit1)
        unit2, z1 = together(unit2, z1)
        x1, y1 = plan.send(z1, 0), plan.send(z1, 2)
        z2_parts = [unit2] + [plan.send(unit2, 1, k) for k in range(1, 4)]
        cot, x1, y1, tok = together(cotangent[0], x1, y1, tok)
        d1a, d1b = plan.send(y1[0:2], 0), plan.send(x1[2:4], 2)
        cot_got = cross(cot)
        pieces1 = [z1, x1, y1, d1a, d1b]
        tail_rows = [p[:, 6 * rows_dev : 6 * rows_dev + 16, 0:256] for p in pieces1]
        table = jnp.take(jnp.concatenate(tail_rows, axis=0), plan.slot_table(-1), axis=0, mode="clip")
        table = table.reshape(plan.chips, 16, 2, 128)
        table = jnp.where(me == 0, table, table[:, :, ::-1])

        def vectors_of(table):
            return [table[:, i, :, : v.shape[0]].reshape(-1).astype(f32) for i, v in enumerate(smalls)]

        vectors = vectors_of(table)
    else:
        first = jnp.concatenate([qkv_weight[:, j * D : (j + 1) * D] for j in range(3)], axis=0)
        second = jnp.concatenate([out_weight] + [in_weight[:, j * D : (j + 1) * D] for j in range(ff_cols)] + [down_weight], axis=0)
        line = jnp.concatenate(smalls)
        both = jnp.concatenate([first, second], axis=0)
        got = swap_pair(half_of(both, 1 - me))
        mine = half_of(both, me)
        cut = 3 * rows_dev
        unit1 = chip_units(me, mine[:cut], got[:cut], sizes1)
        unit2 = chip_units(me, mine[cut:], got[cut:], sizes2)
        line_got = swap_pair(line)
        line_unit = jnp.stack([jnp.where(me == 0, line, line_got), jnp.where(me == 0, line_got, line)])
        pieces1 = [regroup(gather_chips(plan, unit1), [2 * r for r in sizes1], SLOTS)]
        pieces2 = [regroup(gather_chips(plan, unit2), [2 * r for r in sizes2], SLOTS)]
        far2 = [swap_pair(p) for p in pieces2]
        lines = gather_chips(plan, line_unit).reshape(2 * plan.chips, line.shape[0])
        vectors = []
        at = 0
        for piece in smalls:
            size = piece.shape[0]
            vectors.append(lines[:, at : at + size].reshape(2 * plan.chips * size).astype(f32))
            at += size
        counts_here = jnp.where(stays, lengths[0], swap_pair(lengths[0])) // unit_rows
        order_here = jnp.where(stays, block_order[0], swap_pair(block_order[0]))
        cot_got = cross(cotangent[0])
    bias_q, bias_v = vectors[:2]
    bias_qkv = jnp.concatenate([half_of(bias_q, me), jnp.zeros((HALF,), f32), half_of(bias_v, me)])[None]

    spot = jnp.arange(UNITS)
    ends = jnp.sum(jnp.where(spot[None, :] <= spot[:, None], counts_here[None, :], 0), axis=1)
    seg_packed = jnp.sum((spot[:, None] >= ends[None, :]).astype(jnp.int32), axis=1)
    hit = order_here[:, None] == spot[None, :]
    segs = jnp.sum(jnp.where(hit, seg_packed[:, None], 0), axis=0)
    segs = jnp.where(me == 0, segs, jnp.roll(segs, UNITS // 2))

    qkv, w_qkv = project(pull, tok, tok_got, bias_qkv, pieces1)
    if plan.direct:
        *z2_parts, table, qkv = together(*z2_parts, table, qkv)
        vectors = vectors_of(table)
        z2 = jnp.stack(z2_parts)
        x2, y2 = plan.send(z2, 0), plan.send(z2, 2)
        z2_far = swap_pair(z2)
        att = attention(segs, qkv, 0, 2, None)
        vecs, gate_bias = stacked(vectors)
        x2, y2, cot_got, vecs, gate_bias, push, *att = together(x2, y2, cot_got, vecs, gate_bias, push, *att)
        d2a, d2b = plan.send(y2[0:2], 0), plan.send(x2[2:4], 2)
        x2_far, y2_far = swap_pair(x2), swap_pair(y2)
    else:
        att = attention(segs, qkv, 0, 2, None)
        vecs, gate_bias = stacked(vectors)
    o_own, o_far, lse = attention(segs, qkv, 2, PAIRS - 2, att)
    o_got = swap_pair(o_far)
    if plan.direct:
        pieces2 = [z2, x2, y2, d2a, d2b]
        far2 = [z2_far, x2_far, y2_far, swap_pair(d2a), swap_pair(d2b)]
    (out_rows, act, ig, low, branch, attn_grad, resid1, d_own, d_far, sums) = middle(
        pull, tok, o_own, o_got, cotangent[0], cot_got, vecs, gate_bias, pieces2, far2)
    d_got = swap_pair(d_far)
    out_got = cross(out_rows)
    sum_got = swap_pair(half_of(sums, 1 - me))
    grad_args = (low, branch, o_own, o_got)
    give = weight_grads(False, push, act, ig, *grad_args, attn_grad)
    give, attn_grad = together(give, attn_grad)
    got_g = swap_pair(give)
    keep = weight_grads(True, push, act, ig, *grad_args, attn_grad)
    back_args = (o_own, o_far, d_own, d_got, lse)
    if plan.direct:

        def both_sums(lo, hi):
            return keep[lo:hi].astype(f32) + got_g[lo:hi].astype(f32)

        def late(rows):
            return jnp.pad(rows.astype(f32), ((2, 0), (0, 0), (0, 0)))

        def early(rows):
            return jnp.pad(rows.astype(f32), ((0, 2), (0, 0), (0, 0)))

        sx, sy, qkv_back, out_got = together(both_sums(12, 14).astype(bf16), both_sums(14, 16).astype(bf16), qkv, out_got)
        rx, ry = plan.send(sx, 0), plan.send(sy, 2)
        g = attention_back(segs, qkv_back, *back_args, 0, 1, None)
        rx, ry, sum_got, *g = together(rx, ry, sum_got, *g)
        send_x = (both_sums(4, 8) + late(ry)).astype(bf16)
        send_y = (both_sums(8, 12) + early(rx)).astype(bf16)
        send_x, send_y, *g = together(send_x, send_y, *g)
        px, py = plan.send(send_x, 0), plan.send(send_y, 2)
        g = attention_back(segs, qkv_back, *back_args, 1, 1, g)
        px, py, *g = together(px, py, *g)
        z_sum = both_sums(0, 4) + px.astype(f32) + py.astype(f32)
        z_low, ffn, *g = together(z_sum[1:].astype(bf16), z_sum[0], *g)
        z_got = [plan.send(z_low[k - 1], 1, k) for k in range(1, 4)]
        g = attention_back(segs, qkv_back, *back_args, 2, PAIRS - 2, g)
        *z_got, dq, dk, dv = together(*z_got, *g)
        for part in z_got:
            ffn = ffn + part.astype(f32)
    else:
        dq, dk, dv = attention_back(segs, qkv, *back_args, 0, PAIRS, None)
        summed = (keep.astype(f32) + got_g.astype(f32)).astype(bf16)
        scale = plan.chips // SLOTS
        units = regroup_back(summed, [ROWS] * (1 + ff_cols) + [ROWS * ff_cols], scale)
        ffn = reduce_chips(plan, units)
    small = half_of(sums, me) + sum_got
    tail = qkv_grads(push, small, tok, tok_got, dq, dk, dv)
    if plan.direct:
        rx, ry = plan.send(tail[12:14], 0), plan.send(tail[14:16], 2)
        far_back = input_back(w_qkv, dq, dk, dv, True, ())
        rx, ry, far_back = together(rx, ry, far_back)
        far_back = swap_pair(far_back)
        send_x = (tail[4:8].astype(f32) + late(ry)).astype(bf16)
        send_y = (tail[8:12].astype(f32) + early(rx)).astype(bf16)
        px, py = plan.send(send_x, 0), plan.send(send_y, 2)
        packed = input_back(w_qkv, dq, dk, dv, False, (resid1, far_back))
        px, py, packed = together(px, py, packed)
        packed_got = cross(packed)
        z_sum = tail[0:4].astype(f32) + px.astype(f32) + py.astype(f32)
        z_low, out_got = together(z_sum[1:].astype(bf16), out_got)
        qkv_sum = z_sum[0]
        output = settle_rows(out_rows, out_got)
        packed_got, output, *z_got = together(packed_got, output, *[plan.send(z_low[k - 1], 1, k) for k in range(1, 4)])
        for part in z_got:
            qkv_sum = qkv_sum + part.astype(f32)
    else:
        far_back = swap_pair(input_back(w_qkv, dq, dk, dv, True, ()))
        packed = input_back(w_qkv, dq, dk, dv, False, (resid1, far_back))
        packed_got = cross(packed)
        output = settle_rows(out_rows, out_got)
        units = regroup_back(tail[:, : 3 * ROWS], [ROWS] * 3, scale)
        extra = jnp.broadcast_to(tail[0:1, 3 * ROWS :], (plan.chips, 16, HALF))
        qkv_sum = reduce_chips(plan, jnp.concatenate([units, extra], axis=1))
    input_grad = settle_rows(packed, packed_got)

    small_sum = qkv_sum[6 * rows_dev :]
    sizes = sizes1 + sizes2
    total = jnp.concatenate([qkv_sum[: 6 * rows_dev], ffn], axis=0)
    mine, other = own_rows(me, total, sizes)
    got = swap_pair(jnp.concatenate([other, small_sum], axis=0))
    count = mine.shape[0]
    mine = jnp.concatenate([mine, small_sum], axis=0)
    full = jnp.concatenate([jnp.where(me == 0, mine, got), jnp.where(me == 0, got, mine)], axis=1)
    take = lambda at, size: full[at : at + size]
    out_qkv = jnp.concatenate([take(j * rows_dev, rows_dev) for j in range(3)], axis=1)
    out_out = take(3 * rows_dev, rows_dev)
    out_in = jnp.concatenate([take((4 + j) * rows_dev, rows_dev) for j in range(ff_cols)], axis=1)
    out_down = take((4 + ff_cols) * rows_dev, ff_dev)
    small_full = full[count:]
    device = plan.at(0)
    for a in range(1, len(plan.dims)):
        device = device * plan.dims[a] + plan.at(a)
    order = (14, 15, 0, 1, 2, 3, 3 + ff_cols, 4 + ff_cols, 5 + ff_cols)
    wide_row = 3
    thin = lax.dynamic_slice_in_dim(small_full, device * rows_dev, rows_dev, axis=1)
    span = small_full[wide_row : wide_row + ff_cols].reshape(-1)
    s = [lax.dynamic_slice_in_dim(span, device * ff_dev, ff_dev) if row == wide_row and piece is in_bias else thin[row]
         for piece, row in zip(smalls, order)]
    return (output[None], input_grad[None], out_qkv, s[0], s[1], out_out, s[2], s[3], s[4], out_in, s[5], out_down, s[6], s[7], s[8])


def regroup_back(buf, sizes, scale):
    n, _, w = buf.shape
    parts = []
    at = 0
    for size in sizes:
        parts.append(buf[:, at : at + size].reshape(n * scale, size // scale, w))
        at += size
    return jnp.concatenate(parts, axis=1)


def solution(mesh):
    plan = Plan(mesh.shape["seq"], mesh.shape["fsdp"])
    inner_mesh = Mesh(mesh.devices.reshape(plan.dims), tuple(plan.names))
    groups = tuple(plan.names[1:])
    every = tuple(plan.names)
    rows = P(groups, "s", None)
    table = P(groups, None)
    mat = P(every, None)
    vec = P(every)
    placed = (rows, table, table, mat, vec, vec, mat, vec, vec, vec, mat, vec, mat, vec, vec, vec, rows)
    outs = (rows, rows, mat, vec, vec, mat, vec, vec, vec, mat, vec, mat, vec, vec, vec)

    def run(*args):
        return local(plan, *args)

    return jax.shard_map(run, mesh=inner_mesh, in_specs=placed, out_specs=outs, check_vma=False)
```

```python
import jax
import jax.numpy as jnp
import numpy as np
from jax import lax
from jax.sharding import Mesh, PartitionSpec as P
from jax.experimental import pallas as pl
from jax.experimental.pallas import tpu as pltpu

D = 768
HALF = D // 2
HD = 64
UNITS = 16
SLOTS = 16
ROWS = D // SLOTS
PAIRS = HALF // 128
LOG2E = 1.4426950408889634
LN2 = 0.6931471805599453
BIG = 1e30
TQ = 1024
TQ_BACK = 512
STEP = 256
STEP_BACK = 1024
TM = 256
norm_eps = 1e-12
bf16 = jnp.bfloat16
f32 = jnp.float32
NT = (((1,), (1,)), ((), ()))
NN = (((1,), (0,)), ((), ()))
TN = (((0,), (0,)), ((), ()))
VMEM_CAP = 58 << 20


def mxu(a, b, dims=NN):
    return lax.dot_general(a, b, dims, preferred_element_type=f32)


def shape(size, kind=bf16):
    return jax.ShapeDtypeStruct(size, kind)


def params(axes=1):
    return pltpu.CompilerParams(dimension_semantics=("arbitrary",) * axes, vmem_limit_bytes=VMEM_CAP)


def cost(flops, moved):
    return pl.CostEstimate(flops=int(flops), bytes_accessed=int(moved), transcendentals=0)


def tie(value, *others):
    return lax.optimization_barrier((value,) + others)[0]


def lanes(rows):
    return lax.broadcasted_iota(jnp.int32, (rows, 128), 1)


def seg_rows(segs_ref, base_block, rows):
    place = lax.broadcasted_iota(jnp.int32, (rows, 128), 0)
    out = jnp.zeros((rows, 128), jnp.int32)
    for b in range(rows // 128):
        out = jnp.where(place >= b * 128, segs_ref[base_block + b], out)
    return out


def split3(v):
    hi = v.astype(bf16).astype(f32)
    mid = (v - hi).astype(bf16).astype(f32)
    return hi, mid, v - hi - mid


def both_heads(pair_rows):
    lane = lanes(pair_rows.shape[0])
    zero = jnp.zeros_like(pair_rows)
    first = jnp.where(lane < HD, pair_rows, zero)
    return jnp.concatenate([first, jnp.where(lane < HD, zero, pair_rows)], axis=0)


def fill_keys(segs_ref, k_in, v_in, k_aug, v_aug):
    for at in range(0, k_in.shape[0], STEP):
        rows = slice(at, at + STEP)
        lane = lanes(STEP)
        hot = (lane == seg_rows(segs_ref, at // 128, STEP)) | ((lane >= 64) & (lane < 67))
        k_aug[rows, :128] = k_in[rows, :]
        k_aug[rows, 128:] = jnp.where(hot, 1.0, 0.0).astype(bf16)
        v_aug[rows, :128] = v_in[rows, :]
        v_aug[rows, 128:] = jnp.ones((STEP, 128), bf16)


def attend_body(segs_ref, q_in, k_in, v_in, *refs):
    o_own, o_far, lse_ref, k_aug, v_aug = refs[-5:]
    i = pl.program_id(1)
    n_half = pl.num_programs(1) // 2

    @pl.when(i == 0)
    def _():
        fill_keys(segs_ref, k_in, v_in, k_aug, v_aug)

    lane = lanes(TQ)
    seg = seg_rows(segs_ref, i * (TQ // 128), TQ)
    off = jnp.where((lane < 16) & (lane != seg), -BIG, 0.0).astype(bf16)
    q_aug = jnp.concatenate([both_heads(q_in[...]), jnp.concatenate([off, off], axis=0)], axis=1)
    top = None
    acc = None
    for at in range(0, k_aug.shape[0], STEP):
        s = mxu(q_aug, k_aug[at : at + STEP, :], NT)
        here = jnp.max(s, axis=1, keepdims=True)
        new_top = here if top is None else jnp.maximum(top, here)
        p = jnp.exp2(s - new_top).astype(bf16)
        add = mxu(p, v_aug[at : at + STEP, :])
        acc = add if acc is None else acc * jnp.exp2(top - new_top) + add
        top = new_top
    both = jnp.where(lane < HD, acc[:TQ, :128], acc[TQ:, :128])
    sums = jnp.where(lane < HD, acc[:TQ, 128:], acc[TQ:, 128:])
    tops = jnp.where(lane < HD, top[:TQ], top[TQ:])
    out = (both / sums).astype(bf16)
    lse_ref[...] = tops + jnp.log2(sums)

    @pl.when(i < n_half)
    def _():
        o_own[...] = out

    @pl.when(i >= n_half)
    def _():
        o_far[...] = out


def anyspec():
    return pl.BlockSpec(memory_space=pl.ANY)


def pair_specs(n_half, first, rows):
    own = pl.BlockSpec((rows, 128), lambda h, i, *_: (jnp.minimum(i, n_half - 1), first + h))
    far = pl.BlockSpec((rows, 128), lambda h, i, *_: (jnp.maximum(i - n_half, 0), first + h))
    return own, far


def attention(segs, qkv, first, count, prev):
    total = qkv.shape[0]
    half = total // 2
    n_half = half // TQ
    own, far = pair_specs(n_half, first, TQ)
    row = pl.BlockSpec((TQ, 128), lambda h, i, *_: (i, first + h))
    whole = lambda part: pl.BlockSpec((total, 128), lambda h, i, *_: (0, part * PAIRS + first + h))
    prev = () if prev is None else tuple(prev)
    return pl.pallas_call(
        attend_body,
        grid_spec=pltpu.PrefetchScalarGridSpec(
            num_scalar_prefetch=1,
            grid=(count, 2 * n_half),
            in_specs=[row, whole(1), whole(2)] + [anyspec()] * len(prev),
            out_specs=[own, far, row],
            scratch_shapes=[pltpu.VMEM((total, 256), bf16), pltpu.VMEM((total, 256), bf16)],
        ),
        out_shape=[shape((half, HALF)), shape((half, HALF)), shape((total, HALF), f32)],
        input_output_aliases={4 + j: j for j in range(len(prev))},
        compiler_params=params(2),
        cost_estimate=cost(count * total * total * 2048, total * 128 * 2 * 8),
    )(segs, qkv, qkv, qkv, *prev)


def attend_back_body(segs_ref, q_in, k_in, v_in, o_own, o_far, d_own, d_far, lse_ref, *refs):
    dq_out, dk_out, dv_out, k_aug, v_aug, dk_acc, dv_acc, k_turn = refs[-8:]
    i = pl.program_id(1)
    n = pl.num_programs(1)

    @pl.when(i == 0)
    def _():
        fill_keys(segs_ref, k_in, v_in, k_aug, v_aug)
        k_turn[...] = k_in[...].T
        dk_acc[...] = jnp.zeros_like(dk_acc)
        dv_acc[...] = jnp.zeros_like(dv_acc)

    near = i < n // 2
    d_rows = jnp.where(near, d_own[...], d_far[...])
    o_rows = jnp.where(near, o_own[...], o_far[...])
    lane = lanes(TQ_BACK)
    seg = seg_rows(segs_ref, i * (TQ_BACK // 128), TQ_BACK)
    off = jnp.where((lane < 16) & (lane != seg), -BIG, 0.0)
    prod = d_rows.astype(f32) * o_rows.astype(f32)
    q_side, d_side = [], []
    for head in range(2):
        mine = (lane < HD) if head == 0 else (lane >= HD)
        dot_row = jnp.sum(jnp.where(mine, prod, 0.0), axis=1, keepdims=True)
        lse = jnp.broadcast_to(lse_ref[:, head * HD : head * HD + 1], (TQ_BACK, 128))
        for side, value, rest in ((q_side, -lse, off), (d_side, -jnp.broadcast_to(dot_row, (TQ_BACK, 128)), 0.0)):
            h, m, l = split3(value)
            cols = jnp.where(lane == 64, h, jnp.where(lane == 65, m, jnp.where(lane == 66, l, rest)))
            side.append(cols.astype(bf16))
    q2 = both_heads(q_in[...])
    d2 = both_heads(d_rows)
    q_aug = jnp.concatenate([q2, jnp.concatenate(q_side, axis=0)], axis=1)
    d_aug = jnp.concatenate([d2, jnp.concatenate(d_side, axis=0)], axis=1)
    dq = None
    for at in range(0, k_aug.shape[0], STEP_BACK):
        rows = slice(at, at + STEP_BACK)
        p = jnp.exp2(mxu(k_aug[rows, :], q_aug, NT))
        ds = (p * mxu(v_aug[rows, :], d_aug, NT)).astype(bf16)
        dv_acc[rows, :] += mxu(p.astype(bf16), d2)
        dk_acc[rows, :] += mxu(ds, q2)
        add = mxu(k_turn[:, rows], ds)
        dq = add if dq is None else dq + add
    dq = jnp.concatenate([dq[:HD, :TQ_BACK], dq[HD:, TQ_BACK:]], axis=0) * (HD ** -0.5)
    dq_out[...] = dq.T.astype(bf16)

    @pl.when(i == n - 1)
    def _():
        dk_out[...] = (dk_acc[...] * LN2).astype(bf16)
        dv_out[...] = dv_acc[...].astype(bf16)


def attention_back(segs, qkv, o_own, o_far, d_own, d_far, lse, first, count, prev):
    total = qkv.shape[0]
    half = total // 2
    n_half = half // TQ_BACK
    own, far = pair_specs(n_half, first, TQ_BACK)
    row = pl.BlockSpec((TQ_BACK, 128), lambda h, i, *_: (i, first + h))
    whole = lambda part: pl.BlockSpec((total, 128), lambda h, i, *_: (0, part * PAIRS + first + h))
    prev = () if prev is None else tuple(prev)
    return pl.pallas_call(
        attend_back_body,
        grid_spec=pltpu.PrefetchScalarGridSpec(
            num_scalar_prefetch=1,
            grid=(count, 2 * n_half),
            in_specs=[row, whole(1), whole(2), own, far, own, far, row] + [anyspec()] * len(prev),
            out_specs=[row, whole(0), whole(0)],
            scratch_shapes=[
                pltpu.VMEM((total, 256), bf16),
                pltpu.VMEM((total, 256), bf16),
                pltpu.VMEM((total, 128), f32),
                pltpu.VMEM((total, 128), f32),
                pltpu.VMEM((128, total), bf16),
            ],
        ),
        out_shape=[shape((total, HALF))] * 3,
        input_output_aliases={9 + j: j for j in range(len(prev))},
        compiler_params=params(2),
        cost_estimate=cost(count * total * total * 5120, total * 128 * 2 * 12),
    )(segs, qkv, qkv, qkv, o_own, o_far, d_own, d_far, lse, *prev)


def pack_body(qkv, w_out, w_in, w_down, *refs):
    lines, (mine, give) = refs[:-2], refs[-2:]
    me = lax.axis_index("c")
    for half_at, dst in ((me, mine), (1 - me, give)):
        slab = 0

        def cols(base):
            return pl.ds(pl.multiple_of(base + half_at * HALF, 128), HALF)

        for j in range(3):
            dst[slab] = qkv[:, cols(j * D)]
            slab += 1
        dst[slab] = jnp.zeros(dst.shape[1:], bf16)
        for i, line in enumerate(lines):
            value = line[...].astype(f32)
            dst[slab, i : i + 1, 0 : value.shape[1]] = value.astype(bf16)
        dst[slab + 1] = w_out[:, cols(0)]
        slab += 2
        for j in range(w_in.shape[1] // D):
            dst[slab] = w_in[:, cols(j * D)]
            slab += 1
        for j in range(w_down.shape[0]):
            dst[slab] = w_down[j, :, cols(0)]
            slab += 1


def combine_body(mine, got, unit1, unit2):
    me = lax.axis_index("c")
    n = unit2.shape[0] // 2
    wide = n // 2
    unit1[6] = jnp.zeros(unit1.shape[1:], bf16)
    for at, src in ((me, mine), (1 - me, got)):
        for j in range(3):
            unit1[2 * j + at] = src[j]
        for j in range(wide + 1):
            unit2[2 * j + at] = src[4 + j]
        for j in range(wide):
            unit2[2 * (wide + 1) + at * wide + j] = src[5 + wide + j]
    unit1[6, :, 0:128] = mine[3, :, 0:128]
    unit1[6, :, 128:256] = got[3, :, 0:128]


def whole_call(body, outs, *args):
    return pl.pallas_call(
        body,
        in_specs=[pl.BlockSpec(memory_space=pltpu.VMEM)] * len(args),
        out_specs=[pl.BlockSpec(memory_space=pltpu.VMEM)] * len(outs),
        out_shape=[shape(o) for o in outs],
        cost_estimate=cost(0, 2 << 20),
    )(*args)


def each_slot(pieces):
    at = 0
    for ref in pieces:
        for slot in range(ref.shape[0]):
            yield at, ref, slot
            at += 1


def wait_for(dst, sem):
    pltpu.make_async_copy(dst, dst, sem).wait()


def proj_body(info, t_own, t_got, bias, *refs):
    pieces, (out, w_out, w, sem) = refs[:-4], refs[-4:]
    i = pl.program_id(0)

    @pl.when(i == 0)
    def _():
        for at, ref, slot in each_slot(pieces):
            rows = pl.ds(pl.multiple_of(info[1 + at] * ROWS, ROWS), ROWS)
            for j in range(3):
                src = ref.at[slot, j * ROWS : (j + 1) * ROWS, :]
                pltpu.make_async_copy(src, w.at[rows, j * HALF : (j + 1) * HALF], sem).start()
        wait_for(w, sem)

    tile = jnp.where(i < pl.num_programs(0) // 2, t_own[...], t_got[...])
    for j in range(3):
        cols = slice(j * HALF, (j + 1) * HALF)
        part = mxu(tile, w[:, cols]) + bias[0:1, cols]
        if j == 0:
            part = part * (LOG2E * HD ** -0.5)
        out[:, cols] = part.astype(bf16)
    w_out[...] = w[...]


def project(info, t_own, t_got, bias, pieces):
    half = t_own.shape[0]
    tile = 512
    n_half = half // tile
    own = pl.BlockSpec((tile, D), lambda i, *_: (jnp.minimum(i, n_half - 1), 0))
    got = pl.BlockSpec((tile, D), lambda i, *_: (jnp.maximum(i - n_half, 0), 0))
    return pl.pallas_call(
        proj_body,
        grid_spec=pltpu.PrefetchScalarGridSpec(
            num_scalar_prefetch=1,
            grid=(2 * n_half,),
            in_specs=[own, got, pl.BlockSpec((1, 3 * HALF), lambda i, *_: (0, 0))] + [anyspec()] * len(pieces),
            out_specs=[
                pl.BlockSpec((tile, 3 * HALF), lambda i, *_: (i, 0)),
                pl.BlockSpec((D, 3 * HALF), lambda i, *_: (0, 0)),
            ],
            scratch_shapes=[pltpu.VMEM((D, 3 * HALF), bf16), pltpu.SemaphoreType.DMA],
        ),
        out_shape=[shape((2 * half, 3 * HALF)), shape((D, 3 * HALF))],
        compiler_params=params(),
        cost_estimate=cost(half * D * D * 6, half * D * 12),
    )(info, t_own, t_got, bias, *pieces)


def norm_stats(rows):
    mean = jnp.mean(rows, axis=-1, keepdims=True)
    centered = rows - mean
    var = jnp.mean(centered * centered, axis=-1, keepdims=True)
    rstd = lax.rsqrt(var + norm_eps)
    return centered * rstd, rstd


def norm_back(grad, unit, rstd, gain):
    eg = grad * gain
    mean_eg = jnp.mean(eg, axis=-1, keepdims=True)
    mean_en = jnp.mean(eg * unit, axis=-1, keepdims=True)
    return (eg - mean_eg - unit * mean_en) * rstd


def mid_body(info, tok, o_own, o_got, back, back_got, vecs, bias_in, *refs):
    n_out = 10
    outs, scratch = refs[-n_out - 5 : -5], refs[-5:]
    pieces = refs[: -n_out - 5]
    own_pieces, far_pieces = pieces[: len(pieces) // 2], pieces[len(pieces) // 2 :]
    out_rows, act_out, ig_out, low_out, branch_out, attn_out, resid_out, d_own, d_far, sums = outs
    w_out, w_in, w_down, slope, sems = scratch
    ff_cols = w_in.shape[1] // D
    me = info[0]

    @pl.when(pl.program_id(0) == 0)
    def _():
        for kind in range(3):
            for here, part in ((me, own_pieces), (1 - me, far_pieces)):
                for at, ref, slot in each_slot(part):
                    chip = info[1 + at]
                    lane0 = pl.multiple_of(here * HALF, HALF)
                    rows = pl.ds(pl.multiple_of(chip * ROWS, ROWS), ROWS)
                    if kind == 0:
                        pltpu.make_async_copy(ref.at[slot, 0:ROWS, :], w_out.at[rows, pl.ds(lane0, HALF)], sems.at[0]).start()
                    elif kind == 1:
                        for j in range(ff_cols):
                            src = ref.at[slot, (1 + j) * ROWS : (2 + j) * ROWS, :]
                            dst = w_in.at[rows, pl.ds(pl.multiple_of(lane0 + j * D, HALF), HALF)]
                            pltpu.make_async_copy(src, dst, sems.at[1]).start()
                    else:
                        size = ROWS * ff_cols
                        src = ref.at[slot, (1 + ff_cols) * ROWS : (1 + 2 * ff_cols) * ROWS, :]
                        dst = w_down.at[pl.ds(pl.multiple_of(chip * size, size), size), pl.ds(lane0, HALF)]
                        pltpu.make_async_copy(src, dst, sems.at[2]).start()
        sums[...] = jnp.zeros_like(sums)
        wait_for(w_out, sems.at[0])

    bias_o, gain1, shift1 = vecs[0:1, :], vecs[1:2, :], vecs[2:3, :]
    bias_d, gain2, shift2 = vecs[3:4, :], vecs[4:5, :], vecs[5:6, :]
    mine = w_out[pl.ds(pl.multiple_of(me * HALF, HALF), HALF), :]
    other = w_out[pl.ds(pl.multiple_of((1 - me) * HALF, HALF), HALF), :]
    resid = tok[...].astype(f32) + mxu(o_own[...], mine) + mxu(o_got[...], other) + bias_o
    unit1, rstd1 = norm_stats(resid)
    hidden = unit1 * gain1 + shift1
    low = hidden.astype(bf16)
    low_out[...] = low

    @pl.when(pl.program_id(0) == 0)
    def _():
        wait_for(w_in, sems.at[1])
        wait_for(w_down, sems.at[2])

    branch = bias_d
    for j in range(ff_cols):
        cols = slice(j * D, (j + 1) * D)
        inner = mxu(low, w_in[:, cols]) + bias_in[:, cols]
        phi = 0.5 + 0.5 * lax.erf(inner * (0.5 ** 0.5))
        act = (inner * phi).astype(bf16)
        act_out[:, cols] = act
        slope[:, cols] = phi + inner * (jnp.exp2(inner * inner * (-0.5 * LOG2E)) * 0.3989422804014327)
        branch = branch + mxu(act, w_down[cols, :])
    unit2, rstd2 = norm_stats(hidden + branch)
    out_rows[...] = (unit2 * gain2 + shift2).astype(bf16)
    grad = jnp.where(info[1 + SLOTS] == 1, back[...], back_got[...]).astype(f32)
    resid2 = norm_back(grad, unit2, rstd2, gain2)
    low_branch = resid2.astype(bf16)
    branch_out[...] = low_branch
    hidden_grad = resid2
    for j in range(ff_cols):
        cols = slice(j * D, (j + 1) * D)
        ig = (mxu(low_branch, w_down[cols, :], NT) * slope[:, cols]).astype(bf16)
        ig_out[:, cols] = ig
        hidden_grad = hidden_grad + mxu(ig, w_in[:, cols], NT)
        sums[3 + j : 4 + j, :] += jnp.sum(ig.astype(f32), axis=0, keepdims=True)
    resid1 = norm_back(hidden_grad, unit1, rstd1, gain1)
    resid_out[...] = resid1
    attn_grad = resid1.astype(bf16)
    attn_out[...] = attn_grad
    d_own[...] = mxu(attn_grad, mine, NT).astype(bf16)
    d_far[...] = mxu(attn_grad, other, NT).astype(bf16)
    rows = (
        (0, attn_grad.astype(f32)),
        (1, hidden_grad * unit1),
        (2, hidden_grad),
        (3 + ff_cols, low_branch.astype(f32)),
        (4 + ff_cols, grad * unit2),
        (5 + ff_cols, grad),
    )
    for at, value in rows:
        sums[at : at + 1, :] += jnp.sum(value, axis=0, keepdims=True)


def middle(info, tok, o_own, o_got, back, back_got, vecs, bias_in, own_pieces, far_pieces):
    half = tok.shape[0]
    ff = bias_in.shape[1]
    wide = pl.BlockSpec((TM, D), lambda i, *_: (i, 0))
    thin = pl.BlockSpec((TM, HALF), lambda i, *_: (i, 0))
    full = pl.BlockSpec((TM, ff), lambda i, *_: (i, 0))
    fixed = lambda rows, cols: pl.BlockSpec((rows, cols), lambda i, *_: (0, 0))
    pieces = tuple(own_pieces) + tuple(far_pieces)
    return pl.pallas_call(
        mid_body,
        grid_spec=pltpu.PrefetchScalarGridSpec(
            num_scalar_prefetch=1,
            grid=(half // TM,),
            in_specs=[wide, thin, thin, wide, wide, fixed(8, D), fixed(1, ff)] + [anyspec()] * len(pieces),
            out_specs=[wide, full, full, wide, wide, wide, wide, thin, thin, fixed(16, D)],
            scratch_shapes=[
                pltpu.VMEM((D, D), bf16),
                pltpu.VMEM((D, ff), bf16),
                pltpu.VMEM((ff, D), bf16),
                pltpu.VMEM((TM, ff), f32),
                pltpu.SemaphoreType.DMA((3,)),
            ],
        ),
        out_shape=[
            shape((half, D)),
            shape((half, ff)),
            shape((half, ff)),
            shape((half, D)),
            shape((half, D)),
            shape((half, D)),
            shape((half, D), f32),
            shape((half, HALF)),
            shape((half, HALF)),
            shape((16, D), f32),
        ],
        compiler_params=params(),
        cost_estimate=cost(half * D * (D + 2 * ff) * 4, half * D * 40),
    )(info, tok, o_own, o_got, back, back_got, vecs, bias_in, *pieces)


def wgrad_body(info, act, ig, low, branch, o_own, o_got, attn_grad, dst, res_in, res_down, res_out, sems):
    j = pl.program_id(0)
    n = pl.num_programs(0)
    me = info[0]
    par = lax.rem(j, 2)
    down_rows = ROWS * n
    per_step = SLOTS // n
    @pl.when(j == 0)
    def _():
        grad = attn_grad[...]
        for here, rows in ((me, o_own), (1 - me, o_got)):
            spot = pl.ds(pl.multiple_of(here * HALF, HALF), HALF)
            res_out[spot, :] = mxu(rows[...], grad, TN).astype(bf16)
        for chip in range(SLOTS):
            src = res_out.at[chip * ROWS : (chip + 1) * ROWS, :]
            pltpu.make_async_copy(src, dst.at[info[1 + chip], 0:ROWS, :], sems.at[2]).start()

    res_in[par] = mxu(low[...], ig[...], TN).astype(bf16)
    for chip in range(SLOTS):
        src = res_in.at[par, chip * ROWS : (chip + 1) * ROWS, :]
        spot = pl.ds(pl.multiple_of((1 + j) * ROWS, ROWS), ROWS)
        pltpu.make_async_copy(src, dst.at[info[1 + chip], spot, :], sems.at[par]).start()
    res_down[par] = mxu(act[...], branch[...], TN).astype(bf16)
    for q in range(per_step):
        src = res_down.at[par, q * down_rows : (q + 1) * down_rows, :]
        slot = info[1 + j * per_step + q]
        pltpu.make_async_copy(src, dst.at[slot, ROWS * (1 + n) : ROWS * (1 + 2 * n), :], sems.at[par]).start()

    def settle(which):
        wait_for(res_in.at[which], sems.at[which])
        wait_for(res_down.at[which], sems.at[which])

    @pl.when(j > 0)
    def _():
        settle(1 - par)

    @pl.when(j == n - 1)
    def _():
        settle(par)
        wait_for(res_out, sems.at[2])


def weight_grads(own, info, act, ig, low, branch, o_own, o_got, attn_grad):
    half, ff = act.shape
    n = ff // D
    strip = pl.BlockSpec((half, D), lambda j, *_: (0, j))
    fixed = lambda cols: pl.BlockSpec((half, cols), lambda j, *_: (0, 0))
    at = (lambda info: info[0]) if own else (lambda info: 1 - info[0])
    lanes_of = pl.BlockSpec((half, HALF), lambda j, info: (0, 2 * j + at(info)))
    side = pl.BlockSpec((half, HALF), lambda j, info: (0, at(info)))
    return pl.pallas_call(
        wgrad_body,
        grid_spec=pltpu.PrefetchScalarGridSpec(
            num_scalar_prefetch=1,
            grid=(n,),
            in_specs=[strip, lanes_of, fixed(D), side, fixed(HALF), fixed(HALF), side],
            out_specs=anyspec(),
            scratch_shapes=[
                pltpu.VMEM((2, D, HALF), bf16),
                pltpu.VMEM((2, D, HALF), bf16),
                pltpu.VMEM((D, HALF), bf16),
                pltpu.SemaphoreType.DMA((3,)),
            ],
        ),
        out_shape=shape((SLOTS, ROWS * (1 + 2 * n), HALF)),
        compiler_params=params(),
        cost_estimate=cost(half * D * (D + 2 * ff), half * ff * 8),
    )(info, act, ig, low, branch, o_own, o_got, attn_grad)


def qkv_grad_body(info, small, t_own, t_got, dq, dk, dv, out, t_all, d_all, res, res_small, sems):
    half = t_own.shape[0]
    pltpu.make_async_copy(t_own, t_all.at[0:half, :], sems.at[0]).start()
    pltpu.make_async_copy(t_got, t_all.at[half:, :], sems.at[0]).start()
    for j, src in enumerate((dq, dk, dv)):
        pltpu.make_async_copy(src, d_all.at[j], sems.at[1 + j]).start()
    wait_for(t_all, sems.at[0])
    res_small[...] = small[...].astype(bf16)
    row = lax.broadcasted_iota(jnp.int32, (16, HALF), 0)
    for j in range(3):
        wait_for(d_all.at[j], sems.at[1 + j])
        grads = d_all[j]
        res[j] = mxu(t_all[...], grads, TN).astype(bf16)
        for chip in range(SLOTS):
            src = res.at[j, chip * ROWS : (chip + 1) * ROWS, :]
            pltpu.make_async_copy(src, out.at[info[1 + chip], j * ROWS : (j + 1) * ROWS, :], sems.at[4]).start()
        if j != 1:
            total = jnp.sum(grads.astype(f32), axis=0, keepdims=True)
            place = 14 if j == 0 else 15
            res_small[...] = jnp.where(row == place, total, res_small[...].astype(f32)).astype(bf16)
    for slot in range(SLOTS):
        pltpu.make_async_copy(res_small, out.at[slot, 3 * ROWS : 3 * ROWS + 16, :], sems.at[5]).start()
    wait_for(res, sems.at[4])
    for slot in range(SLOTS):
        pltpu.make_async_copy(res_small, out.at[slot, 3 * ROWS : 3 * ROWS + 16, :], sems.at[5]).wait()


def qkv_grads(info, small, t_own, t_got, dq, dk, dv):
    total = dq.shape[0]
    return pl.pallas_call(
        qkv_grad_body,
        grid_spec=pltpu.PrefetchScalarGridSpec(
            num_scalar_prefetch=1,
            grid=(),
            in_specs=[pl.BlockSpec(memory_space=pltpu.VMEM)] + [anyspec()] * 5,
            out_specs=anyspec(),
            scratch_shapes=[
                pltpu.VMEM((total, D), bf16),
                pltpu.VMEM((3, total, HALF), bf16),
                pltpu.VMEM((3, D, HALF), bf16),
                pltpu.VMEM((16, HALF), bf16),
                pltpu.SemaphoreType.DMA((6,)),
            ],
        ),
        out_shape=shape((SLOTS, 3 * ROWS + 16, HALF)),
        compiler_params=pltpu.CompilerParams(vmem_limit_bytes=VMEM_CAP),
        cost_estimate=cost(total * D * HALF * 6, total * D * 5),
    )(info, small, t_own, t_got, dq, dk, dv)


def input_back_body(*refs):
    w = refs[0]
    dq, dk, dv = refs[1:4]
    out = refs[-1]
    total = None
    for j, part in enumerate((dq, dk, dv)):
        add = mxu(part[...], w[:, j * HALF : (j + 1) * HALF], NT)
        total = add if total is None else total + add
    for extra in refs[4:-1]:
        total = total + extra[...].astype(f32)
    out[...] = total.astype(bf16)


def input_back(w, dq, dk, dv, far, extras):
    half = dq.shape[0] // 2
    tile = 512
    base = half // tile if far else 0
    part = pl.BlockSpec((tile, HALF), lambda i: (base + i, 0))
    row = pl.BlockSpec((tile, D), lambda i: (i, 0))
    return pl.pallas_call(
        input_back_body,
        grid=(half // tile,),
        in_specs=[pl.BlockSpec((D, 3 * HALF), lambda i: (0, 0)), part, part, part] + [row] * len(extras),
        out_specs=row,
        out_shape=shape((half, D)),
        compiler_params=params(),
        cost_estimate=cost(half * D * HALF * 6, half * D * 8),
    )(w, dq, dk, dv, *extras)


def shift(n, k):
    return [(i, (i + k) % n) for i in range(n)]


class Plan:
    def __init__(self, seq, fsdp):
        rest = fsdp // 2
        dims = []
        while rest > 1:
            want = 4 if len(dims) % 2 == 0 and rest % 4 == 0 else 2
            dims.append(want)
            rest //= want
        self.dims = [seq] + dims + [2]
        self.names = ["s"] + ["r%d" % i for i in range(len(dims))] + ["c"]
        self.chips = seq * fsdp // 2
        self.direct = self.dims == [2, 4, 2, 2]
        self.stages = ([1] if dims else []) + [0] + list(range(2, len(dims) + 1))

    def at(self, a):
        return lax.axis_index(self.names[a])

    def coords(self):
        return [self.at(a) for a in range(len(self.dims))]

    def chip_table(self, sign, spot):
        if not self.direct:
            return jnp.arange(SLOTS, dtype=jnp.int32)
        spots = []
        for dx, dy in ((0, 0), (1, 0), (0, 1), (1, 1)):
            spots += [(dx, dy, z) for z in range(4)]
        dx, dy, dz = (jnp.asarray(v, jnp.int32) for v in zip(*spots))
        return ((spot[0] + sign * dx) % 2) * 8 + ((spot[1] + sign * dz) % 4) * 2 + (spot[2] + sign * dy) % 2

    def slot_table(self, sign, spot):
        table = self.chip_table(sign, spot)
        hit = table[:, None] == jnp.arange(SLOTS, dtype=jnp.int32)[None, :]
        return jnp.sum(jnp.where(hit, jnp.arange(SLOTS, dtype=jnp.int32)[:, None], 0), axis=0)

    def places(self, sign):
        grid = np.indices(self.dims[:-1]).reshape(len(self.dims) - 1, -1)
        flat = jnp.zeros((self.chips,), jnp.int32)
        if sign < 0:
            for a in reversed(self.stages):
                n = self.dims[a]
                flat = flat * n + (self.at(a) - jnp.asarray(grid[a], jnp.int32)) % n
            return flat
        sizes = [self.dims[a] for a in reversed(self.stages)]
        offs = np.indices(sizes).reshape(len(sizes), -1)
        by_axis = {a: offs[j] for j, a in enumerate(reversed(self.stages))}
        for a in range(len(self.dims) - 1):
            n = self.dims[a]
            flat = flat * n + (self.at(a) + jnp.asarray(by_axis[a], jnp.int32)) % n
        return flat

    def send(self, x, a, k=1):
        return lax.ppermute(x, self.names[a], shift(self.dims[a], k))


def gather_chips(plan, unit):
    buf = unit[None]
    for a in plan.stages:
        n = plan.dims[a]
        if n > 1:
            buf = jnp.concatenate([buf] + [plan.send(buf, a, k) for k in range(1, n)], axis=0)
    return jnp.take(buf, plan.places(-1), axis=0, mode="clip")


def reduce_chips(plan, grads):
    buf = jnp.take(grads, plan.places(1), axis=0, mode="clip")
    for a in reversed(plan.stages):
        n = plan.dims[a]
        size = buf.shape[0] // n
        keep = buf[:size].astype(f32)
        for k in range(1, n):
            keep = keep + plan.send(buf[k * size : (k + 1) * size].astype(bf16), a, k).astype(f32)
        buf = keep if a == plan.stages[0] else keep.astype(bf16)
    return buf[0]


def regroup(buf, sizes, count):
    n, _, w = buf.shape
    parts = []
    at = 0
    for size in sizes:
        parts.append(buf[:, at : at + size].reshape(count, n * size // count, w))
        at += size
    return jnp.concatenate(parts, axis=1)


def gather_z(plan, unit):
    return jnp.concatenate([unit[None]] + [plan.send(unit, 1, k)[None] for k in range(1, 4)], axis=0)


def swap_pair(x):
    return lax.ppermute(x, "c", [(0, 1), (1, 0)])


def cross(x):
    return lax.ppermute(x, ("s", "c"), [(1, 2), (2, 1)])


def together(*values):
    return lax.optimization_barrier(values)


def half_of(x, at):
    return lax.dynamic_slice_in_dim(x, at * HALF, HALF, axis=x.ndim - 1)


def chip_units(me, mine, got, sizes):
    low = jnp.where(me == 0, mine, got)
    high = jnp.where(me == 0, got, mine)
    parts = []
    at = 0
    for size in sizes:
        parts += [low[at : at + size], high[at : at + size]]
        at += size
    return jnp.concatenate(parts, axis=0)


def own_rows(me, total, sizes):
    first, second = [], []
    at = 0
    for size in sizes:
        first.append(total[at : at + size])
        second.append(total[at + size : at + 2 * size])
        at += 2 * size
    first = jnp.concatenate(first, axis=0)
    second = jnp.concatenate(second, axis=0)
    return jnp.where(me == 0, first, second), jnp.where(me == 0, second, first)


def local(plan, tokens, lengths, block_order, qkv_weight, query_bias, value_bias, out_weight, out_bias,
          norm1_gain, norm1_shift, in_weight, in_bias, down_weight, down_bias, norm2_gain, norm2_shift, cotangent):
    half = tokens.shape[1]
    me = plan.at(len(plan.dims) - 1)
    stays = plan.at(0) == me
    rows_dev = qkv_weight.shape[0]
    ff_dev = down_weight.shape[0]
    ff_cols = in_weight.shape[1] // D

    def tables(spot):
        core = spot[-1].astype(jnp.int32)[None]
        same = (spot[0] == spot[-1]).astype(jnp.int32)[None]
        return jnp.concatenate([core, plan.chip_table(-1, spot), same]), jnp.concatenate([core, plan.slot_table(1, spot)])

    sizes1 = [rows_dev] * 3
    sizes2 = [rows_dev] * (1 + ff_cols) + [ff_dev]
    smalls = (query_bias, value_bias, out_bias, norm1_gain, norm1_shift, in_bias, down_bias, norm2_gain, norm2_shift)
    unit_rows = 2 * half // UNITS

    def stacked(vectors):
        bias_o, gain1, shift1, wide, bias_d, gain2, shift2 = vectors[2:]
        zero = jnp.zeros((D,), f32)
        return jnp.stack([bias_o, gain1, shift1, bias_d, gain2, shift2, zero, zero]), wide[None]

    def settle_rows(x, got):
        return jnp.where(stays, x, got)

    tok = settle_rows(tokens[0], cross(tokens[0]))
    tok_got = swap_pair(tok)
    if plan.direct:
        lines = [v[None] for v in smalls] + [lengths, block_order]
        slab = (5 + 2 * ff_cols, rows_dev, HALF)
        mine, give = whole_call(pack_body, (slab, slab), qkv_weight, out_weight, in_weight,
                                down_weight.reshape(ff_cols, rows_dev, D), *lines)
        got = swap_pair(give)
        unit1, unit2 = whole_call(combine_body, ((7, rows_dev, HALF), (2 + 4 * ff_cols, rows_dev, HALF)), mine, got)
        unit1 = unit1.reshape(7 * rows_dev, HALF)
        unit2 = unit2.reshape(-1, HALF)
        other = got[3, len(smalls) : len(smalls) + 2, :UNITS].astype(jnp.int32)
        counts_here = jnp.where(stays, lengths[0], other[0]) // unit_rows
        order_here = jnp.where(stays, block_order[0], other[1])

        z1 = gather_z(plan, unit1)
        unit2, z1 = together(unit2, z1)
        x1, y1 = plan.send(z1, 0), plan.send(z1, 2)
        tok, unit2, *spot = together(tok, unit2, *plan.coords())
        z2_parts = [unit2] + [plan.send(unit2, 1, k) for k in range(1, 4)]
        pull, push = tables(spot)
        cot, x1, y1, tok, pull = together(cotangent[0], x1, y1, tok, pull)
        d1a, d1b = plan.send(y1[0:2], 0), plan.send(x1[2:4], 2)
        cot_got = cross(cot)
        pieces1 = [z1, x1, y1, d1a, d1b]
        tail_rows = [p[:, 6 * rows_dev : 6 * rows_dev + 16, 0:256] for p in pieces1]
        table = jnp.take(jnp.concatenate(tail_rows, axis=0), plan.slot_table(-1, spot), axis=0, mode="clip")
        table = table.reshape(plan.chips, 16, 2, 128)
        table = jnp.where(me == 0, table, table[:, :, ::-1])

        def vectors_of(table):
            return [table[:, i, :, : v.shape[0]].reshape(-1).astype(f32) for i, v in enumerate(smalls)]

        vectors = vectors_of(table)
    else:
        pull, push = tables(plan.coords())
        first = jnp.concatenate([qkv_weight[:, j * D : (j + 1) * D] for j in range(3)], axis=0)
        second = jnp.concatenate([out_weight] + [in_weight[:, j * D : (j + 1) * D] for j in range(ff_cols)] + [down_weight], axis=0)
        line = jnp.concatenate(smalls)
        both = jnp.concatenate([first, second], axis=0)
        got = swap_pair(half_of(both, 1 - me))
        mine = half_of(both, me)
        cut = 3 * rows_dev
        unit1 = chip_units(me, mine[:cut], got[:cut], sizes1)
        unit2 = chip_units(me, mine[cut:], got[cut:], sizes2)
        line_got = swap_pair(line)
        line_unit = jnp.stack([jnp.where(me == 0, line, line_got), jnp.where(me == 0, line_got, line)])
        pieces1 = [regroup(gather_chips(plan, unit1), [2 * r for r in sizes1], SLOTS)]
        pieces2 = [regroup(gather_chips(plan, unit2), [2 * r for r in sizes2], SLOTS)]
        far2 = [swap_pair(p) for p in pieces2]
        lines = gather_chips(plan, line_unit).reshape(2 * plan.chips, line.shape[0])
        vectors = []
        at = 0
        for piece in smalls:
            size = piece.shape[0]
            vectors.append(lines[:, at : at + size].reshape(2 * plan.chips * size).astype(f32))
            at += size
        counts_here = jnp.where(stays, lengths[0], swap_pair(lengths[0])) // unit_rows
        order_here = jnp.where(stays, block_order[0], swap_pair(block_order[0]))
        cot_got = cross(cotangent[0])
    bias_q, bias_v = vectors[:2]
    bias_qkv = jnp.concatenate([half_of(bias_q, me), jnp.zeros((HALF,), f32), half_of(bias_v, me)])[None]

    spot = jnp.arange(UNITS)
    ends = jnp.sum(jnp.where(spot[None, :] <= spot[:, None], counts_here[None, :], 0), axis=1)
    seg_packed = jnp.sum((spot[:, None] >= ends[None, :]).astype(jnp.int32), axis=1)
    hit = order_here[:, None] == spot[None, :]
    segs = jnp.sum(jnp.where(hit, seg_packed[:, None], 0), axis=0)
    segs = jnp.where(me == 0, segs, jnp.roll(segs, UNITS // 2))

    qkv, w_qkv = project(pull, tok, tok_got, bias_qkv, pieces1)
    if plan.direct:
        *z2_parts, table, qkv = together(*z2_parts, table, qkv)
        vectors = vectors_of(table)
        z2 = jnp.stack(z2_parts)
        x2, y2 = plan.send(z2, 0), plan.send(z2, 2)
        z2_far = swap_pair(z2)
        att = attention(segs, qkv, 0, 2, None)
        vecs, gate_bias = stacked(vectors)
        x2, y2, cot_got, vecs, gate_bias, push, *att = together(x2, y2, cot_got, vecs, gate_bias, push, *att)
        d2a, d2b = plan.send(y2[0:2], 0), plan.send(x2[2:4], 2)
        x2_far, y2_far = swap_pair(x2), swap_pair(y2)
    else:
        att = attention(segs, qkv, 0, 2, None)
        vecs, gate_bias = stacked(vectors)
    o_own, o_far, lse = attention(segs, qkv, 2, PAIRS - 2, att)
    o_got = swap_pair(o_far)
    if plan.direct:
        pieces2 = [z2, x2, y2, d2a, d2b]
        far2 = [z2_far, x2_far, y2_far, swap_pair(d2a), swap_pair(d2b)]
    (out_rows, act, ig, low, branch, attn_grad, resid1, d_own, d_far, sums) = middle(
        pull, tok, o_own, o_got, cotangent[0], cot_got, vecs, gate_bias, pieces2, far2)
    d_got = swap_pair(d_far)
    out_got = cross(out_rows)
    sum_got = swap_pair(half_of(sums, 1 - me))
    grad_args = (low, branch, o_own, o_got)
    give = weight_grads(False, push, act, ig, *grad_args, attn_grad)
    give, attn_grad = together(give, attn_grad)
    got_g = swap_pair(give)
    keep = weight_grads(True, push, act, ig, *grad_args, attn_grad)
    back_args = (o_own, o_far, d_own, d_got, lse)
    if plan.direct:

        def both_sums(lo, hi):
            return keep[lo:hi].astype(f32) + got_g[lo:hi].astype(f32)

        def late(rows):
            return jnp.pad(rows.astype(f32), ((2, 0), (0, 0), (0, 0)))

        def early(rows):
            return jnp.pad(rows.astype(f32), ((0, 2), (0, 0), (0, 0)))

        sx, sy, qkv_back, out_got = together(both_sums(12, 14).astype(bf16), both_sums(14, 16).astype(bf16), qkv, out_got)
        rx, ry = plan.send(sx, 0), plan.send(sy, 2)
        g = attention_back(segs, qkv_back, *back_args, 0, 1, None)
        rx, ry, sum_got, *g = together(rx, ry, sum_got, *g)
        send_x = (both_sums(4, 8) + late(ry)).astype(bf16)
        send_y = (both_sums(8, 12) + early(rx)).astype(bf16)
        send_x, send_y, *g = together(send_x, send_y, *g)
        px, py = plan.send(send_x, 0), plan.send(send_y, 2)
        g = attention_back(segs, qkv_back, *back_args, 1, 1, g)
        px, py, *g = together(px, py, *g)
        z_sum = both_sums(0, 4) + px.astype(f32) + py.astype(f32)
        z_low, ffn, *g = together(z_sum[1:].astype(bf16), z_sum[0], *g)
        z_got = [plan.send(z_low[k - 1], 1, k) for k in range(1, 4)]
        g = attention_back(segs, qkv_back, *back_args, 2, PAIRS - 2, g)
        *z_got, dq, dk, dv = together(*z_got, *g)
        for part in z_got:
            ffn = ffn + part.astype(f32)
    else:
        dq, dk, dv = attention_back(segs, qkv, *back_args, 0, PAIRS, None)
        summed = (keep.astype(f32) + got_g.astype(f32)).astype(bf16)
        scale = plan.chips // SLOTS
        units = regroup_back(summed, [ROWS] * (1 + ff_cols) + [ROWS * ff_cols], scale)
        ffn = reduce_chips(plan, units)
    small = half_of(sums, me) + sum_got
    tail = qkv_grads(push, small, tok, tok_got, dq, dk, dv)
    if plan.direct:
        rx, ry = plan.send(tail[12:14], 0), plan.send(tail[14:16], 2)
        far_back = input_back(w_qkv, dq, dk, dv, True, ())
        rx, ry, far_back = together(rx, ry, far_back)
        far_back = swap_pair(far_back)
        send_x = (tail[4:8].astype(f32) + late(ry)).astype(bf16)
        send_y = (tail[8:12].astype(f32) + early(rx)).astype(bf16)
        px, py = plan.send(send_x, 0), plan.send(send_y, 2)
        packed = input_back(w_qkv, dq, dk, dv, False, (resid1, far_back))
        px, py, packed = together(px, py, packed)
        packed_got = cross(packed)
        z_sum = tail[0:4].astype(f32) + px.astype(f32) + py.astype(f32)
        z_low, out_got = together(z_sum[1:].astype(bf16), out_got)
        qkv_sum = z_sum[0]
        output = settle_rows(out_rows, out_got)
        packed_got, output, *z_got = together(packed_got, output, *[plan.send(z_low[k - 1], 1, k) for k in range(1, 4)])
        for part in z_got:
            qkv_sum = qkv_sum + part.astype(f32)
    else:
        far_back = swap_pair(input_back(w_qkv, dq, dk, dv, True, ()))
        packed = input_back(w_qkv, dq, dk, dv, False, (resid1, far_back))
        packed_got = cross(packed)
        output = settle_rows(out_rows, out_got)
        units = regroup_back(tail[:, : 3 * ROWS], [ROWS] * 3, scale)
        extra = jnp.broadcast_to(tail[0:1, 3 * ROWS :], (plan.chips, 16, HALF))
        qkv_sum = reduce_chips(plan, jnp.concatenate([units, extra], axis=1))
    small_sum = qkv_sum[6 * rows_dev :]
    sizes = sizes1 + sizes2
    total = jnp.concatenate([qkv_sum[: 6 * rows_dev], ffn], axis=0)
    mine, other = own_rows(me, total, sizes)
    got = swap_pair(jnp.concatenate([other, small_sum], axis=0))
    count = mine.shape[0]
    mine = jnp.concatenate([mine, small_sum], axis=0)
    full = jnp.concatenate([jnp.where(me == 0, mine, got), jnp.where(me == 0, got, mine)], axis=1)
    take = lambda at, size: full[at : at + size]
    out_qkv = jnp.concatenate([take(j * rows_dev, rows_dev) for j in range(3)], axis=1)
    out_out = take(3 * rows_dev, rows_dev)
    out_in = jnp.concatenate([take((4 + j) * rows_dev, rows_dev) for j in range(ff_cols)], axis=1)
    out_down = take((4 + ff_cols) * rows_dev, ff_dev)
    small_full = full[count:]
    device = plan.at(0)
    for a in range(1, len(plan.dims)):
        device = device * plan.dims[a] + plan.at(a)
    order = (14, 15, 0, 1, 2, 3, 3 + ff_cols, 4 + ff_cols, 5 + ff_cols)
    wide_row = 3
    thin = lax.dynamic_slice_in_dim(small_full, device * rows_dev, rows_dev, axis=1)
    span = small_full[wide_row : wide_row + ff_cols].reshape(-1)
    s = [lax.dynamic_slice_in_dim(span, device * ff_dev, ff_dev) if row == wide_row and piece is in_bias else thin[row]
         for piece, row in zip(smalls, order)]
    input_grad = settle_rows(packed, packed_got)
    return (output[None], input_grad[None], out_qkv, s[0], s[1], out_out, s[2], s[3], s[4], out_in, s[5], out_down, s[6], s[7], s[8])


def regroup_back(buf, sizes, scale):
    n, _, w = buf.shape
    parts = []
    at = 0
    for size in sizes:
        parts.append(buf[:, at : at + size].reshape(n * scale, size // scale, w))
        at += size
    return jnp.concatenate(parts, axis=1)


def solution(mesh):
    plan = Plan(mesh.shape["seq"], mesh.shape["fsdp"])
    inner_mesh = Mesh(mesh.devices.reshape(plan.dims), tuple(plan.names))
    groups = tuple(plan.names[1:])
    every = tuple(plan.names)
    rows = P(groups, "s", None)
    table = P(groups, None)
    mat = P(every, None)
    vec = P(every)
    placed = (rows, table, table, mat, vec, vec, mat, vec, vec, vec, mat, vec, mat, vec, vec, vec, rows)
    outs = (rows, rows, mat, vec, vec, mat, vec, vec, vec, mat, vec, mat, vec, vec, vec)

    def run(*args):
        return local(plan, *args)

    return jax.shard_map(run, mesh=inner_mesh, in_specs=placed, out_specs=outs, check_vma=False)
```

```python
import jax
import jax.numpy as jnp
import numpy as np
from jax import lax
from jax.sharding import Mesh, PartitionSpec as P
from jax.experimental import pallas as pl
from jax.experimental.pallas import tpu as pltpu

D = 768
HALF = D // 2
HD = 64
UNITS = 16
SLOTS = 16
ROWS = D // SLOTS
PAIRS = HALF // 128
LOG2E = 1.4426950408889634
LN2 = 0.6931471805599453
BIG = 1e30
TQ = 1024
TQ_BACK = 512
STEP = 256
STEP_BACK = 1024
TM = 256
norm_eps = 1e-12
bf16 = jnp.bfloat16
f32 = jnp.float32
NT = (((1,), (1,)), ((), ()))
NN = (((1,), (0,)), ((), ()))
TN = (((0,), (0,)), ((), ()))
VMEM_CAP = 58 << 20


def mxu(a, b, dims=NN):
    return lax.dot_general(a, b, dims, preferred_element_type=f32)


def shape(size, kind=bf16):
    return jax.ShapeDtypeStruct(size, kind)


def params(axes=1):
    return pltpu.CompilerParams(dimension_semantics=("arbitrary",) * axes, vmem_limit_bytes=VMEM_CAP)


def cost(flops, moved):
    return pl.CostEstimate(flops=int(flops), bytes_accessed=int(moved), transcendentals=0)


def tie(value, *others):
    return lax.optimization_barrier((value,) + others)[0]


def lanes(rows):
    return lax.broadcasted_iota(jnp.int32, (rows, 128), 1)


def seg_rows(segs_ref, base_block, rows):
    place = lax.broadcasted_iota(jnp.int32, (rows, 128), 0)
    out = jnp.zeros((rows, 128), jnp.int32)
    for b in range(rows // 128):
        out = jnp.where(place >= b * 128, segs_ref[base_block + b], out)
    return out


def split3(v):
    hi = v.astype(bf16).astype(f32)
    mid = (v - hi).astype(bf16).astype(f32)
    return hi, mid, v - hi - mid


def both_heads(pair_rows):
    lane = lanes(pair_rows.shape[0])
    zero = jnp.zeros_like(pair_rows)
    first = jnp.where(lane < HD, pair_rows, zero)
    return jnp.concatenate([first, jnp.where(lane < HD, zero, pair_rows)], axis=0)


def fill_keys(segs_ref, k_in, v_in, k_aug, v_aug):
    for at in range(0, k_in.shape[0], STEP):
        rows = slice(at, at + STEP)
        lane = lanes(STEP)
        hot = (lane == seg_rows(segs_ref, at // 128, STEP)) | ((lane >= 64) & (lane < 67))
        k_aug[rows, :128] = k_in[rows, :]
        k_aug[rows, 128:] = jnp.where(hot, 1.0, 0.0).astype(bf16)
        v_aug[rows, :128] = v_in[rows, :]
        v_aug[rows, 128:] = jnp.ones((STEP, 128), bf16)


def attend_body(segs_ref, q_in, k_in, v_in, *refs):
    o_own, o_far, lse_ref, k_aug, v_aug = refs[-5:]
    i = pl.program_id(1)
    n_half = pl.num_programs(1) // 2

    @pl.when(i == 0)
    def _():
        fill_keys(segs_ref, k_in, v_in, k_aug, v_aug)

    lane = lanes(TQ)
    seg = seg_rows(segs_ref, i * (TQ // 128), TQ)
    off = jnp.where((lane < 16) & (lane != seg), -BIG, 0.0).astype(bf16)
    q_aug = jnp.concatenate([both_heads(q_in[...]), jnp.concatenate([off, off], axis=0)], axis=1)
    top = None
    acc = None
    for at in range(0, k_aug.shape[0], STEP):
        s = mxu(q_aug, k_aug[at : at + STEP, :], NT)
        here = jnp.max(s, axis=1, keepdims=True)
        new_top = here if top is None else jnp.maximum(top, here)
        p = jnp.exp2(s - new_top).astype(bf16)
        add = mxu(p, v_aug[at : at + STEP, :])
        acc = add if acc is None else acc * jnp.exp2(top - new_top) + add
        top = new_top
    both = jnp.where(lane < HD, acc[:TQ, :128], acc[TQ:, :128])
    sums = jnp.where(lane < HD, acc[:TQ, 128:], acc[TQ:, 128:])
    tops = jnp.where(lane < HD, top[:TQ], top[TQ:])
    out = (both / sums).astype(bf16)
    lse_ref[...] = tops + jnp.log2(sums)

    @pl.when(i < n_half)
    def _():
        o_own[...] = out

    @pl.when(i >= n_half)
    def _():
        o_far[...] = out


def anyspec():
    return pl.BlockSpec(memory_space=pl.ANY)


def pair_specs(n_half, first, rows):
    own = pl.BlockSpec((rows, 128), lambda h, i, *_: (jnp.minimum(i, n_half - 1), first + h))
    far = pl.BlockSpec((rows, 128), lambda h, i, *_: (jnp.maximum(i - n_half, 0), first + h))
    return own, far


def attention(segs, qkv, first, count, prev):
    total = qkv.shape[0]
    half = total // 2
    n_half = half // TQ
    own, far = pair_specs(n_half, first, TQ)
    row = pl.BlockSpec((TQ, 128), lambda h, i, *_: (i, first + h))
    whole = lambda part: pl.BlockSpec((total, 128), lambda h, i, *_: (0, part * PAIRS + first + h))
    prev = () if prev is None else tuple(prev)
    return pl.pallas_call(
        attend_body,
        grid_spec=pltpu.PrefetchScalarGridSpec(
            num_scalar_prefetch=1,
            grid=(count, 2 * n_half),
            in_specs=[row, whole(1), whole(2)] + [anyspec()] * len(prev),
            out_specs=[own, far, row],
            scratch_shapes=[pltpu.VMEM((total, 256), bf16), pltpu.VMEM((total, 256), bf16)],
        ),
        out_shape=[shape((half, HALF)), shape((half, HALF)), shape((total, HALF), f32)],
        input_output_aliases={4 + j: j for j in range(len(prev))},
        compiler_params=params(2),
        cost_estimate=cost(count * total * total * 2048, total * 128 * 2 * 8),
    )(segs, qkv, qkv, qkv, *prev)


def attend_back_body(segs_ref, q_in, k_in, v_in, o_own, o_far, d_own, d_far, lse_ref, *refs):
    dq_out, dk_out, dv_out, k_aug, v_aug, dk_acc, dv_acc, k_turn = refs[-8:]
    i = pl.program_id(1)
    n = pl.num_programs(1)

    @pl.when(i == 0)
    def _():
        fill_keys(segs_ref, k_in, v_in, k_aug, v_aug)
        k_turn[...] = k_in[...].T
        dk_acc[...] = jnp.zeros_like(dk_acc)
        dv_acc[...] = jnp.zeros_like(dv_acc)

    near = i < n // 2
    d_rows = jnp.where(near, d_own[...], d_far[...])
    o_rows = jnp.where(near, o_own[...], o_far[...])
    lane = lanes(TQ_BACK)
    seg = seg_rows(segs_ref, i * (TQ_BACK // 128), TQ_BACK)
    off = jnp.where((lane < 16) & (lane != seg), -BIG, 0.0)
    prod = d_rows.astype(f32) * o_rows.astype(f32)
    q_side, d_side = [], []
    for head in range(2):
        mine = (lane < HD) if head == 0 else (lane >= HD)
        dot_row = jnp.sum(jnp.where(mine, prod, 0.0), axis=1, keepdims=True)
        lse = jnp.broadcast_to(lse_ref[:, head * HD : head * HD + 1], (TQ_BACK, 128))
        for side, value, rest in ((q_side, -lse, off), (d_side, -jnp.broadcast_to(dot_row, (TQ_BACK, 128)), 0.0)):
            h, m, l = split3(value)
            cols = jnp.where(lane == 64, h, jnp.where(lane == 65, m, jnp.where(lane == 66, l, rest)))
            side.append(cols.astype(bf16))
    q2 = both_heads(q_in[...])
    d2 = both_heads(d_rows)
    q_aug = jnp.concatenate([q2, jnp.concatenate(q_side, axis=0)], axis=1)
    d_aug = jnp.concatenate([d2, jnp.concatenate(d_side, axis=0)], axis=1)
    dq = None
    for at in range(0, k_aug.shape[0], STEP_BACK):
        rows = slice(at, at + STEP_BACK)
        p = jnp.exp2(mxu(k_aug[rows, :], q_aug, NT))
        ds = (p * mxu(v_aug[rows, :], d_aug, NT)).astype(bf16)
        dv_acc[rows, :] += mxu(p.astype(bf16), d2)
        dk_acc[rows, :] += mxu(ds, q2)
        add = mxu(k_turn[:, rows], ds)
        dq = add if dq is None else dq + add
    dq = jnp.concatenate([dq[:HD, :TQ_BACK], dq[HD:, TQ_BACK:]], axis=0) * (HD ** -0.5)
    dq_out[...] = dq.T.astype(bf16)

    @pl.when(i == n - 1)
    def _():
        dk_out[...] = (dk_acc[...] * LN2).astype(bf16)
        dv_out[...] = dv_acc[...].astype(bf16)


def attention_back(segs, qkv, o_own, o_far, d_own, d_far, lse, first, count, prev):
    total = qkv.shape[0]
    half = total // 2
    n_half = half // TQ_BACK
    own, far = pair_specs(n_half, first, TQ_BACK)
    row = pl.BlockSpec((TQ_BACK, 128), lambda h, i, *_: (i, first + h))
    whole = lambda part: pl.BlockSpec((total, 128), lambda h, i, *_: (0, part * PAIRS + first + h))
    prev = () if prev is None else tuple(prev)
    return pl.pallas_call(
        attend_back_body,
        grid_spec=pltpu.PrefetchScalarGridSpec(
            num_scalar_prefetch=1,
            grid=(count, 2 * n_half),
            in_specs=[row, whole(1), whole(2), own, far, own, far, row] + [anyspec()] * len(prev),
            out_specs=[row, whole(0), whole(0)],
            scratch_shapes=[
                pltpu.VMEM((total, 256), bf16),
                pltpu.VMEM((total, 256), bf16),
                pltpu.VMEM((total, 128), f32),
                pltpu.VMEM((total, 128), f32),
                pltpu.VMEM((128, total), bf16),
            ],
        ),
        out_shape=[shape((total, HALF))] * 3,
        input_output_aliases={9 + j: j for j in range(len(prev))},
        compiler_params=params(2),
        cost_estimate=cost(count * total * total * 5120, total * 128 * 2 * 12),
    )(segs, qkv, qkv, qkv, o_own, o_far, d_own, d_far, lse, *prev)


def pack_body(qkv, w_out, w_in, w_down, *refs):
    lines, (mine, give) = refs[:-2], refs[-2:]
    me = lax.axis_index("c")
    for half_at, dst in ((me, mine), (1 - me, give)):
        slab = 0

        def cols(base):
            return pl.ds(pl.multiple_of(base + half_at * HALF, 128), HALF)

        for j in range(3):
            dst[slab] = qkv[:, cols(j * D)]
            slab += 1
        dst[slab] = jnp.zeros(dst.shape[1:], bf16)
        for i, line in enumerate(lines):
            value = line[...].astype(f32)
            dst[slab, i : i + 1, 0 : value.shape[1]] = value.astype(bf16)
        dst[slab + 1] = w_out[:, cols(0)]
        slab += 2
        for j in range(w_in.shape[1] // D):
            dst[slab] = w_in[:, cols(j * D)]
            slab += 1
        for j in range(w_down.shape[0]):
            dst[slab] = w_down[j, :, cols(0)]
            slab += 1


def combine_body(mine, got, unit1, unit2):
    me = lax.axis_index("c")
    n = unit2.shape[0] // 2
    wide = n // 2
    unit1[6] = jnp.zeros(unit1.shape[1:], bf16)
    for at, src in ((me, mine), (1 - me, got)):
        for j in range(3):
            unit1[2 * j + at] = src[j]
        for j in range(wide + 1):
            unit2[2 * j + at] = src[4 + j]
        for j in range(wide):
            unit2[2 * (wide + 1) + at * wide + j] = src[5 + wide + j]
    unit1[6, :, 0:128] = mine[3, :, 0:128]
    unit1[6, :, 128:256] = got[3, :, 0:128]


def whole_call(body, outs, *args):
    return pl.pallas_call(
        body,
        in_specs=[pl.BlockSpec(memory_space=pltpu.VMEM)] * len(args),
        out_specs=[pl.BlockSpec(memory_space=pltpu.VMEM)] * len(outs),
        out_shape=[shape(o) for o in outs],
        cost_estimate=cost(0, 2 << 20),
    )(*args)


def each_slot(pieces):
    at = 0
    for ref in pieces:
        for slot in range(ref.shape[0]):
            yield at, ref, slot
            at += 1


def wait_for(dst, sem):
    pltpu.make_async_copy(dst, dst, sem).wait()


def proj_body(info, t_own, t_got, bias, *refs):
    pieces, (out, w_out, w, sem) = refs[:-4], refs[-4:]
    i = pl.program_id(0)

    @pl.when(i == 0)
    def _():
        for at, ref, slot in each_slot(pieces):
            rows = pl.ds(pl.multiple_of(info[1 + at] * ROWS, ROWS), ROWS)
            for j in range(3):
                src = ref.at[slot, j * ROWS : (j + 1) * ROWS, :]
                pltpu.make_async_copy(src, w.at[rows, j * HALF : (j + 1) * HALF], sem).start()
        wait_for(w, sem)

    tile = jnp.where(i < pl.num_programs(0) // 2, t_own[...], t_got[...])
    for j in range(3):
        cols = slice(j * HALF, (j + 1) * HALF)
        part = mxu(tile, w[:, cols]) + bias[0:1, cols]
        if j == 0:
            part = part * (LOG2E * HD ** -0.5)
        out[:, cols] = part.astype(bf16)
    w_out[...] = w[...]


def project(info, t_own, t_got, bias, pieces):
    half = t_own.shape[0]
    tile = 512
    n_half = half // tile
    own = pl.BlockSpec((tile, D), lambda i, *_: (jnp.minimum(i, n_half - 1), 0))
    got = pl.BlockSpec((tile, D), lambda i, *_: (jnp.maximum(i - n_half, 0), 0))
    return pl.pallas_call(
        proj_body,
        grid_spec=pltpu.PrefetchScalarGridSpec(
            num_scalar_prefetch=1,
            grid=(2 * n_half,),
            in_specs=[own, got, pl.BlockSpec((1, 3 * HALF), lambda i, *_: (0, 0))] + [anyspec()] * len(pieces),
            out_specs=[
                pl.BlockSpec((tile, 3 * HALF), lambda i, *_: (i, 0)),
                pl.BlockSpec((D, 3 * HALF), lambda i, *_: (0, 0)),
            ],
            scratch_shapes=[pltpu.VMEM((D, 3 * HALF), bf16), pltpu.SemaphoreType.DMA],
        ),
        out_shape=[shape((2 * half, 3 * HALF)), shape((D, 3 * HALF))],
        compiler_params=params(),
        cost_estimate=cost(half * D * D * 6, half * D * 12),
    )(info, t_own, t_got, bias, *pieces)


def table_body(info, *refs):
    pieces, (out, held, sem) = refs[:-3], refs[-3:]
    for at, ref, slot in each_slot(pieces):
        src = ref.at[slot, 3 * ROWS : 3 * ROWS + 16, 0:256]
        pltpu.make_async_copy(src, held.at[at], sem).start()
    wait_for(held, sem)
    me = info[0]
    for chip in range(SLOTS):
        rows = held[info[1 + chip]]
        turned = jnp.concatenate([rows[:, 128:], rows[:, :128]], axis=1)
        out[chip] = jnp.where(me == 0, rows, turned)


def small_table(info, pieces):
    return pl.pallas_call(
        table_body,
        grid_spec=pltpu.PrefetchScalarGridSpec(
            num_scalar_prefetch=1,
            grid=(),
            in_specs=[anyspec()] * len(pieces),
            out_specs=pl.BlockSpec(memory_space=pltpu.VMEM),
            scratch_shapes=[pltpu.VMEM((SLOTS, 16, 256), bf16), pltpu.SemaphoreType.DMA],
        ),
        out_shape=shape((SLOTS, 16, 256)),
        cost_estimate=cost(0, 1 << 18),
    )(info, *pieces)


def norm_stats(rows):
    mean = jnp.mean(rows, axis=-1, keepdims=True)
    centered = rows - mean
    var = jnp.mean(centered * centered, axis=-1, keepdims=True)
    rstd = lax.rsqrt(var + norm_eps)
    return centered * rstd, rstd


def norm_back(grad, unit, rstd, gain):
    eg = grad * gain
    mean_eg = jnp.mean(eg, axis=-1, keepdims=True)
    mean_en = jnp.mean(eg * unit, axis=-1, keepdims=True)
    return (eg - mean_eg - unit * mean_en) * rstd


def mid_body(info, tok, o_own, o_got, back, back_got, vecs, bias_in, *refs):
    n_out = 10
    outs, scratch = refs[-n_out - 5 : -5], refs[-5:]
    pieces = refs[: -n_out - 5]
    own_pieces, far_pieces = pieces[: len(pieces) // 2], pieces[len(pieces) // 2 :]
    out_rows, act_out, ig_out, low_out, branch_out, attn_out, resid_out, d_own, d_far, sums = outs
    w_out, w_in, w_down, slope, sems = scratch
    ff_cols = w_in.shape[1] // D
    me = info[0]

    @pl.when(pl.program_id(0) == 0)
    def _():
        for kind in range(3):
            for here, part in ((me, own_pieces), (1 - me, far_pieces)):
                for at, ref, slot in each_slot(part):
                    chip = info[1 + at]
                    lane0 = pl.multiple_of(here * HALF, HALF)
                    rows = pl.ds(pl.multiple_of(chip * ROWS, ROWS), ROWS)
                    if kind == 0:
                        pltpu.make_async_copy(ref.at[slot, 0:ROWS, :], w_out.at[rows, pl.ds(lane0, HALF)], sems.at[0]).start()
                    elif kind == 1:
                        for j in range(ff_cols):
                            src = ref.at[slot, (1 + j) * ROWS : (2 + j) * ROWS, :]
                            dst = w_in.at[rows, pl.ds(pl.multiple_of(lane0 + j * D, HALF), HALF)]
                            pltpu.make_async_copy(src, dst, sems.at[1]).start()
                    else:
                        size = ROWS * ff_cols
                        src = ref.at[slot, (1 + ff_cols) * ROWS : (1 + 2 * ff_cols) * ROWS, :]
                        dst = w_down.at[pl.ds(pl.multiple_of(chip * size, size), size), pl.ds(lane0, HALF)]
                        pltpu.make_async_copy(src, dst, sems.at[2]).start()
        sums[...] = jnp.zeros_like(sums)
        wait_for(w_out, sems.at[0])

    bias_o, gain1, shift1 = vecs[0:1, :], vecs[1:2, :], vecs[2:3, :]
    bias_d, gain2, shift2 = vecs[3:4, :], vecs[4:5, :], vecs[5:6, :]
    mine = w_out[pl.ds(pl.multiple_of(me * HALF, HALF), HALF), :]
    other = w_out[pl.ds(pl.multiple_of((1 - me) * HALF, HALF), HALF), :]
    resid = tok[...].astype(f32) + mxu(o_own[...], mine) + mxu(o_got[...], other) + bias_o
    unit1, rstd1 = norm_stats(resid)
    hidden = unit1 * gain1 + shift1
    low = hidden.astype(bf16)
    low_out[...] = low

    @pl.when(pl.program_id(0) == 0)
    def _():
        wait_for(w_in, sems.at[1])
        wait_for(w_down, sems.at[2])

    branch = bias_d
    for j in range(ff_cols):
        cols = slice(j * D, (j + 1) * D)
        inner = mxu(low, w_in[:, cols]) + bias_in[:, cols]
        phi = 0.5 + 0.5 * lax.erf(inner * (0.5 ** 0.5))
        act = (inner * phi).astype(bf16)
        act_out[:, cols] = act
        slope[:, cols] = phi + inner * (jnp.exp2(inner * inner * (-0.5 * LOG2E)) * 0.3989422804014327)
        branch = branch + mxu(act, w_down[cols, :])
    unit2, rstd2 = norm_stats(hidden + branch)
    out_rows[...] = (unit2 * gain2 + shift2).astype(bf16)
    grad = jnp.where(info[1 + SLOTS] == 1, back[...], back_got[...]).astype(f32)
    resid2 = norm_back(grad, unit2, rstd2, gain2)
    low_branch = resid2.astype(bf16)
    branch_out[...] = low_branch
    hidden_grad = resid2
    for j in range(ff_cols):
        cols = slice(j * D, (j + 1) * D)
        ig = (mxu(low_branch, w_down[cols, :], NT) * slope[:, cols]).astype(bf16)
        ig_out[:, cols] = ig
        hidden_grad = hidden_grad + mxu(ig, w_in[:, cols], NT)
        sums[3 + j : 4 + j, :] += jnp.sum(ig.astype(f32), axis=0, keepdims=True)
    resid1 = norm_back(hidden_grad, unit1, rstd1, gain1)
    resid_out[...] = resid1
    attn_grad = resid1.astype(bf16)
    attn_out[...] = attn_grad
    d_own[...] = mxu(attn_grad, mine, NT).astype(bf16)
    d_far[...] = mxu(attn_grad, other, NT).astype(bf16)
    rows = (
        (0, attn_grad.astype(f32)),
        (1, hidden_grad * unit1),
        (2, hidden_grad),
        (3 + ff_cols, low_branch.astype(f32)),
        (4 + ff_cols, grad * unit2),
        (5 + ff_cols, grad),
    )
    for at, value in rows:
        sums[at : at + 1, :] += jnp.sum(value, axis=0, keepdims=True)


def middle(info, tok, o_own, o_got, back, back_got, vecs, bias_in, own_pieces, far_pieces):
    half = tok.shape[0]
    ff = bias_in.shape[1]
    wide = pl.BlockSpec((TM, D), lambda i, *_: (i, 0))
    thin = pl.BlockSpec((TM, HALF), lambda i, *_: (i, 0))
    full = pl.BlockSpec((TM, ff), lambda i, *_: (i, 0))
    fixed = lambda rows, cols: pl.BlockSpec((rows, cols), lambda i, *_: (0, 0))
    pieces = tuple(own_pieces) + tuple(far_pieces)
    return pl.pallas_call(
        mid_body,
        grid_spec=pltpu.PrefetchScalarGridSpec(
            num_scalar_prefetch=1,
            grid=(half // TM,),
            in_specs=[wide, thin, thin, wide, wide, fixed(8, D), fixed(1, ff)] + [anyspec()] * len(pieces),
            out_specs=[wide, full, full, wide, wide, wide, wide, thin, thin, fixed(16, D)],
            scratch_shapes=[
                pltpu.VMEM((D, D), bf16),
                pltpu.VMEM((D, ff), bf16),
                pltpu.VMEM((ff, D), bf16),
                pltpu.VMEM((TM, ff), f32),
                pltpu.SemaphoreType.DMA((3,)),
            ],
        ),
        out_shape=[
            shape((half, D)),
            shape((half, ff)),
            shape((half, ff)),
            shape((half, D)),
            shape((half, D)),
            shape((half, D)),
            shape((half, D), f32),
            shape((half, HALF)),
            shape((half, HALF)),
            shape((16, D), f32),
        ],
        compiler_params=params(),
        cost_estimate=cost(half * D * (D + 2 * ff) * 4, half * D * 40),
    )(info, tok, o_own, o_got, back, back_got, vecs, bias_in, *pieces)


def wgrad_body(info, act, ig, low, branch, o_own, o_got, attn_grad, dst, res_in, res_down, res_out, sems):
    j = pl.program_id(0)
    n = pl.num_programs(0)
    me = info[0]
    par = lax.rem(j, 2)
    down_rows = ROWS * n
    per_step = SLOTS // n
    @pl.when(j == 0)
    def _():
        grad = attn_grad[...]
        for here, rows in ((me, o_own), (1 - me, o_got)):
            spot = pl.ds(pl.multiple_of(here * HALF, HALF), HALF)
            res_out[spot, :] = mxu(rows[...], grad, TN).astype(bf16)
        for chip in range(SLOTS):
            src = res_out.at[chip * ROWS : (chip + 1) * ROWS, :]
            pltpu.make_async_copy(src, dst.at[info[1 + chip], 0:ROWS, :], sems.at[2]).start()

    res_in[par] = mxu(low[...], ig[...], TN).astype(bf16)
    for chip in range(SLOTS):
        src = res_in.at[par, chip * ROWS : (chip + 1) * ROWS, :]
        spot = pl.ds(pl.multiple_of((1 + j) * ROWS, ROWS), ROWS)
        pltpu.make_async_copy(src, dst.at[info[1 + chip], spot, :], sems.at[par]).start()
    res_down[par] = mxu(act[...], branch[...], TN).astype(bf16)
    for q in range(per_step):
        src = res_down.at[par, q * down_rows : (q + 1) * down_rows, :]
        slot = info[1 + j * per_step + q]
        pltpu.make_async_copy(src, dst.at[slot, ROWS * (1 + n) : ROWS * (1 + 2 * n), :], sems.at[par]).start()

    def settle(which):
        wait_for(res_in.at[which], sems.at[which])
        wait_for(res_down.at[which], sems.at[which])

    @pl.when(j > 0)
    def _():
        settle(1 - par)

    @pl.when(j == n - 1)
    def _():
        settle(par)
        wait_for(res_out, sems.at[2])


def weight_grads(own, info, act, ig, low, branch, o_own, o_got, attn_grad):
    half, ff = act.shape
    n = ff // D
    strip = pl.BlockSpec((half, D), lambda j, *_: (0, j))
    fixed = lambda cols: pl.BlockSpec((half, cols), lambda j, *_: (0, 0))
    at = (lambda info: info[0]) if own else (lambda info: 1 - info[0])
    lanes_of = pl.BlockSpec((half, HALF), lambda j, info: (0, 2 * j + at(info)))
    side = pl.BlockSpec((half, HALF), lambda j, info: (0, at(info)))
    return pl.pallas_call(
        wgrad_body,
        grid_spec=pltpu.PrefetchScalarGridSpec(
            num_scalar_prefetch=1,
            grid=(n,),
            in_specs=[strip, lanes_of, fixed(D), side, fixed(HALF), fixed(HALF), side],
            out_specs=anyspec(),
            scratch_shapes=[
                pltpu.VMEM((2, D, HALF), bf16),
                pltpu.VMEM((2, D, HALF), bf16),
                pltpu.VMEM((D, HALF), bf16),
                pltpu.SemaphoreType.DMA((3,)),
            ],
        ),
        out_shape=shape((SLOTS, ROWS * (1 + 2 * n), HALF)),
        compiler_params=params(),
        cost_estimate=cost(half * D * (D + 2 * ff), half * ff * 8),
    )(info, act, ig, low, branch, o_own, o_got, attn_grad)


def qkv_grad_body(info, small, t_own, t_got, dq, dk, dv, out, t_all, d_all, res, res_small, sems):
    half = t_own.shape[0]
    pltpu.make_async_copy(t_own, t_all.at[0:half, :], sems.at[0]).start()
    pltpu.make_async_copy(t_got, t_all.at[half:, :], sems.at[0]).start()
    for j, src in enumerate((dq, dk, dv)):
        pltpu.make_async_copy(src, d_all.at[j], sems.at[1 + j]).start()
    wait_for(t_all, sems.at[0])
    res_small[...] = small[...].astype(bf16)
    row = lax.broadcasted_iota(jnp.int32, (16, HALF), 0)
    for j in range(3):
        wait_for(d_all.at[j], sems.at[1 + j])
        grads = d_all[j]
        res[j] = mxu(t_all[...], grads, TN).astype(bf16)
        for chip in range(SLOTS):
            src = res.at[j, chip * ROWS : (chip + 1) * ROWS, :]
            pltpu.make_async_copy(src, out.at[info[1 + chip], j * ROWS : (j + 1) * ROWS, :], sems.at[4]).start()
        if j != 1:
            total = jnp.sum(grads.astype(f32), axis=0, keepdims=True)
            place = 14 if j == 0 else 15
            res_small[...] = jnp.where(row == place, total, res_small[...].astype(f32)).astype(bf16)
    for slot in range(SLOTS):
        pltpu.make_async_copy(res_small, out.at[slot, 3 * ROWS : 3 * ROWS + 16, :], sems.at[5]).start()
    wait_for(res, sems.at[4])
    for slot in range(SLOTS):
        pltpu.make_async_copy(res_small, out.at[slot, 3 * ROWS : 3 * ROWS + 16, :], sems.at[5]).wait()


def qkv_grads(info, small, t_own, t_got, dq, dk, dv):
    total = dq.shape[0]
    return pl.pallas_call(
        qkv_grad_body,
        grid_spec=pltpu.PrefetchScalarGridSpec(
            num_scalar_prefetch=1,
            grid=(),
            in_specs=[pl.BlockSpec(memory_space=pltpu.VMEM)] + [anyspec()] * 5,
            out_specs=anyspec(),
            scratch_shapes=[
                pltpu.VMEM((total, D), bf16),
                pltpu.VMEM((3, total, HALF), bf16),
                pltpu.VMEM((3, D, HALF), bf16),
                pltpu.VMEM((16, HALF), bf16),
                pltpu.SemaphoreType.DMA((6,)),
            ],
        ),
        out_shape=shape((SLOTS, 3 * ROWS + 16, HALF)),
        compiler_params=pltpu.CompilerParams(vmem_limit_bytes=VMEM_CAP),
        cost_estimate=cost(total * D * HALF * 6, total * D * 5),
    )(info, small, t_own, t_got, dq, dk, dv)


def input_back_body(*refs):
    w = refs[0]
    dq, dk, dv = refs[1:4]
    out = refs[-1]
    total = None
    for j, part in enumerate((dq, dk, dv)):
        add = mxu(part[...], w[:, j * HALF : (j + 1) * HALF], NT)
        total = add if total is None else total + add
    for extra in refs[4:-1]:
        total = total + extra[...].astype(f32)
    out[...] = total.astype(bf16)


def input_back(w, dq, dk, dv, far, extras):
    half = dq.shape[0] // 2
    tile = 512
    base = half // tile if far else 0
    part = pl.BlockSpec((tile, HALF), lambda i: (base + i, 0))
    row = pl.BlockSpec((tile, D), lambda i: (i, 0))
    return pl.pallas_call(
        input_back_body,
        grid=(half // tile,),
        in_specs=[pl.BlockSpec((D, 3 * HALF), lambda i: (0, 0)), part, part, part] + [row] * len(extras),
        out_specs=row,
        out_shape=shape((half, D)),
        compiler_params=params(),
        cost_estimate=cost(half * D * HALF * 6, half * D * 8),
    )(w, dq, dk, dv, *extras)


def shift(n, k):
    return [(i, (i + k) % n) for i in range(n)]


class Plan:
    def __init__(self, seq, fsdp):
        rest = fsdp // 2
        dims = []
        while rest > 1:
            want = 4 if len(dims) % 2 == 0 and rest % 4 == 0 else 2
            dims.append(want)
            rest //= want
        self.dims = [seq] + dims + [2]
        self.names = ["s"] + ["r%d" % i for i in range(len(dims))] + ["c"]
        self.chips = seq * fsdp // 2
        self.direct = self.dims == [2, 4, 2, 2]
        self.stages = ([1] if dims else []) + [0] + list(range(2, len(dims) + 1))

    def at(self, a):
        return lax.axis_index(self.names[a])

    def coords(self):
        return [self.at(a) for a in range(len(self.dims))]

    def chip_table(self, sign, spot):
        if not self.direct:
            return jnp.arange(SLOTS, dtype=jnp.int32)
        spots = []
        for dx, dy in ((0, 0), (1, 0), (0, 1), (1, 1)):
            spots += [(dx, dy, z) for z in range(4)]
        dx, dy, dz = (jnp.asarray(v, jnp.int32) for v in zip(*spots))
        return ((spot[0] + sign * dx) % 2) * 8 + ((spot[1] + sign * dz) % 4) * 2 + (spot[2] + sign * dy) % 2

    def slot_table(self, sign, spot):
        table = self.chip_table(sign, spot)
        hit = table[:, None] == jnp.arange(SLOTS, dtype=jnp.int32)[None, :]
        return jnp.sum(jnp.where(hit, jnp.arange(SLOTS, dtype=jnp.int32)[:, None], 0), axis=0)

    def places(self, sign):
        grid = np.indices(self.dims[:-1]).reshape(len(self.dims) - 1, -1)
        flat = jnp.zeros((self.chips,), jnp.int32)
        if sign < 0:
            for a in reversed(self.stages):
                n = self.dims[a]
                flat = flat * n + (self.at(a) - jnp.asarray(grid[a], jnp.int32)) % n
            return flat
        sizes = [self.dims[a] for a in reversed(self.stages)]
        offs = np.indices(sizes).reshape(len(sizes), -1)
        by_axis = {a: offs[j] for j, a in enumerate(reversed(self.stages))}
        for a in range(len(self.dims) - 1):
            n = self.dims[a]
            flat = flat * n + (self.at(a) + jnp.asarray(by_axis[a], jnp.int32)) % n
        return flat

    def send(self, x, a, k=1):
        return lax.ppermute(x, self.names[a], shift(self.dims[a], k))


def gather_chips(plan, unit):
    buf = unit[None]
    for a in plan.stages:
        n = plan.dims[a]
        if n > 1:
            buf = jnp.concatenate([buf] + [plan.send(buf, a, k) for k in range(1, n)], axis=0)
    return jnp.take(buf, plan.places(-1), axis=0, mode="clip")


def reduce_chips(plan, grads):
    buf = jnp.take(grads, plan.places(1), axis=0, mode="clip")
    for a in reversed(plan.stages):
        n = plan.dims[a]
        size = buf.shape[0] // n
        keep = buf[:size].astype(f32)
        for k in range(1, n):
            keep = keep + plan.send(buf[k * size : (k + 1) * size].astype(bf16), a, k).astype(f32)
        buf = keep if a == plan.stages[0] else keep.astype(bf16)
    return buf[0]


def regroup(buf, sizes, count):
    n, _, w = buf.shape
    parts = []
    at = 0
    for size in sizes:
        parts.append(buf[:, at : at + size].reshape(count, n * size // count, w))
        at += size
    return jnp.concatenate(parts, axis=1)


def gather_z(plan, unit):
    return jnp.concatenate([unit[None]] + [plan.send(unit, 1, k)[None] for k in range(1, 4)], axis=0)


def swap_pair(x):
    return lax.ppermute(x, "c", [(0, 1), (1, 0)])


def cross(x):
    return lax.ppermute(x, ("s", "c"), [(1, 2), (2, 1)])


def together(*values):
    return lax.optimization_barrier(values)


def half_of(x, at):
    return lax.dynamic_slice_in_dim(x, at * HALF, HALF, axis=x.ndim - 1)


def chip_units(me, mine, got, sizes):
    low = jnp.where(me == 0, mine, got)
    high = jnp.where(me == 0, got, mine)
    parts = []
    at = 0
    for size in sizes:
        parts += [low[at : at + size], high[at : at + size]]
        at += size
    return jnp.concatenate(parts, axis=0)


def own_rows(me, total, sizes):
    first, second = [], []
    at = 0
    for size in sizes:
        first.append(total[at : at + size])
        second.append(total[at + size : at + 2 * size])
        at += 2 * size
    first = jnp.concatenate(first, axis=0)
    second = jnp.concatenate(second, axis=0)
    return jnp.where(me == 0, first, second), jnp.where(me == 0, second, first)


def local(plan, tokens, lengths, block_order, qkv_weight, query_bias, value_bias, out_weight, out_bias,
          norm1_gain, norm1_shift, in_weight, in_bias, down_weight, down_bias, norm2_gain, norm2_shift, cotangent):
    half = tokens.shape[1]
    me = plan.at(len(plan.dims) - 1)
    stays = plan.at(0) == me
    rows_dev = qkv_weight.shape[0]
    ff_dev = down_weight.shape[0]
    ff_cols = in_weight.shape[1] // D

    def tables(spot):
        core = spot[-1].astype(jnp.int32)[None]
        same = (spot[0] == spot[-1]).astype(jnp.int32)[None]
        return (jnp.concatenate([core, plan.chip_table(-1, spot), same]),
                jnp.concatenate([core, plan.slot_table(1, spot)]), jnp.concatenate([core, plan.slot_table(-1, spot)]))

    sizes1 = [rows_dev] * 3
    sizes2 = [rows_dev] * (1 + ff_cols) + [ff_dev]
    smalls = (query_bias, value_bias, out_bias, norm1_gain, norm1_shift, in_bias, down_bias, norm2_gain, norm2_shift)
    unit_rows = 2 * half // UNITS

    def stacked(vectors):
        bias_o, gain1, shift1, wide, bias_d, gain2, shift2 = vectors[2:]
        zero = jnp.zeros((D,), f32)
        return jnp.stack([bias_o, gain1, shift1, bias_d, gain2, shift2, zero, zero]), wide[None]

    def settle_rows(x, got):
        return jnp.where(stays, x, got)

    tok = settle_rows(tokens[0], cross(tokens[0]))
    tok_got = swap_pair(tok)
    if plan.direct:
        lines = [v[None] for v in smalls] + [lengths, block_order]
        slab = (5 + 2 * ff_cols, rows_dev, HALF)
        mine, give = whole_call(pack_body, (slab, slab), qkv_weight, out_weight, in_weight,
                                down_weight.reshape(ff_cols, rows_dev, D), *lines)
        got = swap_pair(give)
        unit1, unit2 = whole_call(combine_body, ((7, rows_dev, HALF), (2 + 4 * ff_cols, rows_dev, HALF)), mine, got)
        unit1 = unit1.reshape(7 * rows_dev, HALF)
        unit2 = unit2.reshape(-1, HALF)
        other = got[3, len(smalls) : len(smalls) + 2, :UNITS].astype(jnp.int32)
        counts_here = jnp.where(stays, lengths[0], other[0]) // unit_rows
        order_here = jnp.where(stays, block_order[0], other[1])

        z1 = gather_z(plan, unit1)
        unit2, z1 = together(unit2, z1)
        x1, y1 = plan.send(z1, 0), plan.send(z1, 2)
        tok, unit2, *spot = together(tok, unit2, *plan.coords())
        z2_parts = [unit2] + [plan.send(unit2, 1, k) for k in range(1, 4)]
        pull, push, find = tables(spot)
        cot, x1, y1, tok, pull, find = together(cotangent[0], x1, y1, tok, pull, find)
        d1a, d1b = plan.send(y1[0:2], 0), plan.send(x1[2:4], 2)
        cot_got = cross(cot)
        pieces1 = [z1, x1, y1, d1a, d1b]
        table = small_table(find, pieces1).reshape(plan.chips, 16, 2, 128)

        def vectors_of(table):
            return [table[:, i, :, : v.shape[0]].reshape(-1).astype(f32) for i, v in enumerate(smalls)]

        vectors = vectors_of(table)
    else:
        pull, push, _ = tables(plan.coords())
        first = jnp.concatenate([qkv_weight[:, j * D : (j + 1) * D] for j in range(3)], axis=0)
        second = jnp.concatenate([out_weight] + [in_weight[:, j * D : (j + 1) * D] for j in range(ff_cols)] + [down_weight], axis=0)
        line = jnp.concatenate(smalls)
        both = jnp.concatenate([first, second], axis=0)
        got = swap_pair(half_of(both, 1 - me))
        mine = half_of(both, me)
        cut = 3 * rows_dev
        unit1 = chip_units(me, mine[:cut], got[:cut], sizes1)
        unit2 = chip_units(me, mine[cut:], got[cut:], sizes2)
        line_got = swap_pair(line)
        line_unit = jnp.stack([jnp.where(me == 0, line, line_got), jnp.where(me == 0, line_got, line)])
        pieces1 = [regroup(gather_chips(plan, unit1), [2 * r for r in sizes1], SLOTS)]
        pieces2 = [regroup(gather_chips(plan, unit2), [2 * r for r in sizes2], SLOTS)]
        far2 = [swap_pair(p) for p in pieces2]
        lines = gather_chips(plan, line_unit).reshape(2 * plan.chips, line.shape[0])
        vectors = []
        at = 0
        for piece in smalls:
            size = piece.shape[0]
            vectors.append(lines[:, at : at + size].reshape(2 * plan.chips * size).astype(f32))
            at += size
        counts_here = jnp.where(stays, lengths[0], swap_pair(lengths[0])) // unit_rows
        order_here = jnp.where(stays, block_order[0], swap_pair(block_order[0]))
        cot_got = cross(cotangent[0])
    bias_q, bias_v = vectors[:2]
    bias_qkv = jnp.concatenate([half_of(bias_q, me), jnp.zeros((HALF,), f32), half_of(bias_v, me)])[None]

    spot = jnp.arange(UNITS)
    ends = jnp.sum(jnp.where(spot[None, :] <= spot[:, None], counts_here[None, :], 0), axis=1)
    seg_packed = jnp.sum((spot[:, None] >= ends[None, :]).astype(jnp.int32), axis=1)
    hit = order_here[:, None] == spot[None, :]
    segs = jnp.sum(jnp.where(hit, seg_packed[:, None], 0), axis=0)
    segs = jnp.where(me == 0, segs, jnp.roll(segs, UNITS // 2))

    qkv, w_qkv = project(pull, tok, tok_got, bias_qkv, pieces1)
    if plan.direct:
        *z2_parts, table, qkv = together(*z2_parts, table, qkv)
        vectors = vectors_of(table)
        z2 = jnp.stack(z2_parts)
        x2, y2 = plan.send(z2, 0), plan.send(z2, 2)
        z2_far = swap_pair(z2)
        att = attention(segs, qkv, 0, 2, None)
        vecs, gate_bias = stacked(vectors)
        x2, y2, cot_got, vecs, gate_bias, push, *att = together(x2, y2, cot_got, vecs, gate_bias, push, *att)
        d2a, d2b = plan.send(y2[0:2], 0), plan.send(x2[2:4], 2)
        x2_far, y2_far = swap_pair(x2), swap_pair(y2)
    else:
        att = attention(segs, qkv, 0, 2, None)
        vecs, gate_bias = stacked(vectors)
    o_own, o_far, lse = attention(segs, qkv, 2, PAIRS - 2, att)
    o_got = swap_pair(o_far)
    if plan.direct:
        pieces2 = [z2, x2, y2, d2a, d2b]
        far2 = [z2_far, x2_far, y2_far, swap_pair(d2a), swap_pair(d2b)]
    (out_rows, act, ig, low, branch, attn_grad, resid1, d_own, d_far, sums) = middle(
        pull, tok, o_own, o_got, cotangent[0], cot_got, vecs, gate_bias, pieces2, far2)
    d_got = swap_pair(d_far)
    out_got = cross(out_rows)
    sum_got = swap_pair(half_of(sums, 1 - me))
    grad_args = (low, branch, o_own, o_got)
    give = weight_grads(False, push, act, ig, *grad_args, attn_grad)
    give, attn_grad = together(give, attn_grad)
    got_g = swap_pair(give)
    keep = weight_grads(True, push, act, ig, *grad_args, attn_grad)
    back_args = (o_own, o_far, d_own, d_got, lse)
    if plan.direct:

        def both_sums(lo, hi):
            return keep[lo:hi].astype(f32) + got_g[lo:hi].astype(f32)

        def late(rows):
            return jnp.pad(rows.astype(f32), ((2, 0), (0, 0), (0, 0)))

        def early(rows):
            return jnp.pad(rows.astype(f32), ((0, 2), (0, 0), (0, 0)))

        sx, sy, qkv_back, out_got = together(both_sums(12, 14).astype(bf16), both_sums(14, 16).astype(bf16), qkv, out_got)
        rx, ry = plan.send(sx, 0), plan.send(sy, 2)
        g = attention_back(segs, qkv_back, *back_args, 0, 1, None)
        rx, ry, sum_got, *g = together(rx, ry, sum_got, *g)
        send_x = (both_sums(4, 8) + late(ry)).astype(bf16)
        send_y = (both_sums(8, 12) + early(rx)).astype(bf16)
        send_x, send_y, *g = together(send_x, send_y, *g)
        px, py = plan.send(send_x, 0), plan.send(send_y, 2)
        g = attention_back(segs, qkv_back, *back_args, 1, 1, g)
        px, py, *g = together(px, py, *g)
        z_sum = both_sums(0, 4) + px.astype(f32) + py.astype(f32)
        z_low, ffn, *g = together(z_sum[1:].astype(bf16), z_sum[0], *g)
        z_got = [plan.send(z_low[k - 1], 1, k) for k in range(1, 4)]
        g = attention_back(segs, qkv_back, *back_args, 2, PAIRS - 2, g)
        *z_got, dq, dk, dv = together(*z_got, *g)
        for part in z_got:
            ffn = ffn + part.astype(f32)
    else:
        dq, dk, dv = attention_back(segs, qkv, *back_args, 0, PAIRS, None)
        summed = (keep.astype(f32) + got_g.astype(f32)).astype(bf16)
        scale = plan.chips // SLOTS
        units = regroup_back(summed, [ROWS] * (1 + ff_cols) + [ROWS * ff_cols], scale)
        ffn = reduce_chips(plan, units)
    small = half_of(sums, me) + sum_got
    tail = qkv_grads(push, small, tok, tok_got, dq, dk, dv)
    if plan.direct:
        rx, ry = plan.send(tail[12:14], 0), plan.send(tail[14:16], 2)
        far_back = input_back(w_qkv, dq, dk, dv, True, ())
        rx, ry, far_back = together(rx, ry, far_back)
        far_back = swap_pair(far_back)
        send_x = (tail[4:8].astype(f32) + late(ry)).astype(bf16)
        send_y = (tail[8:12].astype(f32) + early(rx)).astype(bf16)
        px, py = plan.send(send_x, 0), plan.send(send_y, 2)
        packed = input_back(w_qkv, dq, dk, dv, False, (resid1, far_back))
        px, py, packed = together(px, py, packed)
        packed_got = cross(packed)
        z_sum = tail[0:4].astype(f32) + px.astype(f32) + py.astype(f32)
        z_low, out_got = together(z_sum[1:].astype(bf16), out_got)
        qkv_sum = z_sum[0]
        output = settle_rows(out_rows, out_got)
        packed_got, output, *z_got = together(packed_got, output, *[plan.send(z_low[k - 1], 1, k) for k in range(1, 4)])
        for part in z_got:
            qkv_sum = qkv_sum + part.astype(f32)
    else:
        far_back = swap_pair(input_back(w_qkv, dq, dk, dv, True, ()))
        packed = input_back(w_qkv, dq, dk, dv, False, (resid1, far_back))
        packed_got = cross(packed)
        output = settle_rows(out_rows, out_got)
        units = regroup_back(tail[:, : 3 * ROWS], [ROWS] * 3, scale)
        extra = jnp.broadcast_to(tail[0:1, 3 * ROWS :], (plan.chips, 16, HALF))
        qkv_sum = reduce_chips(plan, jnp.concatenate([units, extra], axis=1))
    small_sum = qkv_sum[6 * rows_dev :]
    sizes = sizes1 + sizes2
    total = jnp.concatenate([qkv_sum[: 6 * rows_dev], ffn], axis=0)
    mine, other = own_rows(me, total, sizes)
    got = swap_pair(jnp.concatenate([other, small_sum], axis=0))
    count = mine.shape[0]
    mine = jnp.concatenate([mine, small_sum], axis=0)
    full = jnp.concatenate([jnp.where(me == 0, mine, got), jnp.where(me == 0, got, mine)], axis=1)
    take = lambda at, size: full[at : at + size]
    out_qkv = jnp.concatenate([take(j * rows_dev, rows_dev) for j in range(3)], axis=1)
    out_out = take(3 * rows_dev, rows_dev)
    out_in = jnp.concatenate([take((4 + j) * rows_dev, rows_dev) for j in range(ff_cols)], axis=1)
    out_down = take((4 + ff_cols) * rows_dev, ff_dev)
    small_full = full[count:]
    device = plan.at(0)
    for a in range(1, len(plan.dims)):
        device = device * plan.dims[a] + plan.at(a)
    order = (14, 15, 0, 1, 2, 3, 3 + ff_cols, 4 + ff_cols, 5 + ff_cols)
    wide_row = 3
    thin = lax.dynamic_slice_in_dim(small_full, device * rows_dev, rows_dev, axis=1)
    span = small_full[wide_row : wide_row + ff_cols].reshape(-1)
    s = [lax.dynamic_slice_in_dim(span, device * ff_dev, ff_dev) if row == wide_row and piece is in_bias else thin[row]
         for piece, row in zip(smalls, order)]
    input_grad = settle_rows(packed, packed_got)
    return (output[None], input_grad[None], out_qkv, s[0], s[1], out_out, s[2], s[3], s[4], out_in, s[5], out_down, s[6], s[7], s[8])


def regroup_back(buf, sizes, scale):
    n, _, w = buf.shape
    parts = []
    at = 0
    for size in sizes:
        parts.append(buf[:, at : at + size].reshape(n * scale, size // scale, w))
        at += size
    return jnp.concatenate(parts, axis=1)


def solution(mesh):
    plan = Plan(mesh.shape["seq"], mesh.shape["fsdp"])
    inner_mesh = Mesh(mesh.devices.reshape(plan.dims), tuple(plan.names))
    groups = tuple(plan.names[1:])
    every = tuple(plan.names)
    rows = P(groups, "s", None)
    table = P(groups, None)
    mat = P(every, None)
    vec = P(every)
    placed = (rows, table, table, mat, vec, vec, mat, vec, vec, vec, mat, vec, mat, vec, vec, vec, rows)
    outs = (rows, rows, mat, vec, vec, mat, vec, vec, vec, mat, vec, mat, vec, vec, vec)

    def run(*args):
        return local(plan, *args)

    return jax.shard_map(run, mesh=inner_mesh, in_specs=placed, out_specs=outs, check_vma=False)
```

```python
import jax
import jax.numpy as jnp
import numpy as np
from jax import lax
from jax.sharding import Mesh, PartitionSpec as P
from jax.experimental import pallas as pl
from jax.experimental.pallas import tpu as pltpu

D = 768
HALF = D // 2
HD = 64
UNITS = 16
SLOTS = 16
ROWS = D // SLOTS
PAIRS = HALF // 128
LOG2E = 1.4426950408889634
LN2 = 0.6931471805599453
BIG = 1e30
TQ = 1024
TQ_BACK = 512
STEP = 256
STEP_BACK = 1024
TM = 512
norm_eps = 1e-12
bf16 = jnp.bfloat16
f32 = jnp.float32
NT = (((1,), (1,)), ((), ()))
NN = (((1,), (0,)), ((), ()))
TN = (((0,), (0,)), ((), ()))
VMEM_CAP = 58 << 20


def mxu(a, b, dims=NN):
    return lax.dot_general(a, b, dims, preferred_element_type=f32)


def shape(size, kind=bf16):
    return jax.ShapeDtypeStruct(size, kind)


def params(axes=1):
    return pltpu.CompilerParams(dimension_semantics=("arbitrary",) * axes, vmem_limit_bytes=VMEM_CAP)


def cost(flops, moved):
    return pl.CostEstimate(flops=int(flops), bytes_accessed=int(moved), transcendentals=0)


def tie(value, *others):
    return lax.optimization_barrier((value,) + others)[0]


def lanes(rows):
    return lax.broadcasted_iota(jnp.int32, (rows, 128), 1)


def seg_rows(segs_ref, base_block, rows):
    place = lax.broadcasted_iota(jnp.int32, (rows, 128), 0)
    out = jnp.zeros((rows, 128), jnp.int32)
    for b in range(rows // 128):
        out = jnp.where(place >= b * 128, segs_ref[base_block + b], out)
    return out


def split3(v):
    hi = v.astype(bf16).astype(f32)
    mid = (v - hi).astype(bf16).astype(f32)
    return hi, mid, v - hi - mid


def both_heads(pair_rows):
    lane = lanes(pair_rows.shape[0])
    zero = jnp.zeros_like(pair_rows)
    first = jnp.where(lane < HD, pair_rows, zero)
    return jnp.concatenate([first, jnp.where(lane < HD, zero, pair_rows)], axis=0)


def fill_keys(segs_ref, k_in, v_in, k_aug, v_aug):
    for at in range(0, k_in.shape[0], STEP):
        rows = slice(at, at + STEP)
        lane = lanes(STEP)
        hot = (lane == seg_rows(segs_ref, at // 128, STEP)) | ((lane >= 64) & (lane < 67))
        k_aug[rows, :128] = k_in[rows, :]
        k_aug[rows, 128:] = jnp.where(hot, 1.0, 0.0).astype(bf16)
        v_aug[rows, :128] = v_in[rows, :]
        v_aug[rows, 128:] = jnp.ones((STEP, 128), bf16)


def attend_body(segs_ref, q_in, k_in, v_in, *refs):
    o_own, o_far, lse_ref, k_aug, v_aug = refs[-5:]
    i = pl.program_id(1)
    n_half = pl.num_programs(1) // 2

    @pl.when(i == 0)
    def _():
        fill_keys(segs_ref, k_in, v_in, k_aug, v_aug)

    lane = lanes(TQ)
    seg = seg_rows(segs_ref, i * (TQ // 128), TQ)
    off = jnp.where((lane < 16) & (lane != seg), -BIG, 0.0).astype(bf16)
    q_aug = jnp.concatenate([both_heads(q_in[...]), jnp.concatenate([off, off], axis=0)], axis=1)
    top = None
    acc = None
    for at in range(0, k_aug.shape[0], STEP):
        s = mxu(q_aug, k_aug[at : at + STEP, :], NT)
        here = jnp.max(s, axis=1, keepdims=True)
        new_top = here if top is None else jnp.maximum(top, here)
        p = jnp.exp2(s - new_top).astype(bf16)
        add = mxu(p, v_aug[at : at + STEP, :])
        acc = add if acc is None else acc * jnp.exp2(top - new_top) + add
        top = new_top
    both = jnp.where(lane < HD, acc[:TQ, :128], acc[TQ:, :128])
    sums = jnp.where(lane < HD, acc[:TQ, 128:], acc[TQ:, 128:])
    tops = jnp.where(lane < HD, top[:TQ], top[TQ:])
    out = (both / sums).astype(bf16)
    lse_ref[...] = tops + jnp.log2(sums)

    @pl.when(i < n_half)
    def _():
        o_own[...] = out

    @pl.when(i >= n_half)
    def _():
        o_far[...] = out


def anyspec():
    return pl.BlockSpec(memory_space=pl.ANY)


def pair_specs(n_half, first, rows):
    own = pl.BlockSpec((rows, 128), lambda h, i, *_: (jnp.minimum(i, n_half - 1), first + h))
    far = pl.BlockSpec((rows, 128), lambda h, i, *_: (jnp.maximum(i - n_half, 0), first + h))
    return own, far


def attention(segs, qkv, first, count, prev):
    total = qkv.shape[0]
    half = total // 2
    n_half = half // TQ
    own, far = pair_specs(n_half, first, TQ)
    row = pl.BlockSpec((TQ, 128), lambda h, i, *_: (i, first + h))
    whole = lambda part: pl.BlockSpec((total, 128), lambda h, i, *_: (0, part * PAIRS + first + h))
    prev = () if prev is None else tuple(prev)
    return pl.pallas_call(
        attend_body,
        grid_spec=pltpu.PrefetchScalarGridSpec(
            num_scalar_prefetch=1,
            grid=(count, 2 * n_half),
            in_specs=[row, whole(1), whole(2)] + [anyspec()] * len(prev),
            out_specs=[own, far, row],
            scratch_shapes=[pltpu.VMEM((total, 256), bf16), pltpu.VMEM((total, 256), bf16)],
        ),
        out_shape=[shape((half, HALF)), shape((half, HALF)), shape((total, HALF), f32)],
        input_output_aliases={4 + j: j for j in range(len(prev))},
        compiler_params=params(2),
        cost_estimate=cost(count * total * total * 2048, total * 128 * 2 * 8),
    )(segs, qkv, qkv, qkv, *prev)


def attend_back_body(segs_ref, q_in, k_in, v_in, o_own, o_far, d_own, d_far, lse_ref, *refs):
    dq_out, dk_out, dv_out, k_aug, v_aug, dk_acc, dv_acc, k_turn = refs[-8:]
    i = pl.program_id(1)
    n = pl.num_programs(1)

    @pl.when(i == 0)
    def _():
        fill_keys(segs_ref, k_in, v_in, k_aug, v_aug)
        k_turn[...] = k_in[...].T
        dk_acc[...] = jnp.zeros_like(dk_acc)
        dv_acc[...] = jnp.zeros_like(dv_acc)

    near = i < n // 2
    d_rows = jnp.where(near, d_own[...], d_far[...])
    o_rows = jnp.where(near, o_own[...], o_far[...])
    lane = lanes(TQ_BACK)
    seg = seg_rows(segs_ref, i * (TQ_BACK // 128), TQ_BACK)
    off = jnp.where((lane < 16) & (lane != seg), -BIG, 0.0)
    prod = d_rows.astype(f32) * o_rows.astype(f32)
    q_side, d_side = [], []
    for head in range(2):
        mine = (lane < HD) if head == 0 else (lane >= HD)
        dot_row = jnp.sum(jnp.where(mine, prod, 0.0), axis=1, keepdims=True)
        lse = jnp.broadcast_to(lse_ref[:, head * HD : head * HD + 1], (TQ_BACK, 128))
        for side, value, rest in ((q_side, -lse, off), (d_side, -jnp.broadcast_to(dot_row, (TQ_BACK, 128)), 0.0)):
            h, m, l = split3(value)
            cols = jnp.where(lane == 64, h, jnp.where(lane == 65, m, jnp.where(lane == 66, l, rest)))
            side.append(cols.astype(bf16))
    q2 = both_heads(q_in[...])
    d2 = both_heads(d_rows)
    q_aug = jnp.concatenate([q2, jnp.concatenate(q_side, axis=0)], axis=1)
    d_aug = jnp.concatenate([d2, jnp.concatenate(d_side, axis=0)], axis=1)
    dq = None
    for at in range(0, k_aug.shape[0], STEP_BACK):
        rows = slice(at, at + STEP_BACK)
        p = jnp.exp2(mxu(k_aug[rows, :], q_aug, NT))
        ds = (p * mxu(v_aug[rows, :], d_aug, NT)).astype(bf16)
        dv_acc[rows, :] += mxu(p.astype(bf16), d2)
        dk_acc[rows, :] += mxu(ds, q2)
        add = mxu(k_turn[:, rows], ds)
        dq = add if dq is None else dq + add
    dq = jnp.concatenate([dq[:HD, :TQ_BACK], dq[HD:, TQ_BACK:]], axis=0) * (HD ** -0.5)
    dq_out[...] = dq.T.astype(bf16)

    @pl.when(i == n - 1)
    def _():
        dk_out[...] = (dk_acc[...] * LN2).astype(bf16)
        dv_out[...] = dv_acc[...].astype(bf16)


def attention_back(segs, qkv, o_own, o_far, d_own, d_far, lse, first, count, prev):
    total = qkv.shape[0]
    half = total // 2
    n_half = half // TQ_BACK
    own, far = pair_specs(n_half, first, TQ_BACK)
    row = pl.BlockSpec((TQ_BACK, 128), lambda h, i, *_: (i, first + h))
    whole = lambda part: pl.BlockSpec((total, 128), lambda h, i, *_: (0, part * PAIRS + first + h))
    prev = () if prev is None else tuple(prev)
    return pl.pallas_call(
        attend_back_body,
        grid_spec=pltpu.PrefetchScalarGridSpec(
            num_scalar_prefetch=1,
            grid=(count, 2 * n_half),
            in_specs=[row, whole(1), whole(2), own, far, own, far, row] + [anyspec()] * len(prev),
            out_specs=[row, whole(0), whole(0)],
            scratch_shapes=[
                pltpu.VMEM((total, 256), bf16),
                pltpu.VMEM((total, 256), bf16),
                pltpu.VMEM((total, 128), f32),
                pltpu.VMEM((total, 128), f32),
                pltpu.VMEM((128, total), bf16),
            ],
        ),
        out_shape=[shape((total, HALF))] * 3,
        input_output_aliases={9 + j: j for j in range(len(prev))},
        compiler_params=params(2),
        cost_estimate=cost(count * total * total * 5120, total * 128 * 2 * 12),
    )(segs, qkv, qkv, qkv, o_own, o_far, d_own, d_far, lse, *prev)


def pack_body(qkv, w_out, w_in, w_down, *refs):
    lines, (mine, give) = refs[:-2], refs[-2:]
    me = lax.axis_index("c")
    for half_at, dst in ((me, mine), (1 - me, give)):
        slab = 0

        def cols(base):
            return pl.ds(pl.multiple_of(base + half_at * HALF, 128), HALF)

        for j in range(3):
            dst[slab] = qkv[:, cols(j * D)]
            slab += 1
        dst[slab] = jnp.zeros(dst.shape[1:], bf16)
        for i, line in enumerate(lines):
            value = line[...].astype(f32)
            dst[slab, i : i + 1, 0 : value.shape[1]] = value.astype(bf16)
        dst[slab + 1] = w_out[:, cols(0)]
        slab += 2
        for j in range(w_in.shape[1] // D):
            dst[slab] = w_in[:, cols(j * D)]
            slab += 1
        for j in range(w_down.shape[0]):
            dst[slab] = w_down[j, :, cols(0)]
            slab += 1


def combine_body(mine, got, unit1, unit2):
    me = lax.axis_index("c")
    n = unit2.shape[0] // 2
    wide = n // 2
    unit1[6] = jnp.zeros(unit1.shape[1:], bf16)
    for at, src in ((me, mine), (1 - me, got)):
        for j in range(3):
            unit1[2 * j + at] = src[j]
        for j in range(wide + 1):
            unit2[2 * j + at] = src[4 + j]
        for j in range(wide):
            unit2[2 * (wide + 1) + at * wide + j] = src[5 + wide + j]
    unit1[6, :, 0:128] = mine[3, :, 0:128]
    unit1[6, :, 128:256] = got[3, :, 0:128]


def whole_call(body, outs, *args):
    return pl.pallas_call(
        body,
        in_specs=[pl.BlockSpec(memory_space=pltpu.VMEM)] * len(args),
        out_specs=[pl.BlockSpec(memory_space=pltpu.VMEM)] * len(outs),
        out_shape=[shape(o) for o in outs],
        cost_estimate=cost(0, 2 << 20),
    )(*args)


def each_slot(pieces):
    at = 0
    for ref in pieces:
        for slot in range(ref.shape[0]):
            yield at, ref, slot
            at += 1


def wait_for(dst, sem):
    pltpu.make_async_copy(dst, dst, sem).wait()


def proj_body(info, t_own, t_got, bias, *refs):
    pieces, (out, w_out, w, sem) = refs[:-4], refs[-4:]
    i = pl.program_id(0)

    @pl.when(i == 0)
    def _():
        for at, ref, slot in each_slot(pieces):
            rows = pl.ds(pl.multiple_of(info[1 + at] * ROWS, ROWS), ROWS)
            for j in range(3):
                src = ref.at[slot, j * ROWS : (j + 1) * ROWS, :]
                pltpu.make_async_copy(src, w.at[rows, j * HALF : (j + 1) * HALF], sem).start()
        wait_for(w, sem)

    tile = jnp.where(i < pl.num_programs(0) // 2, t_own[...], t_got[...])
    for j in range(3):
        cols = slice(j * HALF, (j + 1) * HALF)
        part = mxu(tile, w[:, cols]) + bias[0:1, cols]
        if j == 0:
            part = part * (LOG2E * HD ** -0.5)
        out[:, cols] = part.astype(bf16)
    w_out[...] = w[...]


def project(info, t_own, t_got, bias, pieces):
    half = t_own.shape[0]
    tile = 512
    n_half = half // tile
    own = pl.BlockSpec((tile, D), lambda i, *_: (jnp.minimum(i, n_half - 1), 0))
    got = pl.BlockSpec((tile, D), lambda i, *_: (jnp.maximum(i - n_half, 0), 0))
    return pl.pallas_call(
        proj_body,
        grid_spec=pltpu.PrefetchScalarGridSpec(
            num_scalar_prefetch=1,
            grid=(2 * n_half,),
            in_specs=[own, got, pl.BlockSpec((1, 3 * HALF), lambda i, *_: (0, 0))] + [anyspec()] * len(pieces),
            out_specs=[
                pl.BlockSpec((tile, 3 * HALF), lambda i, *_: (i, 0)),
                pl.BlockSpec((D, 3 * HALF), lambda i, *_: (0, 0)),
            ],
            scratch_shapes=[pltpu.VMEM((D, 3 * HALF), bf16), pltpu.SemaphoreType.DMA],
        ),
        out_shape=[shape((2 * half, 3 * HALF)), shape((D, 3 * HALF))],
        compiler_params=params(),
        cost_estimate=cost(half * D * D * 6, half * D * 12),
    )(info, t_own, t_got, bias, *pieces)


def table_body(info, *refs):
    pieces, (out, held, sem) = refs[:-3], refs[-3:]
    for at, ref, slot in each_slot(pieces):
        src = ref.at[slot, 3 * ROWS : 3 * ROWS + 16, 0:256]
        pltpu.make_async_copy(src, held.at[at], sem).start()
    wait_for(held, sem)
    me = info[0]
    for chip in range(SLOTS):
        rows = held[info[1 + chip]]
        turned = jnp.concatenate([rows[:, 128:], rows[:, :128]], axis=1)
        out[chip] = jnp.where(me == 0, rows, turned)


def small_table(info, pieces):
    return pl.pallas_call(
        table_body,
        grid_spec=pltpu.PrefetchScalarGridSpec(
            num_scalar_prefetch=1,
            grid=(),
            in_specs=[anyspec()] * len(pieces),
            out_specs=pl.BlockSpec(memory_space=pltpu.VMEM),
            scratch_shapes=[pltpu.VMEM((SLOTS, 16, 256), bf16), pltpu.SemaphoreType.DMA],
        ),
        out_shape=shape((SLOTS, 16, 256)),
        cost_estimate=cost(0, 1 << 18),
    )(info, *pieces)


def norm_stats(rows):
    mean = jnp.mean(rows, axis=-1, keepdims=True)
    centered = rows - mean
    var = jnp.mean(centered * centered, axis=-1, keepdims=True)
    rstd = lax.rsqrt(var + norm_eps)
    return centered * rstd, rstd


def norm_back(grad, unit, rstd, gain):
    eg = grad * gain
    mean_eg = jnp.mean(eg, axis=-1, keepdims=True)
    mean_en = jnp.mean(eg * unit, axis=-1, keepdims=True)
    return (eg - mean_eg - unit * mean_en) * rstd


def mid_body(info, tok, o_own, o_got, back, back_got, vecs, bias_in, *refs):
    n_out = 10
    outs, scratch = refs[-n_out - 5 : -5], refs[-5:]
    pieces = refs[: -n_out - 5]
    own_pieces, far_pieces = pieces[: len(pieces) // 2], pieces[len(pieces) // 2 :]
    out_rows, act_out, ig_out, low_out, branch_out, attn_out, resid_out, d_own, d_far, sums = outs
    w_out, w_in, w_down, slope, sems = scratch
    ff_cols = w_in.shape[1] // D
    me = info[0]

    @pl.when(pl.program_id(0) == 0)
    def _():
        for kind in range(3):
            for here, part in ((me, own_pieces), (1 - me, far_pieces)):
                for at, ref, slot in each_slot(part):
                    chip = info[1 + at]
                    lane0 = pl.multiple_of(here * HALF, HALF)
                    rows = pl.ds(pl.multiple_of(chip * ROWS, ROWS), ROWS)
                    if kind == 0:
                        pltpu.make_async_copy(ref.at[slot, 0:ROWS, :], w_out.at[rows, pl.ds(lane0, HALF)], sems.at[0]).start()
                    elif kind == 1:
                        for j in range(ff_cols):
                            src = ref.at[slot, (1 + j) * ROWS : (2 + j) * ROWS, :]
                            dst = w_in.at[rows, pl.ds(pl.multiple_of(lane0 + j * D, HALF), HALF)]
                            pltpu.make_async_copy(src, dst, sems.at[1]).start()
                    else:
                        size = ROWS * ff_cols
                        src = ref.at[slot, (1 + ff_cols) * ROWS : (1 + 2 * ff_cols) * ROWS, :]
                        dst = w_down.at[pl.ds(pl.multiple_of(chip * size, size), size), pl.ds(lane0, HALF)]
                        pltpu.make_async_copy(src, dst, sems.at[2]).start()
        sums[...] = jnp.zeros_like(sums)
        wait_for(w_out, sems.at[0])

    bias_o, gain1, shift1 = vecs[0:1, :], vecs[1:2, :], vecs[2:3, :]
    bias_d, gain2, shift2 = vecs[3:4, :], vecs[4:5, :], vecs[5:6, :]
    mine = w_out[pl.ds(pl.multiple_of(me * HALF, HALF), HALF), :]
    other = w_out[pl.ds(pl.multiple_of((1 - me) * HALF, HALF), HALF), :]
    resid = tok[...].astype(f32) + mxu(o_own[...], mine) + mxu(o_got[...], other) + bias_o
    unit1, rstd1 = norm_stats(resid)
    hidden = unit1 * gain1 + shift1
    low = hidden.astype(bf16)
    low_out[...] = low

    @pl.when(pl.program_id(0) == 0)
    def _():
        wait_for(w_in, sems.at[1])
        wait_for(w_down, sems.at[2])

    branch = bias_d
    for j in range(ff_cols):
        cols = slice(j * D, (j + 1) * D)
        inner = mxu(low, w_in[:, cols]) + bias_in[:, cols]
        phi = 0.5 + 0.5 * lax.erf(inner * (0.5 ** 0.5))
        act = (inner * phi).astype(bf16)
        act_out[:, cols] = act
        slope[:, cols] = phi + inner * (jnp.exp2(inner * inner * (-0.5 * LOG2E)) * 0.3989422804014327)
        branch = branch + mxu(act, w_down[cols, :])
    unit2, rstd2 = norm_stats(hidden + branch)
    out_rows[...] = (unit2 * gain2 + shift2).astype(bf16)
    grad = jnp.where(info[1 + SLOTS] == 1, back[...], back_got[...]).astype(f32)
    resid2 = norm_back(grad, unit2, rstd2, gain2)
    low_branch = resid2.astype(bf16)
    branch_out[...] = low_branch
    hidden_grad = resid2
    for j in range(ff_cols):
        cols = slice(j * D, (j + 1) * D)
        ig = (mxu(low_branch, w_down[cols, :], NT) * slope[:, cols]).astype(bf16)
        ig_out[:, cols] = ig
        hidden_grad = hidden_grad + mxu(ig, w_in[:, cols], NT)
        sums[3 + j : 4 + j, :] += jnp.sum(ig.astype(f32), axis=0, keepdims=True)
    resid1 = norm_back(hidden_grad, unit1, rstd1, gain1)
    resid_out[...] = resid1
    attn_grad = resid1.astype(bf16)
    attn_out[...] = attn_grad
    d_own[...] = mxu(attn_grad, mine, NT).astype(bf16)
    d_far[...] = mxu(attn_grad, other, NT).astype(bf16)
    rows = (
        (0, attn_grad.astype(f32)),
        (1, hidden_grad * unit1),
        (2, hidden_grad),
        (3 + ff_cols, low_branch.astype(f32)),
        (4 + ff_cols, grad * unit2),
        (5 + ff_cols, grad),
    )
    for at, value in rows:
        sums[at : at + 1, :] += jnp.sum(value, axis=0, keepdims=True)


def middle(info, tok, o_own, o_got, back, back_got, vecs, bias_in, own_pieces, far_pieces):
    half = tok.shape[0]
    ff = bias_in.shape[1]
    wide = pl.BlockSpec((TM, D), lambda i, *_: (i, 0))
    thin = pl.BlockSpec((TM, HALF), lambda i, *_: (i, 0))
    full = pl.BlockSpec((TM, ff), lambda i, *_: (i, 0))
    fixed = lambda rows, cols: pl.BlockSpec((rows, cols), lambda i, *_: (0, 0))
    pieces = tuple(own_pieces) + tuple(far_pieces)
    return pl.pallas_call(
        mid_body,
        grid_spec=pltpu.PrefetchScalarGridSpec(
            num_scalar_prefetch=1,
            grid=(half // TM,),
            in_specs=[wide, thin, thin, wide, wide, fixed(8, D), fixed(1, ff)] + [anyspec()] * len(pieces),
            out_specs=[wide, full, full, wide, wide, wide, wide, thin, thin, fixed(16, D)],
            scratch_shapes=[
                pltpu.VMEM((D, D), bf16),
                pltpu.VMEM((D, ff), bf16),
                pltpu.VMEM((ff, D), bf16),
                pltpu.VMEM((TM, ff), f32),
                pltpu.SemaphoreType.DMA((3,)),
            ],
        ),
        out_shape=[
            shape((half, D)),
            shape((half, ff)),
            shape((half, ff)),
            shape((half, D)),
            shape((half, D)),
            shape((half, D)),
            shape((half, D), f32),
            shape((half, HALF)),
            shape((half, HALF)),
            shape((16, D), f32),
        ],
        compiler_params=params(),
        cost_estimate=cost(half * D * (D + 2 * ff) * 4, half * D * 40),
    )(info, tok, o_own, o_got, back, back_got, vecs, bias_in, *pieces)


def wgrad_body(info, act, ig, low, branch, o_own, o_got, attn_grad, dst, res_in, res_down, res_out, sems):
    j = pl.program_id(0)
    n = pl.num_programs(0)
    me = info[0]
    par = lax.rem(j, 2)
    down_rows = ROWS * n
    per_step = SLOTS // n
    @pl.when(j == 0)
    def _():
        grad = attn_grad[...]
        for here, rows in ((me, o_own), (1 - me, o_got)):
            spot = pl.ds(pl.multiple_of(here * HALF, HALF), HALF)
            res_out[spot, :] = mxu(rows[...], grad, TN).astype(bf16)
        for chip in range(SLOTS):
            src = res_out.at[chip * ROWS : (chip + 1) * ROWS, :]
            pltpu.make_async_copy(src, dst.at[info[1 + chip], 0:ROWS, :], sems.at[2]).start()

    res_in[par] = mxu(low[...], ig[...], TN).astype(bf16)
    for chip in range(SLOTS):
        src = res_in.at[par, chip * ROWS : (chip + 1) * ROWS, :]
        spot = pl.ds(pl.multiple_of((1 + j) * ROWS, ROWS), ROWS)
        pltpu.make_async_copy(src, dst.at[info[1 + chip], spot, :], sems.at[par]).start()
    res_down[par] = mxu(act[...], branch[...], TN).astype(bf16)
    for q in range(per_step):
        src = res_down.at[par, q * down_rows : (q + 1) * down_rows, :]
        slot = info[1 + j * per_step + q]
        pltpu.make_async_copy(src, dst.at[slot, ROWS * (1 + n) : ROWS * (1 + 2 * n), :], sems.at[par]).start()

    def settle(which):
        wait_for(res_in.at[which], sems.at[which])
        wait_for(res_down.at[which], sems.at[which])

    @pl.when(j > 0)
    def _():
        settle(1 - par)

    @pl.when(j == n - 1)
    def _():
        settle(par)
        wait_for(res_out, sems.at[2])


def weight_grads(own, info, act, ig, low, branch, o_own, o_got, attn_grad):
    half, ff = act.shape
    n = ff // D
    strip = pl.BlockSpec((half, D), lambda j, *_: (0, j))
    fixed = lambda cols: pl.BlockSpec((half, cols), lambda j, *_: (0, 0))
    at = (lambda info: info[0]) if own else (lambda info: 1 - info[0])
    lanes_of = pl.BlockSpec((half, HALF), lambda j, info: (0, 2 * j + at(info)))
    side = pl.BlockSpec((half, HALF), lambda j, info: (0, at(info)))
    return pl.pallas_call(
        wgrad_body,
        grid_spec=pltpu.PrefetchScalarGridSpec(
            num_scalar_prefetch=1,
            grid=(n,),
            in_specs=[strip, lanes_of, fixed(D), side, fixed(HALF), fixed(HALF), side],
            out_specs=anyspec(),
            scratch_shapes=[
                pltpu.VMEM((2, D, HALF), bf16),
                pltpu.VMEM((2, D, HALF), bf16),
                pltpu.VMEM((D, HALF), bf16),
                pltpu.SemaphoreType.DMA((3,)),
            ],
        ),
        out_shape=shape((SLOTS, ROWS * (1 + 2 * n), HALF)),
        compiler_params=params(),
        cost_estimate=cost(half * D * (D + 2 * ff), half * ff * 8),
    )(info, act, ig, low, branch, o_own, o_got, attn_grad)


def qkv_grad_body(info, small, t_own, t_got, dq, dk, dv, out, t_all, d_all, res, res_small, sems):
    half = t_own.shape[0]
    pltpu.make_async_copy(t_own, t_all.at[0:half, :], sems.at[0]).start()
    pltpu.make_async_copy(t_got, t_all.at[half:, :], sems.at[0]).start()
    for j, src in enumerate((dq, dk, dv)):
        pltpu.make_async_copy(src, d_all.at[j], sems.at[1 + j]).start()
    wait_for(t_all, sems.at[0])
    res_small[...] = small[...].astype(bf16)
    row = lax.broadcasted_iota(jnp.int32, (16, HALF), 0)
    for j in range(3):
        wait_for(d_all.at[j], sems.at[1 + j])
        grads = d_all[j]
        res[j] = mxu(t_all[...], grads, TN).astype(bf16)
        for chip in range(SLOTS):
            src = res.at[j, chip * ROWS : (chip + 1) * ROWS, :]
            pltpu.make_async_copy(src, out.at[info[1 + chip], j * ROWS : (j + 1) * ROWS, :], sems.at[4]).start()
        if j != 1:
            total = jnp.sum(grads.astype(f32), axis=0, keepdims=True)
            place = 14 if j == 0 else 15
            res_small[...] = jnp.where(row == place, total, res_small[...].astype(f32)).astype(bf16)
    for slot in range(SLOTS):
        pltpu.make_async_copy(res_small, out.at[slot, 3 * ROWS : 3 * ROWS + 16, :], sems.at[5]).start()
    wait_for(res, sems.at[4])
    for slot in range(SLOTS):
        pltpu.make_async_copy(res_small, out.at[slot, 3 * ROWS : 3 * ROWS + 16, :], sems.at[5]).wait()


def qkv_grads(info, small, t_own, t_got, dq, dk, dv):
    total = dq.shape[0]
    return pl.pallas_call(
        qkv_grad_body,
        grid_spec=pltpu.PrefetchScalarGridSpec(
            num_scalar_prefetch=1,
            grid=(),
            in_specs=[pl.BlockSpec(memory_space=pltpu.VMEM)] + [anyspec()] * 5,
            out_specs=anyspec(),
            scratch_shapes=[
                pltpu.VMEM((total, D), bf16),
                pltpu.VMEM((3, total, HALF), bf16),
                pltpu.VMEM((3, D, HALF), bf16),
                pltpu.VMEM((16, HALF), bf16),
                pltpu.SemaphoreType.DMA((6,)),
            ],
        ),
        out_shape=shape((SLOTS, 3 * ROWS + 16, HALF)),
        compiler_params=pltpu.CompilerParams(vmem_limit_bytes=VMEM_CAP),
        cost_estimate=cost(total * D * HALF * 6, total * D * 5),
    )(info, small, t_own, t_got, dq, dk, dv)


def input_back_body(*refs):
    w = refs[0]
    dq, dk, dv = refs[1:4]
    out = refs[-1]
    total = None
    for j, part in enumerate((dq, dk, dv)):
        add = mxu(part[...], w[:, j * HALF : (j + 1) * HALF], NT)
        total = add if total is None else total + add
    for extra in refs[4:-1]:
        total = total + extra[...].astype(f32)
    out[...] = total.astype(bf16)


def input_back(w, dq, dk, dv, far, extras):
    half = dq.shape[0] // 2
    tile = 512
    base = half // tile if far else 0
    part = pl.BlockSpec((tile, HALF), lambda i: (base + i, 0))
    row = pl.BlockSpec((tile, D), lambda i: (i, 0))
    return pl.pallas_call(
        input_back_body,
        grid=(half // tile,),
        in_specs=[pl.BlockSpec((D, 3 * HALF), lambda i: (0, 0)), part, part, part] + [row] * len(extras),
        out_specs=row,
        out_shape=shape((half, D)),
        compiler_params=params(),
        cost_estimate=cost(half * D * HALF * 6, half * D * 8),
    )(w, dq, dk, dv, *extras)


def shift(n, k):
    return [(i, (i + k) % n) for i in range(n)]


class Plan:
    def __init__(self, seq, fsdp):
        rest = fsdp // 2
        dims = []
        while rest > 1:
            want = 4 if len(dims) % 2 == 0 and rest % 4 == 0 else 2
            dims.append(want)
            rest //= want
        self.dims = [seq] + dims + [2]
        self.names = ["s"] + ["r%d" % i for i in range(len(dims))] + ["c"]
        self.chips = seq * fsdp // 2
        self.direct = self.dims == [2, 4, 2, 2]
        self.stages = ([1] if dims else []) + [0] + list(range(2, len(dims) + 1))

    def at(self, a):
        return lax.axis_index(self.names[a])

    def coords(self):
        return [self.at(a) for a in range(len(self.dims))]

    def chip_table(self, sign, spot):
        if not self.direct:
            return jnp.arange(SLOTS, dtype=jnp.int32)
        spots = []
        for dx, dy in ((0, 0), (1, 0), (0, 1), (1, 1)):
            spots += [(dx, dy, z) for z in range(4)]
        dx, dy, dz = (jnp.asarray(v, jnp.int32) for v in zip(*spots))
        return ((spot[0] + sign * dx) % 2) * 8 + ((spot[1] + sign * dz) % 4) * 2 + (spot[2] + sign * dy) % 2

    def slot_table(self, sign, spot):
        table = self.chip_table(sign, spot)
        hit = table[:, None] == jnp.arange(SLOTS, dtype=jnp.int32)[None, :]
        return jnp.sum(jnp.where(hit, jnp.arange(SLOTS, dtype=jnp.int32)[:, None], 0), axis=0)

    def places(self, sign):
        grid = np.indices(self.dims[:-1]).reshape(len(self.dims) - 1, -1)
        flat = jnp.zeros((self.chips,), jnp.int32)
        if sign < 0:
            for a in reversed(self.stages):
                n = self.dims[a]
                flat = flat * n + (self.at(a) - jnp.asarray(grid[a], jnp.int32)) % n
            return flat
        sizes = [self.dims[a] for a in reversed(self.stages)]
        offs = np.indices(sizes).reshape(len(sizes), -1)
        by_axis = {a: offs[j] for j, a in enumerate(reversed(self.stages))}
        for a in range(len(self.dims) - 1):
            n = self.dims[a]
            flat = flat * n + (self.at(a) + jnp.asarray(by_axis[a], jnp.int32)) % n
        return flat

    def send(self, x, a, k=1):
        return lax.ppermute(x, self.names[a], shift(self.dims[a], k))


def gather_chips(plan, unit):
    buf = unit[None]
    for a in plan.stages:
        n = plan.dims[a]
        if n > 1:
            buf = jnp.concatenate([buf] + [plan.send(buf, a, k) for k in range(1, n)], axis=0)
    return jnp.take(buf, plan.places(-1), axis=0, mode="clip")


def reduce_chips(plan, grads):
    buf = jnp.take(grads, plan.places(1), axis=0, mode="clip")
    for a in reversed(plan.stages):
        n = plan.dims[a]
        size = buf.shape[0] // n
        keep = buf[:size].astype(f32)
        for k in range(1, n):
            keep = keep + plan.send(buf[k * size : (k + 1) * size].astype(bf16), a, k).astype(f32)
        buf = keep if a == plan.stages[0] else keep.astype(bf16)
    return buf[0]


def regroup(buf, sizes, count):
    n, _, w = buf.shape
    parts = []
    at = 0
    for size in sizes:
        parts.append(buf[:, at : at + size].reshape(count, n * size // count, w))
        at += size
    return jnp.concatenate(parts, axis=1)


def gather_z(plan, unit):
    return jnp.concatenate([unit[None]] + [plan.send(unit, 1, k)[None] for k in range(1, 4)], axis=0)


def swap_pair(x):
    return lax.ppermute(x, "c", [(0, 1), (1, 0)])


def cross(x):
    return lax.ppermute(x, ("s", "c"), [(1, 2), (2, 1)])


def together(*values):
    return lax.optimization_barrier(values)


def half_of(x, at):
    return lax.dynamic_slice_in_dim(x, at * HALF, HALF, axis=x.ndim - 1)


def chip_units(me, mine, got, sizes):
    low = jnp.where(me == 0, mine, got)
    high = jnp.where(me == 0, got, mine)
    parts = []
    at = 0
    for size in sizes:
        parts += [low[at : at + size], high[at : at + size]]
        at += size
    return jnp.concatenate(parts, axis=0)


def own_rows(me, total, sizes):
    first, second = [], []
    at = 0
    for size in sizes:
        first.append(total[at : at + size])
        second.append(total[at + size : at + 2 * size])
        at += 2 * size
    first = jnp.concatenate(first, axis=0)
    second = jnp.concatenate(second, axis=0)
    return jnp.where(me == 0, first, second), jnp.where(me == 0, second, first)


def local(plan, tokens, lengths, block_order, qkv_weight, query_bias, value_bias, out_weight, out_bias,
          norm1_gain, norm1_shift, in_weight, in_bias, down_weight, down_bias, norm2_gain, norm2_shift, cotangent):
    half = tokens.shape[1]
    me = plan.at(len(plan.dims) - 1)
    stays = plan.at(0) == me
    rows_dev = qkv_weight.shape[0]
    ff_dev = down_weight.shape[0]
    ff_cols = in_weight.shape[1] // D

    def tables(spot):
        core = spot[-1].astype(jnp.int32)[None]
        same = (spot[0] == spot[-1]).astype(jnp.int32)[None]
        return (jnp.concatenate([core, plan.chip_table(-1, spot), same]),
                jnp.concatenate([core, plan.slot_table(1, spot)]), jnp.concatenate([core, plan.slot_table(-1, spot)]))

    sizes1 = [rows_dev] * 3
    sizes2 = [rows_dev] * (1 + ff_cols) + [ff_dev]
    smalls = (query_bias, value_bias, out_bias, norm1_gain, norm1_shift, in_bias, down_bias, norm2_gain, norm2_shift)
    unit_rows = 2 * half // UNITS

    def stacked(vectors):
        bias_o, gain1, shift1, wide, bias_d, gain2, shift2 = vectors[2:]
        zero = jnp.zeros((D,), f32)
        return jnp.stack([bias_o, gain1, shift1, bias_d, gain2, shift2, zero, zero]), wide[None]

    def settle_rows(x, got):
        return jnp.where(stays, x, got)

    tok = settle_rows(tokens[0], cross(tokens[0]))
    tok_got = swap_pair(tok)
    if plan.direct:
        lines = [v[None] for v in smalls] + [lengths, block_order]
        slab = (5 + 2 * ff_cols, rows_dev, HALF)
        mine, give = whole_call(pack_body, (slab, slab), qkv_weight, out_weight, in_weight,
                                down_weight.reshape(ff_cols, rows_dev, D), *lines)
        got = swap_pair(give)
        unit1, unit2 = whole_call(combine_body, ((7, rows_dev, HALF), (2 + 4 * ff_cols, rows_dev, HALF)), mine, got)
        unit1 = unit1.reshape(7 * rows_dev, HALF)
        unit2 = unit2.reshape(-1, HALF)
        other = got[3, len(smalls) : len(smalls) + 2, :UNITS].astype(jnp.int32)
        counts_here = jnp.where(stays, lengths[0], other[0]) // unit_rows
        order_here = jnp.where(stays, block_order[0], other[1])

        z1 = gather_z(plan, unit1)
        unit2, z1 = together(unit2, z1)
        x1, y1 = plan.send(z1, 0), plan.send(z1, 2)
        tok, unit2, *spot = together(tok, unit2, *plan.coords())
        z2_parts = [unit2] + [plan.send(unit2, 1, k) for k in range(1, 4)]
        pull, push, find = tables(spot)
        cot, x1, y1, tok, pull, find = together(cotangent[0], x1, y1, tok, pull, find)
        d1a, d1b = plan.send(y1[0:2], 0), plan.send(x1[2:4], 2)
        cot_got = cross(cot)
        pieces1 = [z1, x1, y1, d1a, d1b]
        table = small_table(find, pieces1).reshape(plan.chips, 16, 2, 128)

        def vectors_of(table):
            return [table[:, i, :, : v.shape[0]].reshape(-1).astype(f32) for i, v in enumerate(smalls)]

        vectors = vectors_of(table)
    else:
        pull, push, _ = tables(plan.coords())
        first = jnp.concatenate([qkv_weight[:, j * D : (j + 1) * D] for j in range(3)], axis=0)
        second = jnp.concatenate([out_weight] + [in_weight[:, j * D : (j + 1) * D] for j in range(ff_cols)] + [down_weight], axis=0)
        line = jnp.concatenate(smalls)
        both = jnp.concatenate([first, second], axis=0)
        got = swap_pair(half_of(both, 1 - me))
        mine = half_of(both, me)
        cut = 3 * rows_dev
        unit1 = chip_units(me, mine[:cut], got[:cut], sizes1)
        unit2 = chip_units(me, mine[cut:], got[cut:], sizes2)
        line_got = swap_pair(line)
        line_unit = jnp.stack([jnp.where(me == 0, line, line_got), jnp.where(me == 0, line_got, line)])
        pieces1 = [regroup(gather_chips(plan, unit1), [2 * r for r in sizes1], SLOTS)]
        pieces2 = [regroup(gather_chips(plan, unit2), [2 * r for r in sizes2], SLOTS)]
        far2 = [swap_pair(p) for p in pieces2]
        lines = gather_chips(plan, line_unit).reshape(2 * plan.chips, line.shape[0])
        vectors = []
        at = 0
        for piece in smalls:
            size = piece.shape[0]
            vectors.append(lines[:, at : at + size].reshape(2 * plan.chips * size).astype(f32))
            at += size
        counts_here = jnp.where(stays, lengths[0], swap_pair(lengths[0])) // unit_rows
        order_here = jnp.where(stays, block_order[0], swap_pair(block_order[0]))
        cot_got = cross(cotangent[0])
    bias_q, bias_v = vectors[:2]
    bias_qkv = jnp.concatenate([half_of(bias_q, me), jnp.zeros((HALF,), f32), half_of(bias_v, me)])[None]

    spot = jnp.arange(UNITS)
    ends = jnp.sum(jnp.where(spot[None, :] <= spot[:, None], counts_here[None, :], 0), axis=1)
    seg_packed = jnp.sum((spot[:, None] >= ends[None, :]).astype(jnp.int32), axis=1)
    hit = order_here[:, None] == spot[None, :]
    segs = jnp.sum(jnp.where(hit, seg_packed[:, None], 0), axis=0)
    segs = jnp.where(me == 0, segs, jnp.roll(segs, UNITS // 2))

    qkv, w_qkv = project(pull, tok, tok_got, bias_qkv, pieces1)
    if plan.direct:
        *z2_parts, table, qkv = together(*z2_parts, table, qkv)
        vectors = vectors_of(table)
        z2 = jnp.stack(z2_parts)
        x2, y2 = plan.send(z2, 0), plan.send(z2, 2)
        z2_far = swap_pair(z2)
        att = attention(segs, qkv, 0, 2, None)
        vecs, gate_bias = stacked(vectors)
        x2, y2, cot_got, vecs, gate_bias, push, *att = together(x2, y2, cot_got, vecs, gate_bias, push, *att)
        d2a, d2b = plan.send(y2[0:2], 0), plan.send(x2[2:4], 2)
        x2_far, y2_far = swap_pair(x2), swap_pair(y2)
    else:
        att = attention(segs, qkv, 0, 2, None)
        vecs, gate_bias = stacked(vectors)
    o_own, o_far, lse = attention(segs, qkv, 2, PAIRS - 2, att)
    o_got = swap_pair(o_far)
    if plan.direct:
        pieces2 = [z2, x2, y2, d2a, d2b]
        far2 = [z2_far, x2_far, y2_far, swap_pair(d2a), swap_pair(d2b)]
    (out_rows, act, ig, low, branch, attn_grad, resid1, d_own, d_far, sums) = middle(
        pull, tok, o_own, o_got, cotangent[0], cot_got, vecs, gate_bias, pieces2, far2)
    d_got = swap_pair(d_far)
    out_got = cross(out_rows)
    sum_got = swap_pair(half_of(sums, 1 - me))
    grad_args = (low, branch, o_own, o_got)
    give = weight_grads(False, push, act, ig, *grad_args, attn_grad)
    give, attn_grad = together(give, attn_grad)
    got_g = swap_pair(give)
    keep = weight_grads(True, push, act, ig, *grad_args, attn_grad)
    back_args = (o_own, o_far, d_own, d_got, lse)
    if plan.direct:

        def both_sums(lo, hi):
            return keep[lo:hi].astype(f32) + got_g[lo:hi].astype(f32)

        def late(rows):
            return jnp.pad(rows.astype(f32), ((2, 0), (0, 0), (0, 0)))

        def early(rows):
            return jnp.pad(rows.astype(f32), ((0, 2), (0, 0), (0, 0)))

        sx, sy, qkv_back, out_got = together(both_sums(12, 14).astype(bf16), both_sums(14, 16).astype(bf16), qkv, out_got)
        rx, ry = plan.send(sx, 0), plan.send(sy, 2)
        g = attention_back(segs, qkv_back, *back_args, 0, 1, None)
        rx, ry, sum_got, *g = together(rx, ry, sum_got, *g)
        send_x = (both_sums(4, 8) + late(ry)).astype(bf16)
        send_y = (both_sums(8, 12) + early(rx)).astype(bf16)
        send_x, send_y, *g = together(send_x, send_y, *g)
        px, py = plan.send(send_x, 0), plan.send(send_y, 2)
        g = attention_back(segs, qkv_back, *back_args, 1, 1, g)
        px, py, *g = together(px, py, *g)
        z_sum = both_sums(0, 4) + px.astype(f32) + py.astype(f32)
        z_low, ffn, *g = together(z_sum[1:].astype(bf16), z_sum[0], *g)
        z_got = [plan.send(z_low[k - 1], 1, k) for k in range(1, 4)]
        g = attention_back(segs, qkv_back, *back_args, 2, PAIRS - 2, g)
        *z_got, dq, dk, dv = together(*z_got, *g)
        for part in z_got:
            ffn = ffn + part.astype(f32)
    else:
        dq, dk, dv = attention_back(segs, qkv, *back_args, 0, PAIRS, None)
        summed = (keep.astype(f32) + got_g.astype(f32)).astype(bf16)
        scale = plan.chips // SLOTS
        units = regroup_back(summed, [ROWS] * (1 + ff_cols) + [ROWS * ff_cols], scale)
        ffn = reduce_chips(plan, units)
    small = half_of(sums, me) + sum_got
    tail = qkv_grads(push, small, tok, tok_got, dq, dk, dv)
    if plan.direct:
        rx, ry = plan.send(tail[12:14], 0), plan.send(tail[14:16], 2)
        far_back = input_back(w_qkv, dq, dk, dv, True, ())
        rx, ry, far_back = together(rx, ry, far_back)
        far_back = swap_pair(far_back)
        send_x = (tail[4:8].astype(f32) + late(ry)).astype(bf16)
        send_y = (tail[8:12].astype(f32) + early(rx)).astype(bf16)
        px, py = plan.send(send_x, 0), plan.send(send_y, 2)
        packed = input_back(w_qkv, dq, dk, dv, False, (resid1, far_back))
        px, py, packed = together(px, py, packed)
        packed_got = cross(packed)
        z_sum = tail[0:4].astype(f32) + px.astype(f32) + py.astype(f32)
        z_low, out_got = together(z_sum[1:].astype(bf16), out_got)
        qkv_sum = z_sum[0]
        output = settle_rows(out_rows, out_got)
        packed_got, output, *z_got = together(packed_got, output, *[plan.send(z_low[k - 1], 1, k) for k in range(1, 4)])
        for part in z_got:
            qkv_sum = qkv_sum + part.astype(f32)
    else:
        far_back = swap_pair(input_back(w_qkv, dq, dk, dv, True, ()))
        packed = input_back(w_qkv, dq, dk, dv, False, (resid1, far_back))
        packed_got = cross(packed)
        output = settle_rows(out_rows, out_got)
        units = regroup_back(tail[:, : 3 * ROWS], [ROWS] * 3, scale)
        extra = jnp.broadcast_to(tail[0:1, 3 * ROWS :], (plan.chips, 16, HALF))
        qkv_sum = reduce_chips(plan, jnp.concatenate([units, extra], axis=1))
    small_sum = qkv_sum[6 * rows_dev :]
    sizes = sizes1 + sizes2
    total = jnp.concatenate([qkv_sum[: 6 * rows_dev], ffn], axis=0)
    mine, other = own_rows(me, total, sizes)
    got = swap_pair(jnp.concatenate([other, small_sum], axis=0))
    count = mine.shape[0]
    mine = jnp.concatenate([mine, small_sum], axis=0)
    full = jnp.concatenate([jnp.where(me == 0, mine, got), jnp.where(me == 0, got, mine)], axis=1)
    take = lambda at, size: full[at : at + size]
    out_qkv = jnp.concatenate([take(j * rows_dev, rows_dev) for j in range(3)], axis=1)
    out_out = take(3 * rows_dev, rows_dev)
    out_in = jnp.concatenate([take((4 + j) * rows_dev, rows_dev) for j in range(ff_cols)], axis=1)
    out_down = take((4 + ff_cols) * rows_dev, ff_dev)
    small_full = full[count:]
    device = plan.at(0)
    for a in range(1, len(plan.dims)):
        device = device * plan.dims[a] + plan.at(a)
    order = (14, 15, 0, 1, 2, 3, 3 + ff_cols, 4 + ff_cols, 5 + ff_cols)
    wide_row = 3
    thin = lax.dynamic_slice_in_dim(small_full, device * rows_dev, rows_dev, axis=1)
    span = small_full[wide_row : wide_row + ff_cols].reshape(-1)
    s = [lax.dynamic_slice_in_dim(span, device * ff_dev, ff_dev) if row == wide_row and piece is in_bias else thin[row]
         for piece, row in zip(smalls, order)]
    input_grad = settle_rows(packed, packed_got)
    return (output[None], input_grad[None], out_qkv, s[0], s[1], out_out, s[2], s[3], s[4], out_in, s[5], out_down, s[6], s[7], s[8])


def regroup_back(buf, sizes, scale):
    n, _, w = buf.shape
    parts = []
    at = 0
    for size in sizes:
        parts.append(buf[:, at : at + size].reshape(n * scale, size // scale, w))
        at += size
    return jnp.concatenate(parts, axis=1)


def solution(mesh):
    plan = Plan(mesh.shape["seq"], mesh.shape["fsdp"])
    inner_mesh = Mesh(mesh.devices.reshape(plan.dims), tuple(plan.names))
    groups = tuple(plan.names[1:])
    every = tuple(plan.names)
    rows = P(groups, "s", None)
    table = P(groups, None)
    mat = P(every, None)
    vec = P(every)
    placed = (rows, table, table, mat, vec, vec, mat, vec, vec, vec, mat, vec, mat, vec, vec, vec, rows)
    outs = (rows, rows, mat, vec, vec, mat, vec, vec, vec, mat, vec, mat, vec, vec, vec)

    def run(*args):
        return local(plan, *args)

    return jax.shard_map(run, mesh=inner_mesh, in_specs=placed, out_specs=outs, check_vma=False)
```
